128 devices in a mesh: ctx: 8 (over y_hi, z), exp: 16 (over y_lo, x, core).
Axes of the slice: x: 4, y: 4 (y_hi: 2, y_lo: 2; y = y_hi * 2 + y_lo), z: 4, core: 2. Of those that a mesh axis runs over, the one named last changes fastest.
Arguments:
- moe_input: bfloat16 [16384, 4096], P(('ctx', 'exp')), may hold values from -6 to 6
- out_grad: bfloat16 [16384, 4096], P(('ctx', 'exp')), may hold values from -6 to 6
- w_gate: bfloat16 [32, 4096, 1408], P('exp', None, 'ctx'), may hold values from -0.09375 to 0.09375
- w_up: bfloat16 [32, 4096, 1408], P('exp', None, 'ctx'), may hold values from -0.09375 to 0.09375
- w_down: bfloat16 [32, 1408, 4096], P('exp', 'ctx'), may hold values from -0.15625 to 0.15625
- expert_picks: int32 [32, 128], replicated, may hold values from 0 to 16383, as said below
- gate_probs: float32 [32, 128], replicated, may hold values from 0.2 to 1
- queries: bfloat16 [16384, 2048], P('ctx', 'exp'), may hold values from -6 to 6
- attn_keys: bfloat16 [16384, 2048], P('ctx', 'exp'), may hold values from -6 to 6
- values: bfloat16 [16384, 2048], P('ctx', 'exp'), may hold values from -6 to 6
- attn_out: bfloat16 [16384, 2048], P('ctx', 'exp'), may hold values from -1.5 to 1.5
- log_norm: float32 [16, 16384], P('exp'), may hold values from -1 to 12
- w_out: bfloat16 [2048, 4096], P('exp'), may hold values from -0.09375 to 0.09375
Outputs:
- d_resid: bfloat16 [16384, 4096], P(('ctx', 'exp'))
- dw_gate: bfloat16 [32, 4096, 1408], P('exp', None, 'ctx')
- dw_up: bfloat16 [32, 4096, 1408], P('exp', None, 'ctx')
- dw_down: bfloat16 [32, 1408, 4096], P('exp', 'ctx')
- d_gates: float32 [32, 128], P('exp', 'ctx')
- dw_out: bfloat16 [2048, 4096], P('exp', 'ctx')
- grad_q: bfloat16 [16384, 2048], P('ctx', 'exp')
- grad_k: bfloat16 [16384, 2048], P('ctx', 'exp')
- grad_v: bfloat16 [16384, 2048], P('ctx', 'exp')
The draws below stay inside these ranges and needn't reach their ends.
Inputs may be any that keep to these rules, and one draw needn't show every extreme that they name: expert_picks[e] lists distinct tokens in ascending order: exactly 16 from each context group of 2048 consecutive tokens and at most 2 from each aligned block of 128 tokens; in every group some block gives exactly 2.
All inputs are finite; a program needn't handle non-finite values.
Results may differ from the reference program's by a relative error of at most 0.023.
Values may be sent and summed in bfloat16 or wider, within the bound.
A program may use at most 256 MiB of HBM per device.

```python
import jax
import jax.numpy as jnp
from jax import lax

D = 4096
HEAD = 128
FF = 1408
MOST = 2
TOK_DEV = 128
HEADS = 16
EXPERTS = 32
TOK_CTX = 2048
TOKENS = 16384
GROUP_PICKS = 16
CAPACITY = 128
FF_DEV = 176
N_CTX = 8


def draw_expert_picks(key, part):
    n_groups = CAPACITY // GROUP_PICKS
    blocks = GROUP_PICKS
    slot_total = MOST * blocks
    key_order = jax.random.fold_in(key, 11)
    key_full = jax.random.fold_in(key, 12)
    key_first = jax.random.fold_in(key, 13)
    key_second = jax.random.fold_in(key, 14)
    ranks = jax.random.randint(key_order, (EXPERTS, n_groups, slot_total), 0, 1 << 20)
    slot_ids = jnp.arange(slot_total, dtype=jnp.int32)
    scores = ranks * slot_total + slot_ids[None, None, :]
    full_block = jax.random.randint(key_full, (EXPERTS, n_groups, 1), 0, blocks)
    scores = jnp.where(slot_ids[None, None, :] // MOST == full_block, -1 - slot_ids[None, None, :] % MOST, scores)
    order = jnp.argsort(scores, axis=-1, stable=True)[:, :, :GROUP_PICKS]
    picked_block = order // MOST
    picked_slot = order % MOST
    first_tok = jax.random.randint(key_first, (EXPERTS, n_groups, blocks), 0, TOK_DEV)
    step_tok = jax.random.randint(key_second, (EXPERTS, n_groups, blocks), 1, TOK_DEV)
    second_tok = (first_tok + step_tok) % TOK_DEV
    tok_first = jnp.take_along_axis(first_tok, picked_block, axis=-1)
    tok_second = jnp.take_along_axis(second_tok, picked_block, axis=-1)
    local_tok = jnp.where(picked_slot == 0, tok_first, tok_second)
    group_ids = jnp.arange(n_groups, dtype=jnp.int32)[None, :, None]
    global_ids = (group_ids * blocks + picked_block) * TOK_DEV + local_tok
    ordered = jnp.sort(global_ids, axis=-1)
    return ordered.reshape(EXPERTS, CAPACITY).astype(jnp.int32)


def draw_log_norm(key, part):
    positions = jnp.arange(TOKENS, dtype=jnp.float32)
    base_level = jnp.log(positions + 1.0) + 0.5
    noise = jnp.clip(jax.random.normal(key, (HEADS, TOKENS), jnp.float32) * 0.15, -0.6, 0.6)
    return (base_level[None, :] + noise).astype(jnp.float32)


def shard_levels(stream_key, dims, split, least, top_value):
    factor_of = 1.0
    for dim, parts in split:
        steps = jax.random.uniform(jax.random.fold_in(jax.random.fold_in(stream_key, 6), dim), (parts,), jnp.float32, least / len(split), top_value / len(split))
        factor_of = factor_of * jnp.repeat(jnp.exp(steps), dims[dim] // parts).reshape((-1,) + (1,) * (len(dims) - 1 - dim))
    return factor_of


def scatter_about(stream_key, shape, spread, reach, shards=(), kind=jnp.bfloat16):
    entries = spread * jax.random.normal(stream_key, shape, jnp.float32)
    if shards:
        entries = entries * shard_levels(stream_key, shape, shards, -0.22, 0.18)
    return jnp.clip(entries, -reach, reach).astype(kind)


def setup_inputs(seed: int = 0) -> dict:
    keys = jax.random.split(jax.random.key(seed), 14)
    return {
        "moe_input": scatter_about(keys[0], (TOKENS, D), 1.0, 6.0, ((0, 128),)),
        "out_grad": scatter_about(keys[1], (TOKENS, D), 1.0, 6.0, ((0, 128),)),
        "w_gate": scatter_about(keys[2], (EXPERTS, D, FF), D ** -0.5, 0.09375, ((0, 16), (2, 8))),
        "w_up": scatter_about(keys[3], (EXPERTS, D, FF), D ** -0.5, 0.09375, ((0, 16), (2, 8))),
        "w_down": scatter_about(keys[4], (EXPERTS, FF, D), FF ** -0.5, 0.15625, ((0, 16), (1, 8))),
        "expert_picks": draw_expert_picks(jax.random.fold_in(keys[13], 71), 0),
        "gate_probs": jnp.clip(jax.random.uniform(keys[6], (EXPERTS, CAPACITY), jnp.float32, 0.2, 1.0), 0.2, 1.0),
        "queries": scatter_about(keys[7], (TOKENS, HEADS * HEAD), 1.0, 6.0, ((0, 8), (1, 16))),
        "attn_keys": scatter_about(keys[8], (TOKENS, HEADS * HEAD), 1.0, 6.0, ((0, 8), (1, 16))),
        "values": scatter_about(keys[9], (TOKENS, HEADS * HEAD), 1.0, 6.0, ((0, 8), (1, 16))),
        "attn_out": scatter_about(keys[10], (TOKENS, HEADS * HEAD), 0.25, 1.5, ((0, 8), (1, 16))),
        "log_norm": draw_log_norm(jax.random.fold_in(keys[13], 71), 0),
        "w_out": scatter_about(keys[12], (HEADS * HEAD, D), D ** -0.5, 0.09375, ((0, 16),)),
    }


def activation(pre_act):
    sigmoid_val = jax.nn.sigmoid(pre_act)
    return pre_act * sigmoid_val, sigmoid_val * (1.0 + pre_act * (1.0 - sigmoid_val))


def settle(value):
    return lax.optimization_barrier(value.astype(jnp.bfloat16)).astype(jnp.float32)


def contract_first(left, right):
    return lax.dot_general(left, right, (((0,), (0,)), ((), ())), preferred_element_type=jnp.float32)


def contract_last(left, right):
    return lax.dot_general(left, right, (((1,), (1,)), ((), ())), preferred_element_type=jnp.float32)


def reference(moe_input, out_grad, w_gate, w_up, w_down, expert_picks, gate_probs, queries, attn_keys, values, attn_out, log_norm, w_out):
    def one_expert(packed):
        w_gate_e, w_up_e, w_down_e, chosen, gate_row = packed
        slot_rows = moe_input[chosen]
        slot_grads = out_grad[chosen]
        pre_gate = jnp.dot(slot_rows, w_gate_e, preferred_element_type=jnp.float32)
        pre_up = jnp.dot(slot_rows, w_up_e, preferred_element_type=jnp.float32)
        gated_act, act_slope = activation(pre_gate)
        hidden_full = gated_act * pre_up
        hidden = hidden_full.astype(jnp.bfloat16)
        down_back = contract_last(slot_grads, w_down_e)
        group_sums = jnp.sum((down_back * hidden_full).reshape(CAPACITY, N_CTX, FF_DEV), axis=2)
        d_gate_prob = jnp.sum(settle(group_sums), axis=1)
        scaled = gate_row[:, None] * down_back
        d_gate = (scaled * pre_up * act_slope).astype(jnp.bfloat16)
        d_up = (scaled * gated_act).astype(jnp.bfloat16)
        weighted = (gate_row[:, None] * slot_grads.astype(jnp.float32)).astype(jnp.bfloat16)
        dw_down_e = contract_first(hidden, weighted).astype(jnp.bfloat16)
        dw_gate_e = contract_first(slot_rows, d_gate).astype(jnp.bfloat16)
        dw_up_e = contract_first(slot_rows, d_up).astype(jnp.bfloat16)
        gate_groups = d_gate.astype(jnp.float32).reshape(CAPACITY, N_CTX, FF_DEV)
        up_groups = d_up.astype(jnp.float32).reshape(CAPACITY, N_CTX, FF_DEV)
        wg_groups = w_gate_e.astype(jnp.float32).reshape(D, N_CTX, FF_DEV)
        wu_groups = w_up_e.astype(jnp.float32).reshape(D, N_CTX, FF_DEV)
        group_terms = jnp.einsum("cnf,dnf->ncd", gate_groups, wg_groups) + jnp.einsum("cnf,dnf->ncd", up_groups, wu_groups)
        dx_slot = jnp.sum(settle(group_terms), axis=0).astype(jnp.bfloat16)
        return dw_gate_e, dw_up_e, dw_down_e, d_gate_prob, dx_slot

    dw_gate, dw_up, dw_down, d_gates, dx_slot = lax.map(one_expert, (w_gate, w_up, w_down, expert_picks, gate_probs))
    contrib = jnp.zeros((TOKENS, D), jnp.float32).at[expert_picks.reshape(-1)].add(dx_slot.reshape(-1, D).astype(jnp.float32))
    d_resid = (out_grad.astype(jnp.float32) + contrib).astype(jnp.bfloat16)

    key_scale = HEAD ** -0.5
    positions = jnp.arange(TOKENS, dtype=jnp.int32)

    def one_head(head_idx):
        column = head_idx * HEAD
        w_rows = lax.dynamic_slice_in_dim(w_out, column, HEAD, 0)
        d_out = contract_last(d_resid, w_rows).astype(jnp.bfloat16)
        q_head = lax.dynamic_slice_in_dim(queries, column, HEAD, 1)
        k_head = lax.dynamic_slice_in_dim(attn_keys, column, HEAD, 1)
        v_head = lax.dynamic_slice_in_dim(values, column, HEAD, 1)
        out_head = lax.dynamic_slice_in_dim(attn_out, column, HEAD, 1)
        out_groups = out_head.astype(jnp.float32).reshape(N_CTX, TOK_CTX, HEAD)
        resid_groups = d_resid.astype(jnp.float32).reshape(N_CTX, TOK_CTX, D)
        dw_head = jnp.sum(settle(jnp.einsum("ntk,ntd->nkd", out_groups, resid_groups)), axis=0).astype(jnp.bfloat16)
        row_delta = jnp.sum(d_out.astype(jnp.float32) * out_head.astype(jnp.float32), axis=1)
        norm_row = lax.dynamic_slice_in_dim(log_norm, head_idx, 1, 0)[0]

        def query_block(carried, block_idx):
            grad_keys, grad_values = carried
            start = block_idx * TOK_CTX
            q_block = lax.dynamic_slice_in_dim(q_head, start, TOK_CTX, 0)
            do_block = lax.dynamic_slice_in_dim(d_out, start, TOK_CTX, 0)
            norm_block = lax.dynamic_slice_in_dim(norm_row, start, TOK_CTX, 0)
            delta_block = lax.dynamic_slice_in_dim(row_delta, start, TOK_CTX, 0)
            q_positions = start + jnp.arange(TOK_CTX, dtype=jnp.int32)
            scores = contract_last(q_block, k_head) * key_scale
            causal = positions[None, :] <= q_positions[:, None]
            attn_probs = jnp.exp(jnp.where(causal, scores - norm_block[:, None], -1e30))
            d_probs = contract_last(do_block, v_head)
            d_scores = (attn_probs * (d_probs - delta_block[:, None])).astype(jnp.bfloat16)
            probs_low = attn_probs.astype(jnp.bfloat16)
            grad_values = grad_values + contract_first(probs_low, do_block)
            grad_keys = grad_keys + contract_first(d_scores, q_block) * key_scale
            grad_block = (jnp.dot(d_scores, k_head, preferred_element_type=jnp.float32) * key_scale).astype(jnp.bfloat16)
            return (grad_keys, grad_values), grad_block

        empty = jnp.zeros((TOKENS, HEAD), jnp.float32)
        (grad_keys, grad_values), q_blocks = lax.scan(query_block, (empty, empty), jnp.arange(N_CTX, dtype=jnp.int32))
        return q_blocks.reshape(TOKENS, HEAD), grad_keys.astype(jnp.bfloat16), grad_values.astype(jnp.bfloat16), dw_head

    grad_q, grad_k, grad_v, dw_heads = lax.map(one_head, jnp.arange(HEADS, dtype=jnp.int32))
    grad_q = jnp.transpose(grad_q, (1, 0, 2)).reshape(TOKENS, HEADS * HEAD)
    grad_k = jnp.transpose(grad_k, (1, 0, 2)).reshape(TOKENS, HEADS * HEAD)
    grad_v = jnp.transpose(grad_v, (1, 0, 2)).reshape(TOKENS, HEADS * HEAD)
    dw_out = dw_heads.reshape(HEADS * HEAD, D)
    return (d_resid, dw_gate, dw_up, dw_down, d_gates, dw_out, grad_q, grad_k, grad_v)
```

```python
import functools
import math

import jax
import jax.numpy as jnp
from jax import lax
from jax.experimental import pallas as pl
from jax.experimental.pallas import tpu as pltpu
from jax.sharding import PartitionSpec as P

MOST = 2
MESH = pl.DeviceIdType.MESH
LOG2E = 1.4426950408889634
BF = jnp.bfloat16
F32 = jnp.float32
VLIM = 56 * 1024 * 1024
VM = pltpu.VMEM


def activation(pre_act):
    sigmoid_val = jax.nn.sigmoid(pre_act)
    return (pre_act * sigmoid_val, sigmoid_val * (1.0 + pre_act * (1.0 - sigmoid_val)))


def contract_first(left, right):
    return lax.dot_general(left, right, (((0,), (0,)), ((), ())), preferred_element_type=F32)


def contract_last(left, right):
    return lax.dot_general(left, right, (((1,), (1,)), ((), ())), preferred_element_type=F32)


class Place:
    def __init__(self, axis):
        self.axis = axis
        me = lax.axis_index(axis)
        if axis == "ctx":
            step, span = 1, 4
        else:
            step, span = 2, 8
        low = lax.rem(me, step)
        pos = lax.rem(me // step, 4)
        row = me // span
        other = 1 - row

        def at(r, p):
            return r * span + lax.rem(p + 4, 4) * step + low

        self.me = me
        self.up, self.down, self.far = at(row, pos + 1), at(row, pos - 1), at(row, pos + 2)
        self.mate = at(other, pos)
        self.mate_up, self.mate_down = at(other, pos + 1), at(other, pos - 1)
        self.mate_far = at(other, pos + 2)


def greet(peers):
    barrier = pltpu.get_barrier_semaphore()
    for axis, dev in peers:
        pl.semaphore_signal(barrier, inc=1, device_id={axis: dev}, device_id_type=MESH)
    pl.semaphore_wait(barrier, len(peers))


class Lanes:
    def __init__(self, send_sems, recv_sems):
        self.send_sems, self.recv_sems, self.sent = send_sems, recv_sems, []

    def copy(self, k, src, dst, axis, dev):
        return pltpu.make_async_remote_copy(
            src_ref=src,
            dst_ref=dst,
            send_sem=self.send_sems.at[k],
            recv_sem=self.recv_sems.at[k],
            device_id={axis: dev},
            device_id_type=MESH,
        )

    def send(self, k, src, dst, axis, dev):
        one = self.copy(k, src, dst, axis, dev)
        one.start()
        self.sent.append(one)

    def recv(self, k, dst, axis, dev):
        self.copy(k, dst, dst, axis, dev).wait_recv()

    def finish(self):
        for one in self.sent:
            one.wait_send()


AG_LANES = 14


def gather_ring(pieces, place, lanes, base, arrived=None):
    axis = place.axis
    n = len(pieces)

    def send(k, block, half, dev):
        for i, piece in enumerate(pieces):
            lanes.send(base + k * n + i, piece(block, half), piece(block, half), axis, dev)

    def recv(k, block, half, dev):
        for i, piece in enumerate(pieces):
            lanes.recv(base + k * n + i, piece(block, half), axis, dev)
        if arrived is not None:
            arrived(k, block, half)

    p = place
    send(0, p.me, 0, p.mate)
    send(2, p.me, 0, p.up)
    send(4, p.me, 1, p.down)
    send(1, p.me, 1, p.mate)
    send(3, p.me, 1, p.up)
    send(5, p.me, 0, p.down)
    recv(2, p.down, 0, p.down)
    send(6, p.down, 0, p.up)
    recv(4, p.up, 1, p.up)
    send(7, p.up, 1, p.down)
    recv(0, p.mate, 0, p.mate)
    send(8, p.mate, 0, p.up)
    send(10, p.mate, 0, p.down)
    recv(1, p.mate, 1, p.mate)
    send(11, p.mate, 1, p.down)
    send(9, p.mate, 1, p.up)
    recv(8, p.mate_down, 0, p.down)
    send(12, p.mate_down, 0, p.up)
    recv(11, p.mate_up, 1, p.up)
    send(13, p.mate_up, 1, p.down)
    recv(3, p.down, 1, p.down)
    recv(5, p.up, 0, p.up)
    recv(6, p.far, 0, p.down)
    recv(7, p.far, 1, p.up)
    recv(10, p.mate_up, 0, p.up)
    recv(9, p.mate_down, 1, p.down)
    recv(12, p.mate_far, 0, p.down)
    recv(13, p.mate_far, 1, p.up)


def add_into(dst, *srcs):
    total = srcs[0][...].astype(F32)
    for src in srcs[1:]:
        total = total + src[...].astype(F32)
    dst[...] = total.astype(dst.dtype)


def scatter_ring(parts, place, lanes, base, bufs, outs):
    axis = place.axis
    n = len(parts)
    p = place
    groups = (
        (p.mate_far, p.mate_up, p.mate_down, p.mate),
        (p.far, p.up, p.down, p.me),
    )

    def slot(i, s):
        return bufs[i](s)

    def send(k, i, src, s, dev):
        lanes.send(base + k * n + i, src, slot(i, s), axis, dev)

    def recv(k, i, s, dev):
        lanes.recv(base + k * n + i, slot(i, s), axis, dev)

    every = range(n)
    for g, (far, up, down, own) in enumerate(groups):
        for i in every:
            send(6 * g + 0, i, parts[i](far, 0), 6 * g + 0, p.up)
            send(6 * g + 1, i, parts[i](far, 1), 6 * g + 1, p.down)
        for i in every:
            send(6 * g + 3, i, parts[i](up, 1), 6 * g + 3, p.up)
            send(6 * g + 4, i, parts[i](down, 0), 6 * g + 4, p.down)
        if g == 0:
            continue
    for g, (far, up, down, own) in enumerate(groups):
        for i in every:
            recv(6 * g + 0, i, 6 * g + 0, p.down)
            add_into(slot(i, 6 * g + 0), slot(i, 6 * g + 0), parts[i](up, 0))
            send(6 * g + 2, i, slot(i, 6 * g + 0), 6 * g + 2, p.up)
            recv(6 * g + 1, i, 6 * g + 1, p.up)
            add_into(slot(i, 6 * g + 1), slot(i, 6 * g + 1), parts[i](down, 1))
            send(6 * g + 5, i, slot(i, 6 * g + 1), 6 * g + 5, p.down)
    far, up, down, own = groups[0]
    for half in (1, 0):
        for i in every:
            recv(2 + half, i, 2 + half, p.down)
            recv(4 + half, i, 4 + half, p.up)
            add_into(slot(i, 2 + half), slot(i, 2 + half), slot(i, 4 + half), parts[i](own, half))
            send(12 + half, i, slot(i, 2 + half), 12 + half, p.mate)
    for half in (1, 0):
        for i in every:
            recv(8 + half, i, 8 + half, p.down)
            recv(10 + half, i, 10 + half, p.up)
            recv(12 + half, i, 12 + half, p.mate)
            add_into(
                outs[i](half),
                slot(i, 8 + half),
                slot(i, 10 + half),
                slot(i, 12 + half),
                parts[i](p.me, half),
            )


def around(place):
    return [(place.axis, place.up), (place.axis, place.down), (place.axis, place.mate)]


def dispatch_kernel(mi_ref, og_ref, pick_ref, place_ref, out_ref, send, got, ss, rs):
    ctx = Place("ctx")
    me = lax.axis_index("exp")
    n_exp = send.shape[0]
    peers = [("exp", lax.rem(me + d, n_exp)) for d in range(1, n_exp)]
    greet(peers + around(ctx))
    lanes = Lanes(ss, rs)
    rows = jnp.dot(pick_ref[:, :128], mi_ref[...], preferred_element_type=F32)
    rows = rows + jnp.dot(pick_ref[:, 128:], og_ref[...], preferred_element_type=F32)
    send[...] = rows.reshape(n_exp, 8, rows.shape[1]).astype(BF)
    for d in range(1, n_exp):
        to = lax.rem(me + d, n_exp)
        lanes.send(d - 1, send.at[to], got.at[d], "exp", to)
    got[0] = send[me]
    for d in range(1, n_exp):
        lanes.recv(d - 1, got.at[d], "exp", lax.rem(me + n_exp - d, n_exp))
    flat = got[...].astype(F32).reshape(n_exp * 8, got.shape[2]).astype(BF)
    mine = jnp.dot(place_ref[...], flat, preferred_element_type=F32).astype(BF)
    mine = mine.reshape(2, 2, 16, got.shape[2])
    for a in range(2):
        for k in range(2):
            out_ref[a, k, ctx.me] = mine[a, k]

    def piece(block, half):
        return out_ref.at[half, :, block]

    gather_ring([piece], ctx, lanes, n_exp - 1)
    lanes.finish()


def dispatch(moe_input, out_grad, pick, place):
    n_exp, n_ctx = lax.axis_size("exp"), lax.axis_size("ctx")
    width = moe_input.shape[1]
    n_sem = n_exp - 1 + AG_LANES
    return pl.pallas_call(
        dispatch_kernel,
        out_shape=jax.ShapeDtypeStruct((2, 2, n_ctx, 16, width), BF),
        in_specs=[pl.BlockSpec(memory_space=VM)] * 4,
        out_specs=pl.BlockSpec(memory_space=VM),
        scratch_shapes=[
            VM((n_exp, 8, width), BF),
            VM((n_exp, 8, width), BF),
            pltpu.SemaphoreType.DMA((n_sem,)),
            pltpu.SemaphoreType.DMA((n_sem,)),
        ],
        compiler_params=pltpu.CompilerParams(
            collective_id=1, has_side_effects=True, vmem_limit_bytes=VLIM
        ),
        cost_estimate=pl.CostEstimate(flops=10**9, bytes_accessed=150 * 10**6, transcendentals=0),
    )(moe_input, out_grad, pick, place)


def combine_kernel(part_ref, out_ref, buf, ss, rs):
    ctx, exp = Place("ctx"), Place("exp")
    twin = exp.me + 1 - 2 * lax.rem(exp.me, 2)
    greet(around(ctx) + around(exp) + [("exp", twin)])
    lanes = Lanes(ss, rs)
    scatter_ring(
        [lambda block, half: part_ref.at[half, block]],
        ctx,
        lanes,
        0,
        [lambda s: buf.at[s]],
        [lambda half: out_ref.at[exp.me, half]],
    )

    def piece(block, half):
        return out_ref.at[block, half]

    base = AG_LANES
    over = 2 * AG_LANES
    flip = 1 - 2 * lax.rem(exp.me, 2)
    for half in range(2):
        lanes.send(over + 14 + half, piece(exp.me, half), piece(exp.me, half), "exp", twin)

    def arrived(k, block, half):
        lanes.send(over + k, piece(block, half), piece(block, half), "exp", twin)

    gather_ring([piece], exp, lanes, base, arrived)
    srcs = {
        0: (exp.mate, 0), 1: (exp.mate, 1), 2: (exp.down, 0), 3: (exp.down, 1),
        4: (exp.up, 1), 5: (exp.up, 0), 6: (exp.far, 0), 7: (exp.far, 1),
        8: (exp.mate_down, 0), 9: (exp.mate_down, 1), 10: (exp.mate_up, 0),
        11: (exp.mate_up, 1), 12: (exp.mate_far, 0), 13: (exp.mate_far, 1),
        14: (exp.me, 0), 15: (exp.me, 1),
    }
    for k, (block, half) in srcs.items():
        lanes.recv(over + k, piece(block + flip, half), "exp", twin)
    lanes.finish()


def combine(part):
    n_exp = lax.axis_size("exp")
    rows, width = part.shape[2:]
    n_sem = 2 * AG_LANES + 16
    return pl.pallas_call(
        combine_kernel,
        out_shape=jax.ShapeDtypeStruct((n_exp, 2, rows, width), BF),
        in_specs=[pl.BlockSpec(memory_space=VM)],
        out_specs=pl.BlockSpec(memory_space=VM),
        scratch_shapes=[
            VM((14, rows, width), BF),
            pltpu.SemaphoreType.DMA((n_sem,)),
            pltpu.SemaphoreType.DMA((n_sem,)),
        ],
        compiler_params=pltpu.CompilerParams(
            collective_id=2, has_side_effects=True, vmem_limit_bytes=VLIM
        ),
        cost_estimate=pl.CostEstimate(flops=10**8, bytes_accessed=120 * 10**6, transcendentals=0),
    )(part)


def spread_kernel(do_ref, delta_ref, do_all, delta_all, ss, rs):
    ctx = Place("ctx")
    greet(around(ctx))
    lanes = Lanes(ss, rs)
    do_all[ctx.me] = do_ref[...]
    delta_all[ctx.me] = delta_ref[...]
    rows = do_ref.shape[0] // 2

    def piece_do(block, half):
        return do_all.at[block, pl.ds(half * rows, rows)]

    def piece_delta(block, half):
        return delta_all.at[block, :, pl.ds(half * rows, rows)]

    gather_ring([piece_do, piece_delta], ctx, lanes, 0)
    lanes.finish()


def spread(d_out, delta):
    n_ctx = lax.axis_size("ctx")
    n_sem = 2 * AG_LANES
    return pl.pallas_call(
        spread_kernel,
        out_shape=(
            jax.ShapeDtypeStruct((n_ctx,) + d_out.shape, BF),
            jax.ShapeDtypeStruct((n_ctx,) + delta.shape, F32),
        ),
        in_specs=[pl.BlockSpec(memory_space=VM)] * 2,
        out_specs=(pl.BlockSpec(memory_space=VM),) * 2,
        scratch_shapes=[
            pltpu.SemaphoreType.DMA((n_sem,)),
            pltpu.SemaphoreType.DMA((n_sem,)),
        ],
        compiler_params=pltpu.CompilerParams(
            collective_id=3, has_side_effects=True, vmem_limit_bytes=VLIM
        ),
        cost_estimate=pl.CostEstimate(flops=10**6, bytes_accessed=120 * 10**6, transcendentals=0),
    )(d_out, delta)


def settle_kernel(dq_ref, dw_ref, dq_out, dw_out, dq_buf, dw_buf, ss, rs):
    ctx = Place("ctx")
    greet(around(ctx))
    lanes = Lanes(ss, rs)
    rows_q, rows_w = dq_ref.shape[1] // 2, dw_ref.shape[1] // 2
    scatter_ring(
        [
            lambda block, half: dq_ref.at[block, pl.ds(half * rows_q, rows_q)],
            lambda block, half: dw_ref.at[block, pl.ds(half * rows_w, rows_w)],
        ],
        ctx,
        lanes,
        0,
        [lambda s: dq_buf.at[s], lambda s: dw_buf.at[s]],
        [
            lambda half: dq_out.at[pl.ds(half * rows_q, rows_q)],
            lambda half: dw_out.at[pl.ds(half * rows_w, rows_w)],
        ],
    )
    lanes.finish()


def settle_grads(dq, dw):
    n_sem = 2 * AG_LANES
    return pl.pallas_call(
        settle_kernel,
        out_shape=(
            jax.ShapeDtypeStruct(dq.shape[1:], BF),
            jax.ShapeDtypeStruct(dw.shape[1:], BF),
        ),
        in_specs=[pl.BlockSpec(memory_space=VM)] * 2,
        out_specs=(pl.BlockSpec(memory_space=VM),) * 2,
        scratch_shapes=[
            VM((14, dq.shape[1] // 2, dq.shape[2]), BF),
            VM((14, dw.shape[1] // 2, dw.shape[2]), BF),
            pltpu.SemaphoreType.DMA((n_sem,)),
            pltpu.SemaphoreType.DMA((n_sem,)),
        ],
        compiler_params=pltpu.CompilerParams(
            collective_id=4, has_side_effects=True, vmem_limit_bytes=VLIM
        ),
        cost_estimate=pl.CostEstimate(flops=10**7, bytes_accessed=120 * 10**6, transcendentals=0),
    )(dq, dw)


CHUNK = 1024
TILE = 512


def attention_kernel(
    scale, n_chunk, k_ref, v_ref, q_ref, do_ref, lse_ref, delta_ref,
    dq_ref, dk_ref, dv_ref, dk_acc, dv_acc, dq_acc,
):
    i = pl.program_id(0)
    c = lax.axis_index("ctx")
    first = jnp.where(lax.rem(c, 2) == 0, c, n_chunk - 1 - c)
    ids = (first, n_chunk - 1 - first)

    @pl.when(i == 0)
    def _():
        dk_acc[...] = jnp.zeros_like(dk_acc)
        dv_acc[...] = jnp.zeros_like(dv_acc)

    dq_acc[...] = jnp.zeros_like(dq_acc)

    def tile(part, row, key, key_len, masked):
        q = q_ref[pl.ds(row, TILE), :]
        do = do_ref[0, pl.ds(row, TILE), :]
        lse = lse_ref[:, pl.ds(row, TILE)] * LOG2E
        delta = delta_ref[0, :, pl.ds(row, TILE)]
        k = k_ref[part, pl.ds(key, key_len), :]
        v = v_ref[part, pl.ds(key, key_len), :]
        s = contract_last(k, q) * (scale * LOG2E) - lse
        if masked:
            rk = lax.broadcasted_iota(jnp.int32, s.shape, 0)
            cq = lax.broadcasted_iota(jnp.int32, s.shape, 1)
            s = jnp.where(rk <= cq, s, -1e30)
        p = jnp.exp2(s)
        dp = contract_last(v, do)
        ds = (p * (dp - delta)).astype(BF)
        dv_acc[part, pl.ds(key, key_len), :] += jnp.dot(
            p.astype(BF), do, preferred_element_type=F32
        )
        dk_acc[part, pl.ds(key, key_len), :] += jnp.dot(ds, q, preferred_element_type=F32)
        dq_acc[pl.ds(row, TILE), :] += contract_first(ds, k)

    for part in range(2):

        @pl.when(i > ids[part])
        def _(part=part):
            for row in range(0, CHUNK, TILE):
                for key in range(0, CHUNK, TILE):
                    tile(part, row, key, TILE, False)

        @pl.when(i == ids[part])
        def _(part=part):
            for row in range(0, CHUNK, TILE):
                for key in range(0, row + 1, TILE):
                    tile(part, row, key, TILE, key == row)

    dq_ref[...] = (dq_acc[...] * scale).astype(BF)

    @pl.when(i == n_chunk - 1)
    def _():
        dk_ref[...] = (dk_acc[...] * scale).astype(BF)
        dv_ref[...] = dv_acc[...].astype(BF)


def attention(k, v, q_all, do_all, lse, delta_all, scale):
    total, head = q_all.shape
    n_chunk = total // CHUNK
    per = do_all.shape[1] // CHUNK
    whole = pl.BlockSpec((2, CHUNK, head), lambda i: (0, 0, 0))
    return pl.pallas_call(
        functools.partial(attention_kernel, scale, n_chunk),
        grid=(n_chunk,),
        out_shape=(
            jax.ShapeDtypeStruct((total, head), BF),
            jax.ShapeDtypeStruct(k.shape, BF),
            jax.ShapeDtypeStruct(v.shape, BF),
        ),
        in_specs=[
            whole,
            whole,
            pl.BlockSpec((CHUNK, head), lambda i: (i, 0)),
            pl.BlockSpec((1, CHUNK, head), lambda i: (i // per, i % per, 0)),
            pl.BlockSpec((1, CHUNK), lambda i: (0, i)),
            pl.BlockSpec((1, 1, CHUNK), lambda i: (i // per, 0, i % per)),
        ],
        out_specs=(pl.BlockSpec((CHUNK, head), lambda i: (i, 0)), whole, whole),
        scratch_shapes=[
            VM((2, CHUNK, head), F32),
            VM((2, CHUNK, head), F32),
            VM((CHUNK, head), F32),
        ],
        compiler_params=pltpu.CompilerParams(
            dimension_semantics=("arbitrary",), vmem_limit_bytes=VLIM
        ),
        cost_estimate=pl.CostEstimate(
            flops=40 * 10**9, bytes_accessed=20 * 10**6, transcendentals=17 * 10**6
        ),
    )(k, v, q_all, do_all, lse, delta_all)


def body(
    moe_input,
    out_grad,
    w_gate,
    w_up,
    w_down,
    expert_picks,
    gate_probs,
    queries,
    attn_keys,
    values,
    attn_out,
    log_norm,
    w_out,
):
    n_ctx = lax.axis_size("ctx")
    n_exp = lax.axis_size("exp")
    ctx_id = lax.axis_index("ctx")
    exp_id = lax.axis_index("exp")
    tok_dev, feat_width = moe_input.shape
    n_local = w_gate.shape[0]
    group_picks = expert_picks.shape[1] // n_ctx
    tok_ctx, head_dim = queries.shape
    key_scale = head_dim ** (-0.5)
    i32 = jnp.int32

    og_all = lax.all_gather(out_grad, "exp", axis=0, tiled=True)
    q_all = lax.all_gather(queries, "ctx", axis=0, tiled=True)

    half = tok_ctx // 2
    top = 2 * n_ctx - 1
    to_even = [(g, 2 * g if g < n_ctx // 2 else top - 2 * g) for g in range(n_ctx)]
    to_odd = [(g, 2 * g + 1 if g < n_ctx // 2 else top - 1 - 2 * g) for g in range(n_ctx)]
    kv = jnp.stack([attn_keys, values])
    kv_first = lax.ppermute(kv[:, :half], "ctx", to_even)
    kv_second = lax.ppermute(kv[:, half:], "ctx", to_odd)
    k_dealt = jnp.stack([kv_first[0], kv_second[0]])
    v_dealt = jnp.stack([kv_first[1], kv_second[1]])

    base_row = (ctx_id * n_exp + exp_id) * tok_dev
    below = jnp.sum((expert_picks < base_row).astype(i32), axis=1, keepdims=True)
    inside = (expert_picks >= base_row) & (expert_picks < base_row + tok_dev)
    spot = jnp.arange(expert_picks.shape[1], dtype=i32)[None, :] - below
    local = expert_picks - base_row
    chosen = jnp.stack(
        [jnp.sum(jnp.where(inside & (spot == s), local + 1, 0), axis=1) - 1 for s in range(MOST)],
        axis=1,
    )
    chosen = chosen.reshape(n_exp, n_local * MOST)
    away = jnp.full_like(chosen, -1)
    columns = jnp.arange(2 * tok_dev, dtype=i32)
    wanted = jnp.stack(
        [chosen, jnp.where(chosen >= 0, chosen + tok_dev, away)], axis=1
    ).reshape(-1)
    pick = (wanted[:, None] == columns[None, :]).astype(BF)

    my_picks = lax.dynamic_slice(
        expert_picks, (exp_id * n_local, ctx_id * group_picks), (n_local, group_picks)
    )
    block_of = my_picks // tok_dev
    src_exp = block_of - ctx_id * n_exp
    slot_rank = jnp.arange(group_picks, dtype=i32)[None, :] - jnp.sum(
        (my_picks[:, None, :] < (block_of * tok_dev)[:, :, None]).astype(i32), axis=2
    )
    dist = lax.rem(exp_id - src_exp + n_exp, n_exp)
    spot_x = dist * 8 + jnp.arange(n_local, dtype=i32)[:, None] * MOST + slot_rank
    spots = jnp.stack([spot_x, spot_x + n_local * MOST]).reshape(-1)
    place = (spots[:, None] == jnp.arange(8 * n_exp, dtype=i32)[None, :]).astype(BF)

    slots = dispatch(moe_input, out_grad, pick, place)
    slots = slots.reshape(2, n_local, n_ctx * group_picks, feat_width)
    slot_rows, slot_grads = slots[0], slots[1]

    gate_rows = lax.dynamic_slice_in_dim(gate_probs, exp_id * n_local, n_local, 0)
    pre_gate = jnp.einsum("kcd,kdf->kcf", slot_rows, w_gate, preferred_element_type=F32)
    pre_up = jnp.einsum("kcd,kdf->kcf", slot_rows, w_up, preferred_element_type=F32)
    gated_act, act_slope = activation(pre_gate)
    hidden_full = gated_act * pre_up
    hidden = hidden_full.astype(BF)
    down_back = jnp.einsum("kcd,kfd->kcf", slot_grads, w_down, preferred_element_type=F32)
    gate_part = jnp.sum(down_back * hidden_full, axis=2).astype(BF)
    scaled = gate_rows[..., None] * down_back
    d_gate = (scaled * pre_up * act_slope).astype(BF)
    d_up = (scaled * gated_act).astype(BF)
    dx_part = (
        jnp.einsum("kcf,kdf->kcd", d_gate, w_gate, preferred_element_type=F32)
        + jnp.einsum("kcf,kdf->kcd", d_up, w_up, preferred_element_type=F32)
    ).astype(BF)
    d_gates = lax.psum_scatter(gate_part, "ctx", scatter_dimension=1, tiled=True).astype(F32)

    dx_all = combine(dx_part.reshape(n_local, n_ctx, group_picks, feat_width))
    dx_all = dx_all.reshape(-1, feat_width)

    weighted = (gate_rows[..., None] * slot_grads.astype(F32)).astype(BF)
    dw_down = jnp.einsum("kcf,kcd->kfd", hidden, weighted, preferred_element_type=F32).astype(BF)
    dw_gate = jnp.einsum("kcd,kcf->kdf", slot_rows, d_gate, preferred_element_type=F32).astype(BF)
    dw_up = jnp.einsum("kcd,kcf->kdf", slot_rows, d_up, preferred_element_type=F32).astype(BF)

    group_ids = lax.dynamic_slice_in_dim(
        expert_picks, ctx_id * group_picks, group_picks, 1
    ).reshape(-1) - ctx_id * tok_ctx
    spread_hot = (jnp.arange(tok_ctx, dtype=i32)[:, None] == group_ids[None, :]).astype(BF)
    own_hot = (
        (jnp.arange(tok_dev, dtype=i32) + exp_id * tok_dev)[:, None] == group_ids[None, :]
    ).astype(BF)
    d_resid = (
        out_grad.astype(F32) + jnp.dot(own_hot, dx_all, preferred_element_type=F32)
    ).astype(BF)

    d_out_base = contract_last(og_all, w_out)
    dx_out = contract_last(dx_all, w_out).astype(BF)
    d_out = (d_out_base + jnp.dot(spread_hot, dx_out, preferred_element_type=F32)).astype(BF)
    product = d_out.astype(F32) * attn_out.astype(F32)
    delta = lax.dot_general(
        jnp.ones((1, head_dim), F32), product, (((1,), (1,)), ((), ())),
        precision=lax.Precision.HIGHEST, preferred_element_type=F32,
    )
    do_all, delta_all = spread(d_out, delta)

    dq, dk, dv = attention(k_dealt, v_dealt, q_all, do_all, log_norm, delta_all, key_scale)

    out_taken = contract_first(spread_hot, attn_out).astype(BF)
    dw_part = contract_first(attn_out, og_all) + contract_first(out_taken, dx_all)
    dw_part = dw_part.astype(BF).reshape(head_dim, n_ctx, -1).transpose(1, 0, 2)

    back = jnp.stack([dk, dv], axis=1)
    from_even = [(b, a) for a, b in to_even]
    from_odd = [(b, a) for a, b in to_odd]
    kv_low = lax.ppermute(back[0], "ctx", from_even)
    kv_high = lax.ppermute(back[1], "ctx", from_odd)
    grad_kv = jnp.concatenate([kv_low, kv_high], axis=1)
    grad_q, dw_out = settle_grads(dq.reshape(n_ctx, tok_ctx, head_dim), dw_part)
    return (
        d_resid, dw_gate, dw_up, dw_down, d_gates, dw_out, grad_q, grad_kv[0], grad_kv[1],
    )


def solution(mesh):
    return jax.shard_map(
        body,
        mesh=mesh,
        in_specs=(
            P(("ctx", "exp"), None),
            P(("ctx", "exp"), None),
            P("exp", None, "ctx"),
            P("exp", None, "ctx"),
            P("exp", "ctx", None),
            P(),
            P(),
            P("ctx", "exp"),
            P("ctx", "exp"),
            P("ctx", "exp"),
            P("ctx", "exp"),
            P("exp", None),
            P("exp", None),
        ),
        out_specs=(
            P(("ctx", "exp"), None),
            P("exp", None, "ctx"),
            P("exp", None, "ctx"),
            P("exp", "ctx", None),
            P("exp", "ctx"),
            P("exp", "ctx"),
            P("ctx", "exp"),
            P("ctx", "exp"),
            P("ctx", "exp"),
        ),
        check_vma=False,
    )
```

```python
import functools
import math

import jax
import jax.numpy as jnp
from jax import lax
from jax.experimental import pallas as pl
from jax.experimental.pallas import tpu as pltpu
from jax.sharding import PartitionSpec as P

MOST = 2
MESH = pl.DeviceIdType.MESH
LOG2E = 1.4426950408889634
BF = jnp.bfloat16
F32 = jnp.float32
VLIM = 56 * 1024 * 1024
VM = pltpu.VMEM


def activation(pre_act):
    sigmoid_val = jax.nn.sigmoid(pre_act)
    return (pre_act * sigmoid_val, sigmoid_val * (1.0 + pre_act * (1.0 - sigmoid_val)))


def contract_first(left, right):
    return lax.dot_general(left, right, (((0,), (0,)), ((), ())), preferred_element_type=F32)


def contract_last(left, right):
    return lax.dot_general(left, right, (((1,), (1,)), ((), ())), preferred_element_type=F32)


class Place:
    def __init__(self, axis):
        self.axis = axis
        me = lax.axis_index(axis)
        if axis == "ctx":
            step, span = 1, 4
        else:
            step, span = 2, 8
        low = lax.rem(me, step)
        pos = lax.rem(me // step, 4)
        row = me // span
        other = 1 - row

        def at(r, p):
            return r * span + lax.rem(p + 4, 4) * step + low

        self.me = me
        self.up, self.down, self.far = at(row, pos + 1), at(row, pos - 1), at(row, pos + 2)
        self.mate = at(other, pos)
        self.mate_up, self.mate_down = at(other, pos + 1), at(other, pos - 1)
        self.mate_far = at(other, pos + 2)


def greet(peers):
    barrier = pltpu.get_barrier_semaphore()
    for axis, dev in peers:
        pl.semaphore_signal(barrier, inc=1, device_id={axis: dev}, device_id_type=MESH)
    pl.semaphore_wait(barrier, len(peers))


class Lanes:
    def __init__(self, send_sems, recv_sems):
        self.send_sems, self.recv_sems, self.sent = send_sems, recv_sems, []

    def copy(self, k, src, dst, axis, dev):
        return pltpu.make_async_remote_copy(
            src_ref=src,
            dst_ref=dst,
            send_sem=self.send_sems.at[k],
            recv_sem=self.recv_sems.at[k],
            device_id={axis: dev},
            device_id_type=MESH,
        )

    def send(self, k, src, dst, axis, dev):
        one = self.copy(k, src, dst, axis, dev)
        one.start()
        self.sent.append(one)

    def recv(self, k, dst, axis, dev):
        self.copy(k, dst, dst, axis, dev).wait_recv()

    def finish(self):
        for one in self.sent:
            one.wait_send()


AG_LANES = 14


def gather_ring(pieces, place, lanes, base, arrived=None, work=()):
    axis = place.axis
    n = len(pieces)
    work = list(work)

    def fill():
        if work:
            work.pop(0)()

    def send(k, block, half, dev):
        for i, piece in enumerate(pieces):
            lanes.send(base + k * n + i, piece(block, half), piece(block, half), axis, dev)

    def recv(k, block, half, dev):
        for i, piece in enumerate(pieces):
            lanes.recv(base + k * n + i, piece(block, half), axis, dev)
        if arrived is not None:
            arrived(k, block, half)

    p = place
    send(0, p.me, 0, p.mate)
    send(2, p.me, 0, p.up)
    send(4, p.me, 1, p.down)
    send(1, p.me, 1, p.mate)
    send(3, p.me, 1, p.up)
    send(5, p.me, 0, p.down)
    fill()
    recv(2, p.down, 0, p.down)
    send(6, p.down, 0, p.up)
    recv(4, p.up, 1, p.up)
    send(7, p.up, 1, p.down)
    fill()
    recv(0, p.mate, 0, p.mate)
    send(8, p.mate, 0, p.up)
    send(10, p.mate, 0, p.down)
    fill()
    recv(1, p.mate, 1, p.mate)
    send(11, p.mate, 1, p.down)
    send(9, p.mate, 1, p.up)
    fill()
    recv(8, p.mate_down, 0, p.down)
    send(12, p.mate_down, 0, p.up)
    recv(11, p.mate_up, 1, p.up)
    send(13, p.mate_up, 1, p.down)
    while work:
        fill()
    recv(3, p.down, 1, p.down)
    recv(5, p.up, 0, p.up)
    recv(6, p.far, 0, p.down)
    recv(7, p.far, 1, p.up)
    recv(10, p.mate_up, 0, p.up)
    recv(9, p.mate_down, 1, p.down)
    recv(12, p.mate_far, 0, p.down)
    recv(13, p.mate_far, 1, p.up)


def add_into(dst, *srcs):
    total = srcs[0][...].astype(F32)
    for src in srcs[1:]:
        total = total + src[...].astype(F32)
    dst[...] = total.astype(dst.dtype)


def scatter_ring(parts, place, lanes, base, bufs, outs):
    axis = place.axis
    n = len(parts)
    p = place
    groups = (
        (p.mate_far, p.mate_up, p.mate_down, p.mate),
        (p.far, p.up, p.down, p.me),
    )

    def slot(i, s):
        return bufs[i](s)

    def send(k, i, src, s, dev):
        lanes.send(base + k * n + i, src, slot(i, s), axis, dev)

    def recv(k, i, s, dev):
        lanes.recv(base + k * n + i, slot(i, s), axis, dev)

    every = range(n)
    for g, (far, up, down, own) in enumerate(groups):
        for i in every:
            send(6 * g + 0, i, parts[i](far, 0), 6 * g + 0, p.up)
            send(6 * g + 1, i, parts[i](far, 1), 6 * g + 1, p.down)
        for i in every:
            send(6 * g + 3, i, parts[i](up, 1), 6 * g + 3, p.up)
            send(6 * g + 4, i, parts[i](down, 0), 6 * g + 4, p.down)
        if g == 0:
            continue
    for g, (far, up, down, own) in enumerate(groups):
        for i in every:
            recv(6 * g + 0, i, 6 * g + 0, p.down)
            add_into(slot(i, 6 * g + 0), slot(i, 6 * g + 0), parts[i](up, 0))
            send(6 * g + 2, i, slot(i, 6 * g + 0), 6 * g + 2, p.up)
            recv(6 * g + 1, i, 6 * g + 1, p.up)
            add_into(slot(i, 6 * g + 1), slot(i, 6 * g + 1), parts[i](down, 1))
            send(6 * g + 5, i, slot(i, 6 * g + 1), 6 * g + 5, p.down)
    far, up, down, own = groups[0]
    for half in (1, 0):
        for i in every:
            recv(2 + half, i, 2 + half, p.down)
            recv(4 + half, i, 4 + half, p.up)
            add_into(slot(i, 2 + half), slot(i, 2 + half), slot(i, 4 + half), parts[i](own, half))
            send(12 + half, i, slot(i, 2 + half), 12 + half, p.mate)
    for half in (1, 0):
        for i in every:
            recv(8 + half, i, 8 + half, p.down)
            recv(10 + half, i, 10 + half, p.up)
            recv(12 + half, i, 12 + half, p.mate)
            add_into(
                outs[i](half),
                slot(i, 8 + half),
                slot(i, 10 + half),
                slot(i, 12 + half),
                parts[i](p.me, half),
            )


def around(place):
    return [(place.axis, place.up), (place.axis, place.down), (place.axis, place.mate)]


def deal_targets(g, n):
    low = g < n // 2
    return jnp.where(low, 2 * g, 2 * n - 1 - 2 * g), jnp.where(low, 2 * g + 1, 2 * n - 2 - 2 * g)


def deal_sources(c, n):
    even = lax.rem(c, 2) == 0
    first = jnp.where(even, c // 2, (2 * n - 1 - c) // 2)
    second = jnp.where(even, (2 * n - 2 - c) // 2, (c - 1) // 2)
    return first, second


def trade_start(lanes, base, moves, me):
    for j, (src, dst, to, _) in enumerate(moves):

        @pl.when(to != me)
        def _(j=j, src=src, dst=dst, to=to):
            lanes.copy(base + j, src, dst, "ctx", to).start()


def trade_finish(lanes, base, moves, me):
    for j, (src, dst, to, frm) in enumerate(moves):

        @pl.when(to == me)
        def _(src=src, dst=dst):
            dst[...] = src[...]

        @pl.when(frm != me)
        def _(j=j, src=src, dst=dst, frm=frm):
            lanes.copy(base + j, src, dst, "ctx", frm).wait_recv()

        @pl.when(to != me)
        def _(j=j, src=src, dst=dst, to=to):
            lanes.copy(base + j, src, dst, "ctx", to).wait_send()


def dispatch_kernel(
    n_ctx, mi_ref, og_ref, pick_ref, place_ref, key_ref, val_ref,
    mine_ref, k_out, v_out, send, got, ss, rs,
):
    me = lax.axis_index("exp")
    ctx_me = lax.axis_index("ctx")
    n_exp = send.shape[0]
    half = key_ref.shape[0] // 2
    greet(
        [("exp", lax.rem(me + d, n_exp)) for d in range(1, n_exp)]
        + [("ctx", lax.rem(ctx_me + d, n_ctx)) for d in range(1, n_ctx)]
    )
    lanes = Lanes(ss, rs)
    rows = jnp.dot(pick_ref[:, :128], mi_ref[...], preferred_element_type=F32)
    rows = rows + jnp.dot(pick_ref[:, 128:], og_ref[...], preferred_element_type=F32)
    send[...] = rows.reshape(n_exp, 8, rows.shape[1]).astype(BF)
    for d in range(1, n_exp):
        to = lax.rem(me + d, n_exp)
        lanes.send(d - 1, send.at[to], got.at[d], "exp", to)
    targets, sources = deal_targets(ctx_me, n_ctx), deal_sources(ctx_me, n_ctx)
    moves = [
        (ref.at[pl.ds(h * half, half)], out.at[h], targets[h], sources[h])
        for h in range(2)
        for ref, out in ((key_ref, k_out), (val_ref, v_out))
    ]
    trade_start(lanes, n_exp - 1, moves, ctx_me)
    got[0] = send[me]
    for d in range(1, n_exp):
        lanes.recv(d - 1, got.at[d], "exp", lax.rem(me + n_exp - d, n_exp))
    flat = got[...].astype(F32).reshape(n_exp * 8, got.shape[2]).astype(BF)
    mine = jnp.dot(place_ref[...], flat, preferred_element_type=F32).astype(BF)
    mine_ref[...] = mine.reshape(2, 2, 16, got.shape[2])
    trade_finish(lanes, n_exp - 1, moves, ctx_me)
    lanes.finish()


def dispatch(moe_input, out_grad, pick, place, keys, values):
    n_exp, n_ctx = lax.axis_size("exp"), lax.axis_size("ctx")
    width = moe_input.shape[1]
    dealt = jax.ShapeDtypeStruct((2, keys.shape[0] // 2, keys.shape[1]), BF)
    n_sem = n_exp - 1 + 4
    return pl.pallas_call(
        functools.partial(dispatch_kernel, n_ctx),
        out_shape=(jax.ShapeDtypeStruct((2, 2, 16, width), BF), dealt, dealt),
        in_specs=[pl.BlockSpec(memory_space=VM)] * 6,
        out_specs=(pl.BlockSpec(memory_space=VM),) * 3,
        scratch_shapes=[
            VM((n_exp, 8, width), BF),
            VM((n_exp, 8, width), BF),
            pltpu.SemaphoreType.DMA((n_sem,)),
            pltpu.SemaphoreType.DMA((n_sem,)),
        ],
        compiler_params=pltpu.CompilerParams(
            collective_id=1, has_side_effects=True, vmem_limit_bytes=VLIM
        ),
        cost_estimate=pl.CostEstimate(flops=10**6, bytes_accessed=10**6, transcendentals=0),
    )(moe_input, out_grad, pick, place, keys, values)


def share_kernel(mine_ref, out_ref, ss, rs):
    ctx = Place("ctx")
    greet(around(ctx))
    lanes = Lanes(ss, rs)
    for a in range(2):
        for k in range(2):
            out_ref[a, k, ctx.me] = mine_ref[a, k]
    gather_ring([lambda block, half: out_ref.at[half, :, block]], ctx, lanes, 0)
    lanes.finish()


def share(mine):
    n_ctx = lax.axis_size("ctx")
    return pl.pallas_call(
        share_kernel,
        out_shape=jax.ShapeDtypeStruct(mine.shape[:2] + (n_ctx,) + mine.shape[2:], BF),
        in_specs=[pl.BlockSpec(memory_space=VM)],
        out_specs=pl.BlockSpec(memory_space=VM),
        scratch_shapes=[
            pltpu.SemaphoreType.DMA((AG_LANES,)),
            pltpu.SemaphoreType.DMA((AG_LANES,)),
        ],
        compiler_params=pltpu.CompilerParams(
            collective_id=5, has_side_effects=True, vmem_limit_bytes=VLIM
        ),
        cost_estimate=pl.CostEstimate(flops=10**6, bytes_accessed=10**6, transcendentals=0),
    )(mine)


def combine_kernel(part_ref, gate_ref, out_ref, gate_out, buf, gate_buf, ss, rs):
    ctx, exp = Place("ctx"), Place("exp")
    twin = exp.me + 1 - 2 * lax.rem(exp.me, 2)
    greet(around(ctx) + around(exp) + [("exp", twin)])
    lanes = Lanes(ss, rs)
    scatter_ring(
        [
            lambda block, half: part_ref.at[half, block],
            lambda block, half: gate_ref.at[half, block],
        ],
        ctx,
        lanes,
        0,
        [lambda s: buf.at[s], lambda s: gate_buf.at[s]],
        [lambda half: out_ref.at[exp.me, half], lambda half: gate_out.at[half]],
    )

    def piece(block, half):
        return out_ref.at[block, half]

    base = 2 * AG_LANES
    over = 3 * AG_LANES
    flip = 1 - 2 * lax.rem(exp.me, 2)
    for half in range(2):
        lanes.send(over + 14 + half, piece(exp.me, half), piece(exp.me, half), "exp", twin)

    def arrived(k, block, half):
        lanes.send(over + k, piece(block, half), piece(block, half), "exp", twin)

    gather_ring([piece], exp, lanes, base, arrived)
    srcs = {
        0: (exp.mate, 0), 1: (exp.mate, 1), 2: (exp.down, 0), 3: (exp.down, 1),
        4: (exp.up, 1), 5: (exp.up, 0), 6: (exp.far, 0), 7: (exp.far, 1),
        8: (exp.mate_down, 0), 9: (exp.mate_down, 1), 10: (exp.mate_up, 0),
        11: (exp.mate_up, 1), 12: (exp.mate_far, 0), 13: (exp.mate_far, 1),
        14: (exp.me, 0), 15: (exp.me, 1),
    }
    for k, (block, half) in srcs.items():
        lanes.recv(over + k, piece(block + flip, half), "exp", twin)
    lanes.finish()


def combine(part, gate_part):
    n_exp = lax.axis_size("exp")
    rows, width = part.shape[2:]
    n_sem = 3 * AG_LANES + 16
    return pl.pallas_call(
        combine_kernel,
        out_shape=(
            jax.ShapeDtypeStruct((n_exp, 2, rows, width), BF),
            jax.ShapeDtypeStruct((2,) + gate_part.shape[2:], F32),
        ),
        in_specs=[pl.BlockSpec(memory_space=VM)] * 2,
        out_specs=(pl.BlockSpec(memory_space=VM),) * 2,
        scratch_shapes=[
            VM((14, rows, width), BF),
            VM((14,) + gate_part.shape[2:], F32),
            pltpu.SemaphoreType.DMA((n_sem,)),
            pltpu.SemaphoreType.DMA((n_sem,)),
        ],
        compiler_params=pltpu.CompilerParams(
            collective_id=2, has_side_effects=True, vmem_limit_bytes=VLIM
        ),
        cost_estimate=pl.CostEstimate(flops=10**6, bytes_accessed=10**6, transcendentals=0),
    )(part, gate_part)


def spread_kernel(
    do_ref, delta_ref, og_ref, o_ref, taken_ref, dx_ref,
    do_all, delta_all, dw_ref, og_buf, dw_acc, ss, rs, load_sems,
):
    ctx = Place("ctx")
    greet(around(ctx))
    lanes = Lanes(ss, rs)
    do_all[ctx.me] = do_ref[...]
    delta_all[ctx.me] = delta_ref[...]
    rows = do_ref.shape[0] // 2
    load_rows = og_buf.shape[1]
    n_load = og_ref.shape[0] // load_rows
    n_out, _, part = dw_ref.shape

    def load(j):
        slot = lax.rem(j, 2)
        return pltpu.make_async_copy(
            og_ref.at[pl.ds(j * load_rows, load_rows)], og_buf.at[slot], load_sems.at[slot]
        )

    load(0).start()
    dw_acc[...] = jnp.zeros_like(dw_acc)

    def add_rows(j, carry):
        @pl.when(j + 1 < n_load)
        def _():
            load(j + 1).start()

        load(j).wait()
        o = o_ref[pl.ds(j * load_rows, load_rows), :]
        slot = lax.rem(j, 2)
        for b in range(n_out):
            cols = pl.ds(b * part, part)
            dw_acc[:, cols] += contract_first(o, og_buf[slot, :, cols])
        return carry

    def stretch(first, last):
        return lambda: lax.fori_loop(first, last, add_rows, 0)

    def close():
        for b in range(n_out):
            cols = pl.ds(b * part, part)
            total = dw_acc[:, cols] + contract_first(taken_ref[...], dx_ref[:, cols])
            dw_ref[b] = total.astype(BF)

    quarter = n_load // 4
    work = [stretch(j * quarter, (j + 1) * quarter) for j in range(4)] + [close]

    def piece_do(block, half):
        return do_all.at[block, pl.ds(half * rows, rows)]

    def piece_delta(block, half):
        return delta_all.at[block, :, pl.ds(half * rows, rows)]

    gather_ring([piece_do, piece_delta], ctx, lanes, 0, work=work)
    lanes.finish()


def spread(d_out, delta, og_all, attn_out, out_taken, dx_all):
    n_ctx = lax.axis_size("ctx")
    n_sem = 2 * AG_LANES
    width = og_all.shape[1]
    head = d_out.shape[1]
    vmem = pl.BlockSpec(memory_space=VM)
    return pl.pallas_call(
        spread_kernel,
        out_shape=(
            jax.ShapeDtypeStruct((n_ctx,) + d_out.shape, BF),
            jax.ShapeDtypeStruct((n_ctx,) + delta.shape, F32),
            jax.ShapeDtypeStruct((n_ctx, head, width // n_ctx), BF),
        ),
        in_specs=[vmem, vmem, pl.BlockSpec(memory_space=pl.ANY), vmem, vmem, vmem],
        out_specs=(vmem,) * 3,
        scratch_shapes=[
            VM((2, 256, width), BF),
            VM((head, width), F32),
            pltpu.SemaphoreType.DMA((n_sem,)),
            pltpu.SemaphoreType.DMA((n_sem,)),
            pltpu.SemaphoreType.DMA((2,)),
        ],
        compiler_params=pltpu.CompilerParams(
            collective_id=3, has_side_effects=True, vmem_limit_bytes=VLIM
        ),
        cost_estimate=pl.CostEstimate(flops=10**6, bytes_accessed=10**6, transcendentals=0),
    )(d_out, delta, og_all, attn_out, out_taken, dx_all)


CHUNK = 1024
TILE = 512


def attention_kernel(
    scale, n_ctx, k_ref, v_ref, q_ref, do_ref, lse_ref, delta_ref, dw_ref,
    gq_out, gw_out, gk_out, gv_out,
    dq_part, dk_acc, dv_acc, dq_acc, back, dq_buf, dw_buf, ss, rs,
):
    p = Place("ctx")
    c = p.me
    greet([("ctx", lax.rem(c + d, n_ctx)) for d in range(1, n_ctx)])
    lanes = Lanes(ss, rs)
    n_chunk = 2 * n_ctx
    first = jnp.where(lax.rem(c, 2) == 0, c, n_chunk - 1 - c)
    ids = (first, n_chunk - 1 - first)
    dk_acc[...] = jnp.zeros_like(dk_acc)
    dv_acc[...] = jnp.zeros_like(dv_acc)

    def tile(part, group, half, row, key, masked):
        at = half * CHUNK + row
        spot = group * 2 * CHUNK + at
        q = q_ref[pl.ds(spot, TILE), :]
        do = do_ref[group, pl.ds(at, TILE), :]
        lse = lse_ref[:, pl.ds(spot, TILE)] * LOG2E
        delta = delta_ref[group, :, pl.ds(at, TILE)]
        k = k_ref[part, pl.ds(key, TILE), :]
        v = v_ref[part, pl.ds(key, TILE), :]
        s = contract_last(k, q) * (scale * LOG2E) - lse
        if masked:
            rk = lax.broadcasted_iota(jnp.int32, s.shape, 0)
            cq = lax.broadcasted_iota(jnp.int32, s.shape, 1)
            s = jnp.where(rk <= cq, s, -1e30)
        probs = jnp.exp2(s)
        dp = contract_last(v, do)
        ds = (probs * (dp - delta)).astype(BF)
        dv_acc[part, pl.ds(key, TILE), :] += jnp.dot(
            probs.astype(BF), do, preferred_element_type=F32
        )
        dk_acc[part, pl.ds(key, TILE), :] += jnp.dot(ds, q, preferred_element_type=F32)
        dq_acc[pl.ds(row, TILE), :] += contract_first(ds, k)

    w_rows = dw_ref.shape[1] // 2
    parts = (
        lambda block, h: dq_part.at[block, pl.ds(h * CHUNK, CHUNK)],
        lambda block, h: dw_ref.at[block, pl.ds(h * w_rows, w_rows)],
    )
    slots = (lambda s: dq_buf.at[s], lambda s: dw_buf.at[s])
    n = len(parts)

    def send(k, src, dev):
        for i in range(n):
            lanes.copy(k * n + i, src[i], slots[i](k), "ctx", dev).start()

    def recv(k, dev):
        for i in range(n):
            lanes.copy(k * n + i, slots[i](k), slots[i](k), "ctx", dev).wait_recv()

    def terms(block, h):
        return [parts[i](block, h) for i in range(n)]

    def plain(k, block, h, dev):
        send(k, terms(block, h), dev)

    def summed(k, into, others, block, h, dev):
        for i in range(n):
            add_into(
                slots[i](into), slots[i](into), *[slots[i](o) for o in others], parts[i](block, h)
            )
        send(k, [slots[i](into) for i in range(n)], dev)

    def near_up():
        recv(0, p.down)
        summed(2, 0, (), p.mate_up, 0, p.up)

    def near_down():
        recv(1, p.up)
        summed(5, 1, (), p.mate_down, 1, p.down)

    def over(h):
        recv(2 + h, p.down)
        recv(4 + h, p.up)
        summed(12 + h, 2 + h, (4 + h,), p.mate, h, p.mate)

    def own_up():
        recv(6, p.down)
        summed(8, 6, (), p.up, 0, p.up)

    def own_down():
        recv(7, p.up)
        summed(11, 7, (), p.down, 1, p.down)

    plan = {
        0: [lambda: plain(0, p.mate_far, 0, p.up)],
        1: [lambda: plain(1, p.mate_far, 1, p.down)],
        3: [lambda: plain(3, p.mate_up, 1, p.up)],
        4: [lambda: plain(4, p.mate_down, 0, p.down)],
        8: [lambda: plain(6, p.far, 0, p.up), near_up],
        9: [lambda: plain(7, p.far, 1, p.down), near_down],
        11: [lambda: plain(9, p.up, 1, p.up), own_up, lambda: over(0)],
        12: [lambda: plain(10, p.down, 0, p.down), lambda: over(1)],
        13: [own_down],
    }
    order = [p.mate_far, p.mate_up, p.mate_down, p.mate, p.far, p.up, p.down, p.me]

    def step(t, carry):
        place = t // 2
        half = lax.rem(t, 2)
        group = order[0]
        for j in range(1, len(order)):
            group = jnp.where(place == j, order[j], group)
        chunk = 2 * group + half
        dq_acc[...] = jnp.zeros_like(dq_acc)
        for part in range(2):

            @pl.when(chunk > ids[part])
            def _(part=part):
                for row in range(0, CHUNK, TILE):
                    for key in range(0, CHUNK, TILE):
                        tile(part, group, half, row, key, False)

            @pl.when(chunk == ids[part])
            def _(part=part):
                for row in range(0, CHUNK, TILE):
                    for key in range(0, row + 1, TILE):
                        tile(part, group, half, row, key, key == row)

        dq_part[group, pl.ds(half * CHUNK, CHUNK), :] = (dq_acc[...] * scale).astype(BF)
        for when, acts in plan.items():

            @pl.when(t == when)
            def _(acts=acts):
                for act in acts:
                    act()

        return carry

    lax.fori_loop(0, n_chunk, step, 0)

    targets, sources = deal_targets(c, n_ctx), deal_sources(c, n_ctx)
    for part in range(2):
        back[part, 0] = (dk_acc[part] * scale).astype(BF)
        back[part, 1] = dv_acc[part].astype(BF)
    moves = [
        (back.at[h, j], out.at[pl.ds(h * CHUNK, CHUNK)], sources[h], targets[h])
        for h in range(2)
        for j, out in enumerate((gk_out, gv_out))
    ]
    base = n * AG_LANES
    trade_start(lanes, base, moves, c)
    finals = (
        lambda h: gq_out.at[pl.ds(h * CHUNK, CHUNK)],
        lambda h: gw_out.at[pl.ds(h * w_rows, w_rows)],
    )
    for h in range(2):
        recv(8 + h, p.down)
        recv(10 + h, p.up)
        recv(12 + h, p.mate)
        for i in range(n):
            add_into(
                finals[i](h), slots[i](8 + h), slots[i](10 + h), slots[i](12 + h),
                parts[i](p.me, h),
            )
    for k in range(AG_LANES):
        for i in range(n):
            lanes.copy(k * n + i, slots[i](k), slots[i](k), "ctx", p.up).wait_send()
    trade_finish(lanes, base, moves, c)


def attention(k, v, q_all, do_all, lse, delta_all, dw_part, scale):
    total, head = q_all.shape
    n_ctx, tok_ctx, _ = do_all.shape
    vmem = pl.BlockSpec(memory_space=VM)
    own = jax.ShapeDtypeStruct((tok_ctx, head), BF)
    n_sem = 2 * AG_LANES + 4
    return pl.pallas_call(
        functools.partial(attention_kernel, scale, n_ctx),
        out_shape=(own, jax.ShapeDtypeStruct(dw_part.shape[1:], BF), own, own),
        in_specs=[vmem] * 7,
        out_specs=(vmem,) * 4,
        scratch_shapes=[
            VM(do_all.shape, BF),
            VM((2, CHUNK, head), F32),
            VM((2, CHUNK, head), F32),
            VM((CHUNK, head), F32),
            VM((2, 2, CHUNK, head), BF),
            VM((AG_LANES, CHUNK, head), BF),
            VM((AG_LANES, dw_part.shape[1] // 2, dw_part.shape[2]), BF),
            pltpu.SemaphoreType.DMA((n_sem,)),
            pltpu.SemaphoreType.DMA((n_sem,)),
        ],
        compiler_params=pltpu.CompilerParams(
            collective_id=4, has_side_effects=True, vmem_limit_bytes=VLIM
        ),
        cost_estimate=pl.CostEstimate(
            flops=40 * 10**9, bytes_accessed=20 * 10**6, transcendentals=17 * 10**6
        ),
    )(k, v, q_all, do_all, lse, delta_all, dw_part)


def body(
    moe_input,
    out_grad,
    w_gate,
    w_up,
    w_down,
    expert_picks,
    gate_probs,
    queries,
    attn_keys,
    values,
    attn_out,
    log_norm,
    w_out,
):
    n_ctx = lax.axis_size("ctx")
    n_exp = lax.axis_size("exp")
    ctx_id = lax.axis_index("ctx")
    exp_id = lax.axis_index("exp")
    tok_dev, feat_width = moe_input.shape
    n_local = w_gate.shape[0]
    group_picks = expert_picks.shape[1] // n_ctx
    tok_ctx, head_dim = queries.shape
    key_scale = head_dim ** (-0.5)
    i32 = jnp.int32

    base_row = (ctx_id * n_exp + exp_id) * tok_dev
    below = jnp.sum((expert_picks < base_row).astype(i32), axis=1, keepdims=True)
    inside = (expert_picks >= base_row) & (expert_picks < base_row + tok_dev)
    spot = jnp.arange(expert_picks.shape[1], dtype=i32)[None, :] - below
    local = expert_picks - base_row
    chosen = jnp.stack(
        [jnp.sum(jnp.where(inside & (spot == s), local + 1, 0), axis=1) - 1 for s in range(MOST)],
        axis=1,
    )
    chosen = chosen.reshape(n_exp, n_local * MOST)
    away = jnp.full_like(chosen, -1)
    columns = jnp.arange(2 * tok_dev, dtype=i32)
    wanted = jnp.stack(
        [chosen, jnp.where(chosen >= 0, chosen + tok_dev, away)], axis=1
    ).reshape(-1)
    pick = (wanted[:, None] == columns[None, :]).astype(BF)

    my_picks = lax.dynamic_slice(
        expert_picks, (exp_id * n_local, ctx_id * group_picks), (n_local, group_picks)
    )
    block_of = my_picks // tok_dev
    src_exp = block_of - ctx_id * n_exp
    slot_rank = jnp.arange(group_picks, dtype=i32)[None, :] - jnp.sum(
        (my_picks[:, None, :] < (block_of * tok_dev)[:, :, None]).astype(i32), axis=2
    )
    dist = lax.rem(exp_id - src_exp + n_exp, n_exp)
    spot_x = dist * 8 + jnp.arange(n_local, dtype=i32)[:, None] * MOST + slot_rank
    spots = jnp.stack([spot_x, spot_x + n_local * MOST]).reshape(-1)
    place = (spots[:, None] == jnp.arange(8 * n_exp, dtype=i32)[None, :]).astype(BF)

    mine, k_dealt, v_dealt = dispatch(moe_input, out_grad, pick, place, attn_keys, values)
    og_late, mine = lax.optimization_barrier((out_grad, mine))
    og_all = lax.all_gather(og_late, "exp", axis=0, tiled=True)
    slots = share(mine)
    q_late, slots = lax.optimization_barrier((queries, slots))
    q_all = lax.all_gather(q_late, "ctx", axis=0, tiled=True)
    slots = slots.reshape(2, n_local, n_ctx * group_picks, feat_width)
    slot_rows, slot_grads = slots[0], slots[1]

    gate_rows = lax.dynamic_slice_in_dim(gate_probs, exp_id * n_local, n_local, 0)
    pre_gate = jnp.einsum("kcd,kdf->kcf", slot_rows, w_gate, preferred_element_type=F32)
    pre_up = jnp.einsum("kcd,kdf->kcf", slot_rows, w_up, preferred_element_type=F32)
    gated_act, act_slope = activation(pre_gate)
    hidden_full = gated_act * pre_up
    hidden = hidden_full.astype(BF)
    down_back = jnp.einsum("kcd,kfd->kcf", slot_grads, w_down, preferred_element_type=F32)
    gate_part = jnp.sum(down_back * hidden_full, axis=2).reshape(n_local, n_ctx, 1, group_picks)
    gate_part = jnp.pad(gate_part, ((0, 0), (0, 0), (0, 0), (0, 128 - group_picks)))
    scaled = gate_rows[..., None] * down_back
    d_gate = (scaled * pre_up * act_slope).astype(BF)
    d_up = (scaled * gated_act).astype(BF)
    dx_part = (
        jnp.einsum("kcf,kdf->kcd", d_gate, w_gate, preferred_element_type=F32)
        + jnp.einsum("kcf,kdf->kcd", d_up, w_up, preferred_element_type=F32)
    ).astype(BF)
    dx_all, gate_sum = combine(
        dx_part.reshape(n_local, n_ctx, group_picks, feat_width), gate_part
    )
    d_gates = gate_sum[:, 0, :group_picks]
    dx_all = dx_all.reshape(-1, feat_width)

    weighted = (gate_rows[..., None] * slot_grads.astype(F32)).astype(BF)
    dw_down = jnp.einsum("kcf,kcd->kfd", hidden, weighted, preferred_element_type=F32).astype(BF)
    dw_gate = jnp.einsum("kcd,kcf->kdf", slot_rows, d_gate, preferred_element_type=F32).astype(BF)
    dw_up = jnp.einsum("kcd,kcf->kdf", slot_rows, d_up, preferred_element_type=F32).astype(BF)

    group_ids = lax.dynamic_slice_in_dim(
        expert_picks, ctx_id * group_picks, group_picks, 1
    ).reshape(-1) - ctx_id * tok_ctx
    spread_hot = (jnp.arange(tok_ctx, dtype=i32)[:, None] == group_ids[None, :]).astype(BF)
    own_hot = (
        (jnp.arange(tok_dev, dtype=i32) + exp_id * tok_dev)[:, None] == group_ids[None, :]
    ).astype(BF)
    d_resid = (
        out_grad.astype(F32) + jnp.dot(own_hot, dx_all, preferred_element_type=F32)
    ).astype(BF)

    d_out_base = contract_last(og_all, w_out)
    dx_out = contract_last(dx_all, w_out).astype(BF)
    d_out = (d_out_base + jnp.dot(spread_hot, dx_out, preferred_element_type=F32)).astype(BF)
    product = d_out.astype(F32) * attn_out.astype(F32)
    delta = lax.dot_general(
        jnp.ones((1, head_dim), F32), product, (((1,), (1,)), ((), ())),
        precision=lax.Precision.HIGHEST, preferred_element_type=F32,
    )
    out_taken = contract_first(spread_hot, attn_out).astype(BF)
    do_all, delta_all, dw_part = spread(d_out, delta, og_all, attn_out, out_taken, dx_all)
    grad_q, dw_out, grad_k, grad_v = attention(
        k_dealt, v_dealt, q_all, do_all, log_norm, delta_all, dw_part, key_scale
    )
    return (
        d_resid, dw_gate, dw_up, dw_down, d_gates, dw_out, grad_q, grad_k, grad_v,
    )


def solution(mesh):
    return jax.shard_map(
        body,
        mesh=mesh,
        in_specs=(
            P(("ctx", "exp"), None),
            P(("ctx", "exp"), None),
            P("exp", None, "ctx"),
            P("exp", None, "ctx"),
            P("exp", "ctx", None),
            P(),
            P(),
            P("ctx", "exp"),
            P("ctx", "exp"),
            P("ctx", "exp"),
            P("ctx", "exp"),
            P("exp", None),
            P("exp", None),
        ),
        out_specs=(
            P(("ctx", "exp"), None),
            P("exp", None, "ctx"),
            P("exp", None, "ctx"),
            P("exp", "ctx", None),
            P("exp", "ctx"),
            P("exp", "ctx"),
            P("ctx", "exp"),
            P("ctx", "exp"),
            P("ctx", "exp"),
        ),
        check_vma=False,
    )
```

```python
import functools
import math

import jax
import jax.numpy as jnp
from jax import lax
from jax.experimental import pallas as pl
from jax.experimental.pallas import tpu as pltpu
from jax.sharding import PartitionSpec as P

MOST = 2
MESH = pl.DeviceIdType.MESH
LOG2E = 1.4426950408889634
BF = jnp.bfloat16
F32 = jnp.float32
VLIM = 56 * 1024 * 1024
VM = pltpu.VMEM


def activation(pre_act):
    sigmoid_val = jax.nn.sigmoid(pre_act)
    return (pre_act * sigmoid_val, sigmoid_val * (1.0 + pre_act * (1.0 - sigmoid_val)))


def contract_first(left, right):
    return lax.dot_general(left, right, (((0,), (0,)), ((), ())), preferred_element_type=F32)


def contract_last(left, right):
    return lax.dot_general(left, right, (((1,), (1,)), ((), ())), preferred_element_type=F32)


class Place:
    def __init__(self, axis):
        self.axis = axis
        me = lax.axis_index(axis)
        if axis == "ctx":
            step, span = 1, 4
        else:
            step, span = 2, 8
        low = lax.rem(me, step)
        pos = lax.rem(me // step, 4)
        row = me // span
        other = 1 - row

        def at(r, p):
            return r * span + lax.rem(p + 4, 4) * step + low

        self.me = me
        self.up, self.down, self.far = at(row, pos + 1), at(row, pos - 1), at(row, pos + 2)
        self.mate = at(other, pos)
        self.mate_up, self.mate_down = at(other, pos + 1), at(other, pos - 1)
        self.mate_far = at(other, pos + 2)
        self.spots = tuple(lax.rem(pos + d, 4) for d in (0, 1, 3, 2))
        self.flip = 1 - 2 * low
        self.twin, self.mate_twin = me + self.flip, self.mate + self.flip


def greet(peers):
    barrier = pltpu.get_barrier_semaphore()
    for axis, dev in peers:
        pl.semaphore_signal(barrier, inc=1, device_id={axis: dev}, device_id_type=MESH)
    pl.semaphore_wait(barrier, len(peers))


class Lanes:
    def __init__(self, send_sems, recv_sems):
        self.send_sems, self.recv_sems, self.sent = send_sems, recv_sems, []

    def copy(self, k, src, dst, axis, dev):
        return pltpu.make_async_remote_copy(
            src_ref=src,
            dst_ref=dst,
            send_sem=self.send_sems.at[k],
            recv_sem=self.recv_sems.at[k],
            device_id={axis: dev},
            device_id_type=MESH,
        )

    def send(self, k, src, dst, axis, dev):
        one = self.copy(k, src, dst, axis, dev)
        one.start()
        self.sent.append(one)

    def recv(self, k, dst, axis, dev):
        self.copy(k, dst, dst, axis, dev).wait_recv()

    def finish(self):
        for one in self.sent:
            one.wait_send()


AG_LANES = 14


def gather_ring(pieces, place, lanes, base, arrived=None, work=(), ready=None):
    axis = place.axis
    n = len(pieces)
    work = list(work)

    def fill():
        if work:
            work.pop(0)()

    def send(k, block, half, dev):
        for i, piece in enumerate(pieces):
            lanes.send(base + k * n + i, piece(block, half), piece(block, half), axis, dev)

    def recv(k, block, half, dev):
        for i, piece in enumerate(pieces):
            lanes.recv(base + k * n + i, piece(block, half), axis, dev)
        if arrived is not None:
            arrived(k, block, half)

    p = place
    if ready is not None:
        ready(0)
    send(0, p.me, 0, p.mate)
    send(2, p.me, 0, p.up)
    send(5, p.me, 0, p.down)
    if ready is not None:
        ready(1)
    send(4, p.me, 1, p.down)
    send(1, p.me, 1, p.mate)
    send(3, p.me, 1, p.up)
    fill()
    recv(2, p.down, 0, p.down)
    send(6, p.down, 0, p.up)
    recv(4, p.up, 1, p.up)
    send(7, p.up, 1, p.down)
    fill()
    recv(0, p.mate, 0, p.mate)
    send(8, p.mate, 0, p.up)
    send(10, p.mate, 0, p.down)
    fill()
    recv(1, p.mate, 1, p.mate)
    send(11, p.mate, 1, p.down)
    send(9, p.mate, 1, p.up)
    fill()
    recv(8, p.mate_down, 0, p.down)
    send(12, p.mate_down, 0, p.up)
    recv(11, p.mate_up, 1, p.up)
    send(13, p.mate_up, 1, p.down)
    while work:
        fill()
    recv(3, p.down, 1, p.down)
    recv(5, p.up, 0, p.up)
    recv(6, p.far, 0, p.down)
    recv(7, p.far, 1, p.up)
    recv(10, p.mate_up, 0, p.up)
    recv(9, p.mate_down, 1, p.down)
    recv(12, p.mate_far, 0, p.down)
    recv(13, p.mate_far, 1, p.up)


RING_LANES = 6


class Ring:
    def __init__(self, piece, place, lanes, base):
        self.piece, self.place, self.lanes, self.base = piece, place, lanes, base
        self.pos = place.spots

    def send(self, k, pos, half, dev):
        one = self.piece(pos, half)
        self.lanes.send(self.base + k, one, one, self.place.axis, dev)

    def recv(self, k, pos, half, dev):
        self.lanes.recv(self.base + k, self.piece(pos, half), self.place.axis, dev)

    def begin(self, half):
        me, up, down, far = self.pos
        if half == 0:
            self.send(0, me, 0, self.place.up)
            self.send(2, me, 0, self.place.down)
        else:
            self.send(3, me, 1, self.place.down)
            self.send(1, me, 1, self.place.up)

    def forward(self):
        me, up, down, far = self.pos
        self.recv(0, down, 0, self.place.down)
        self.send(4, down, 0, self.place.up)
        self.recv(3, up, 1, self.place.up)
        self.send(5, up, 1, self.place.down)

    def end(self):
        me, up, down, far = self.pos
        self.recv(1, down, 1, self.place.down)
        self.recv(2, up, 0, self.place.up)
        self.recv(4, far, 0, self.place.down)
        self.recv(5, far, 1, self.place.up)


def add_into(dst, *srcs):
    total = srcs[0][...].astype(F32)
    for src in srcs[1:]:
        total = total + src[...].astype(F32)
    dst[...] = total.astype(dst.dtype)


def scatter_ring(parts, place, lanes, base, bufs, outs, started=None):
    axis = place.axis
    n = len(parts)
    p = place
    groups = (
        (p.mate_far, p.mate_up, p.mate_down, p.mate),
        (p.far, p.up, p.down, p.me),
    )

    def slot(i, s):
        return bufs[i](s)

    def send(k, i, src, s, dev):
        lanes.send(base + k * n + i, src, slot(i, s), axis, dev)

    def recv(k, i, s, dev):
        lanes.recv(base + k * n + i, slot(i, s), axis, dev)

    every = range(n)
    for g, (far, up, down, own) in enumerate(groups):
        for i in every:
            send(6 * g + 0, i, parts[i](far, 0), 6 * g + 0, p.up)
            send(6 * g + 1, i, parts[i](far, 1), 6 * g + 1, p.down)
        for i in every:
            send(6 * g + 3, i, parts[i](up, 1), 6 * g + 3, p.up)
            send(6 * g + 4, i, parts[i](down, 0), 6 * g + 4, p.down)
    if started is not None:
        started()
    for g, (far, up, down, own) in enumerate(groups):
        for i in every:
            recv(6 * g + 0, i, 6 * g + 0, p.down)
            add_into(slot(i, 6 * g + 0), slot(i, 6 * g + 0), parts[i](up, 0))
            send(6 * g + 2, i, slot(i, 6 * g + 0), 6 * g + 2, p.up)
            recv(6 * g + 1, i, 6 * g + 1, p.up)
            add_into(slot(i, 6 * g + 1), slot(i, 6 * g + 1), parts[i](down, 1))
            send(6 * g + 5, i, slot(i, 6 * g + 1), 6 * g + 5, p.down)
    far, up, down, own = groups[0]
    for half in (1, 0):
        for i in every:
            recv(2 + half, i, 2 + half, p.down)
            recv(4 + half, i, 4 + half, p.up)
            add_into(slot(i, 2 + half), slot(i, 2 + half), slot(i, 4 + half), parts[i](own, half))
            send(12 + half, i, slot(i, 2 + half), 12 + half, p.mate)
    for half in (1, 0):
        for i in every:
            recv(8 + half, i, 8 + half, p.down)
            recv(10 + half, i, 10 + half, p.up)
            recv(12 + half, i, 12 + half, p.mate)
            add_into(
                outs[i](half),
                slot(i, 8 + half),
                slot(i, 10 + half),
                slot(i, 12 + half),
                parts[i](p.me, half),
            )


def around(place):
    return [(place.axis, place.up), (place.axis, place.down), (place.axis, place.mate)]


def dispatch_kernel(
    n_ctx, mi_ref, og_ref, pick_ref, place_ref, key_ref, val_ref, q_ref,
    mine_ref, k_out, v_out, q_row, send, got, ss, rs,
):
    me = lax.axis_index("exp")
    ctx = Place("ctx")
    swap = n_ctx - 1 - ctx.me
    n_exp = send.shape[0]
    half = key_ref.shape[0] // 2
    greet(
        [("exp", lax.rem(me + d, n_exp)) for d in range(1, n_exp)]
        + [("ctx", dev) for dev in (ctx.up, ctx.down, swap)]
    )
    lanes = Lanes(ss, rs)
    rows = jnp.dot(pick_ref[:, :128], mi_ref[...], preferred_element_type=F32)
    rows = rows + jnp.dot(pick_ref[:, 128:], og_ref[...], preferred_element_type=F32)
    send[...] = rows.reshape(n_exp, 8, rows.shape[1]).astype(BF)
    for d in range(1, n_exp):
        to = lax.rem(me + d, n_exp)
        lanes.send(d - 1, send.at[to], got.at[d], "exp", to)
    upper = pl.ds(half, half)
    lanes.send(n_exp - 1, key_ref.at[upper], k_out, "ctx", swap)
    lanes.send(n_exp, val_ref.at[upper], v_out, "ctx", swap)
    q_row[lax.rem(ctx.me, 4)] = q_ref[...]
    ring = Ring(lambda pos, h: q_row.at[pos, pl.ds(h * half, half)], ctx, lanes, n_exp + 1)
    ring.begin(0)
    ring.begin(1)
    got[0] = send[me]
    ring.forward()
    for d in range(1, n_exp):
        lanes.recv(d - 1, got.at[d], "exp", lax.rem(me + n_exp - d, n_exp))
    flat = got[...].astype(F32).reshape(n_exp * 8, got.shape[2]).astype(BF)
    mine = jnp.dot(place_ref[...], flat, preferred_element_type=F32).astype(BF)
    mine_ref[...] = mine.reshape(2, 2, 16, got.shape[2])
    lanes.recv(n_exp - 1, k_out, "ctx", swap)
    lanes.recv(n_exp, v_out, "ctx", swap)
    ring.end()
    lanes.finish()


def dispatch(moe_input, out_grad, pick, place, keys, values, queries):
    n_exp, n_ctx = lax.axis_size("exp"), lax.axis_size("ctx")
    width = moe_input.shape[1]
    dealt = jax.ShapeDtypeStruct((keys.shape[0] // 2, keys.shape[1]), BF)
    n_sem = n_exp + 1 + RING_LANES
    return pl.pallas_call(
        functools.partial(dispatch_kernel, n_ctx),
        out_shape=(
            jax.ShapeDtypeStruct((2, 2, 16, width), BF),
            dealt,
            dealt,
            jax.ShapeDtypeStruct((4,) + queries.shape, BF),
        ),
        in_specs=[pl.BlockSpec(memory_space=VM)] * 7,
        out_specs=(pl.BlockSpec(memory_space=VM),) * 4,
        scratch_shapes=[
            VM((n_exp, 8, width), BF),
            VM((n_exp, 8, width), BF),
            pltpu.SemaphoreType.DMA((n_sem,)),
            pltpu.SemaphoreType.DMA((n_sem,)),
        ],
        compiler_params=pltpu.CompilerParams(
            collective_id=1, has_side_effects=True, vmem_limit_bytes=VLIM
        ),
        cost_estimate=pl.CostEstimate(flops=10**6, bytes_accessed=10**6, transcendentals=0),
    )(moe_input, out_grad, pick, place, keys, values, queries)


def member_of(e):
    return (e // 8) * 2 + lax.rem(e, 2)


def share_kernel(
    mine_ref, og_ref, w_ref, o_ref, out_ref, og_row, w_group, o_group, ss, rs
):
    ctx, exp = Place("ctx"), Place("exp")
    others = (exp.twin, exp.mate, exp.mate_twin)
    greet(around(ctx) + [("exp", d) for d in (exp.up, exp.down) + others])
    lanes = Lanes(ss, rs)
    for a in range(2):
        for k in range(2):
            out_ref[a, k, ctx.me] = mine_ref[a, k]
    half_rows = og_ref.shape[0] // 2
    ring = Ring(
        lambda pos, h: og_row.at[pos, pl.ds(h * half_rows, half_rows)], exp, lanes, AG_LANES
    )
    og_row[exp.spots[0]] = og_ref[...]
    me = member_of(exp.me)
    w_group[me] = w_ref[...]
    o_group[me] = o_ref[exp.me // 8, :, lax.rem(exp.me, 2)]
    base = AG_LANES + RING_LANES

    def more():
        ring.begin(0)
        ring.begin(1)
        lanes.send(base, w_ref, w_group.at[me], "exp", exp.mate)
        lanes.send(base + 1, w_ref, w_group.at[me], "exp", exp.twin)
        for j, dev in enumerate(others):
            lanes.send(
                base + 3 + j, o_ref.at[dev // 8, :, lax.rem(dev, 2)], o_group.at[me], "exp", dev
            )

    def pass_on():
        block = w_group.at[member_of(exp.mate)]
        lanes.recv(base, block, "exp", exp.mate)
        lanes.send(base + 2, block, block, "exp", exp.twin)

    nothing = lambda: None
    work = [more, ring.forward, nothing, nothing, pass_on]
    gather_ring([lambda block, half: out_ref.at[half, :, block]], ctx, lanes, 0, work=work)
    ring.end()
    lanes.recv(base + 1, w_group.at[member_of(exp.twin)], "exp", exp.twin)
    lanes.recv(base + 2, w_group.at[member_of(exp.mate_twin)], "exp", exp.twin)
    for j, dev in enumerate(others):
        lanes.recv(base + 3 + j, o_group.at[member_of(dev)], "exp", dev)
    lanes.finish()


def share(mine, out_grad, w_out, attn_out):
    n_ctx = lax.axis_size("ctx")
    rows, head = out_grad.shape[0], attn_out.shape[1]
    n_sem = AG_LANES + RING_LANES + 6
    vmem = pl.BlockSpec(memory_space=VM)
    return pl.pallas_call(
        share_kernel,
        out_shape=(
            jax.ShapeDtypeStruct(mine.shape[:2] + (n_ctx,) + mine.shape[2:], BF),
            jax.ShapeDtypeStruct((4,) + out_grad.shape, BF),
            jax.ShapeDtypeStruct((4,) + w_out.shape, BF),
            jax.ShapeDtypeStruct((4, 4, rows, head), BF),
        ),
        in_specs=[vmem] * 4,
        out_specs=(vmem,) * 4,
        scratch_shapes=[
            pltpu.SemaphoreType.DMA((n_sem,)),
            pltpu.SemaphoreType.DMA((n_sem,)),
        ],
        compiler_params=pltpu.CompilerParams(
            collective_id=5, has_side_effects=True, vmem_limit_bytes=VLIM
        ),
        cost_estimate=pl.CostEstimate(flops=10**6, bytes_accessed=10**6, transcendentals=0),
    )(mine, out_grad, w_out, attn_out.reshape(2, 4, 2, rows, head))


def combine_kernel(
    part_ref, gate_ref, q_ref, og_row, w_group, out_ref, gate_out, q_mate, base_out,
    buf, gate_buf, base_send, ss, rs,
):
    ctx, exp = Place("ctx"), Place("exp")
    twin = exp.twin
    greet(around(ctx) + around(exp) + [("exp", twin), ("exp", exp.mate_twin)])
    lanes = Lanes(ss, rs)
    rows = q_ref.shape[0] // 2
    pos = lax.rem(ctx.me, 4)
    q_base = 3 * AG_LANES + 16
    d_base = q_base + 2 + RING_LANES
    others = (exp.twin, exp.mate, exp.mate_twin)

    def q_piece(at, half):
        return q_mate.at[at, pl.ds(half * rows, rows)]

    def q_start():
        for half in range(2):
            src = q_ref.at[pl.ds(half * rows, rows)]
            lanes.send(q_base + half, src, q_piece(pos, half), "ctx", ctx.mate)
        rows_og = og_row[...].reshape(-1, og_row.shape[2])
        y_lo, core = exp.me // 8, lax.rem(exp.me, 2)
        for j, dev in enumerate(others + (exp.me,)):
            value = contract_last(rows_og, w_group[member_of(dev)]).astype(BF)
            value = value.reshape(base_send.shape[1:])
            if j < 3:
                base_send[j] = value
                lanes.send(
                    d_base + j, base_send.at[j], base_out.at[y_lo, :, core], "exp", dev
                )
            else:
                base_out[y_lo, :, core] = value

    ring = Ring(q_piece, ctx, lanes, q_base + 2)

    def q_ring(half):
        lanes.recv(q_base + half, q_piece(pos, half), "ctx", ctx.mate)
        ring.begin(half)

    scatter_ring(
        [
            lambda block, half: part_ref.at[half, block],
            lambda block, half: gate_ref.at[half, block],
        ],
        ctx,
        lanes,
        0,
        [lambda s: buf.at[s], lambda s: gate_buf.at[s]],
        [lambda half: out_ref.at[exp.me, half], lambda half: gate_out.at[half]],
        q_start,
    )

    def piece(block, half):
        return out_ref.at[block, half]

    base = 2 * AG_LANES
    over = 3 * AG_LANES
    flip = exp.flip
    for half in range(2):
        lanes.send(over + 14 + half, piece(exp.me, half), piece(exp.me, half), "exp", twin)

    def arrived(k, block, half):
        lanes.send(over + k, piece(block, half), piece(block, half), "exp", twin)

    work = [lambda: q_ring(0), lambda: q_ring(1), ring.forward]
    gather_ring([piece], exp, lanes, base, arrived, work)
    ring.end()
    srcs = {
        0: (exp.mate, 0), 1: (exp.mate, 1), 2: (exp.down, 0), 3: (exp.down, 1),
        4: (exp.up, 1), 5: (exp.up, 0), 6: (exp.far, 0), 7: (exp.far, 1),
        8: (exp.mate_down, 0), 9: (exp.mate_down, 1), 10: (exp.mate_up, 0),
        11: (exp.mate_up, 1), 12: (exp.mate_far, 0), 13: (exp.mate_far, 1),
        14: (exp.me, 0), 15: (exp.me, 1),
    }
    for k, (block, half) in srcs.items():
        lanes.recv(over + k, piece(block + flip, half), "exp", twin)
    for j, dev in enumerate(others):
        lanes.recv(d_base + j, base_out.at[dev // 8, :, lax.rem(dev, 2)], "exp", dev)
    lanes.finish()


def combine(part, gate_part, queries, og_row, w_group):
    n_exp = lax.axis_size("exp")
    rows, width = part.shape[2:]
    n_sem = 3 * AG_LANES + 16 + 2 + RING_LANES + 3
    tok, head = og_row.shape[1], queries.shape[1]
    return pl.pallas_call(
        combine_kernel,
        out_shape=(
            jax.ShapeDtypeStruct((n_exp, 2, rows, width), BF),
            jax.ShapeDtypeStruct((2,) + gate_part.shape[2:], F32),
            jax.ShapeDtypeStruct((4,) + queries.shape, BF),
            jax.ShapeDtypeStruct((2, 4, 2, tok, head), BF),
        ),
        in_specs=[pl.BlockSpec(memory_space=VM)] * 5,
        out_specs=(pl.BlockSpec(memory_space=VM),) * 4,
        scratch_shapes=[
            VM((14, rows, width), BF),
            VM((14,) + gate_part.shape[2:], F32),
            VM((3, 4, tok, head), BF),
            pltpu.SemaphoreType.DMA((n_sem,)),
            pltpu.SemaphoreType.DMA((n_sem,)),
        ],
        compiler_params=pltpu.CompilerParams(
            collective_id=2, has_side_effects=True, vmem_limit_bytes=VLIM
        ),
        cost_estimate=pl.CostEstimate(flops=10**6, bytes_accessed=10**6, transcendentals=0),
    )(part, gate_part, queries, og_row, w_group)


def spread_kernel(
    base_ref, w_ref, o_ref, ids_ref, dx_ref, og_row, o_group,
    do_all, delta_all, dw_ref, dw_acc, dx_out, taken, dw_buf, ss, rs,
):
    ctx, exp = Place("ctx"), Place("exp")
    greet(around(ctx) + [("exp", exp.twin), ("exp", exp.mate)])
    lanes = Lanes(ss, rs)
    chunk = 256
    rows = base_ref.shape[0] // 2
    n_out, _, part = dw_ref.shape
    taken[...] = jnp.zeros_like(taken)
    dx_out[...] = contract_last(dx_ref[...], w_ref[...]).astype(BF)
    ones = jnp.ones((8, o_ref.shape[1]), BF)

    def project(j, carry):
        here = pl.ds(pl.multiple_of(j * chunk, chunk), chunk)
        o = o_ref[here, :]
        at = lax.broadcasted_iota(jnp.int32, (chunk, ids_ref.shape[1]), 0) + j * chunk
        pick = jnp.where(at == ids_ref[...], 1.0, 0.0).astype(BF)
        value = base_ref[here, :].astype(F32)
        value = value + jnp.dot(pick, dx_out[...], preferred_element_type=F32)
        value = value.astype(BF)
        do_all[ctx.me, here, :] = value
        taken[...] += contract_first(pick, o)
        rest = value.astype(F32) * o.astype(F32)
        total = jnp.zeros((8, chunk), F32)
        for _ in range(3):
            term = rest.astype(BF)
            total = total + contract_last(ones, term)
            rest = rest - term.astype(F32)
        delta_all[ctx.me, :, here] = total[0:1]
        return carry

    def ready(half):
        first = half * (rows // chunk)
        lax.fori_loop(first, first + rows // chunk, project, 0)

    base = 2 * AG_LANES
    n_rows = og_row.shape[0] * og_row.shape[1]

    def term(dev, cols):
        o = o_group[member_of(dev)].reshape(n_rows, o_ref.shape[1])
        return contract_first(o, og_row[:, :, cols].reshape(n_rows, part))

    def fill(slot, dev):
        for b in range(n_out):
            cols = pl.ds(b * part, part)
            dw_buf[slot, :, cols] = term(dev, cols).astype(BF)

    def first():
        fill(0, exp.mate_twin)
        lanes.send(base, dw_buf.at[0], dw_buf.at[3], "exp", exp.twin)
        fill(1, exp.mate)

    def second():
        lanes.recv(base, dw_buf.at[3], "exp", exp.twin)
        add_into(dw_buf.at[1], dw_buf.at[1], dw_buf.at[3])
        lanes.send(base + 1, dw_buf.at[1], dw_buf.at[4], "exp", exp.mate)

    def third():
        fill(2, exp.twin)
        lanes.send(base + 2, dw_buf.at[2], dw_buf.at[5], "exp", exp.twin)

    def fourth():
        rows_taken = taken[...].astype(BF)
        for b in range(n_out):
            cols = pl.ds(b * part, part)
            dw_acc[:, cols] = term(exp.me, cols) + contract_first(rows_taken, dx_ref[:, cols])

    def close():
        lanes.recv(base + 2, dw_buf.at[5], "exp", exp.twin)
        lanes.recv(base + 1, dw_buf.at[4], "exp", exp.mate)
        for b in range(n_out):
            cols = pl.ds(b * part, part)
            total = dw_acc[:, cols]
            for slot in (4, 5):
                total = total + dw_buf[slot, :, cols].astype(F32)
            dw_ref[b] = total.astype(BF)

    def piece_do(block, half):
        return do_all.at[block, pl.ds(half * rows, rows)]

    def piece_delta(block, half):
        return delta_all.at[block, :, pl.ds(half * rows, rows)]

    gather_ring(
        [piece_do, piece_delta], ctx, lanes, 0,
        work=[first, second, third, fourth], ready=ready,
    )
    close()
    lanes.finish()


def spread(d_base, w_out, attn_out, ids, dx_all, og_row, o_group):
    n_ctx = lax.axis_size("ctx")
    n_sem = 2 * AG_LANES + 3
    tokens, head = d_base.shape
    width = w_out.shape[1]
    vmem = pl.BlockSpec(memory_space=VM)
    return pl.pallas_call(
        spread_kernel,
        out_shape=(
            jax.ShapeDtypeStruct((n_ctx, tokens, head), BF),
            jax.ShapeDtypeStruct((n_ctx, 1, tokens), F32),
            jax.ShapeDtypeStruct((n_ctx, head, width // n_ctx), BF),
        ),
        in_specs=[vmem] * 7,
        out_specs=(vmem,) * 3,
        scratch_shapes=[
            VM((head, width), F32),
            VM((dx_all.shape[0], head), BF),
            VM((dx_all.shape[0], head), F32),
            VM((6, head, width), BF),
            pltpu.SemaphoreType.DMA((n_sem,)),
            pltpu.SemaphoreType.DMA((n_sem,)),
        ],
        compiler_params=pltpu.CompilerParams(
            collective_id=3, has_side_effects=True, vmem_limit_bytes=VLIM
        ),
        cost_estimate=pl.CostEstimate(flops=10**6, bytes_accessed=10**6, transcendentals=0),
    )(d_base, w_out, attn_out, ids, dx_all, og_row, o_group)


CHUNK = 1024
TILE = 512


def attention_kernel(
    scale, n_ctx, k_own, k_far, v_own, v_far, q_row, q_mate, do_ref, lse_ref, delta_ref, dw_ref,
    grads_out, gw_out,
    q_ref, k_ref, v_ref, dq_part, dk_acc, dv_acc, dq_acc, back, dq_buf, dw_buf, ss, rs, load_sems,
):
    p = Place("ctx")
    c = p.me
    swap = n_ctx - 1 - c
    n_ring = q_row.shape[0]
    low = c // n_ring
    loads = [
        pltpu.make_async_copy(src, q_ref.at[pl.ds(at * n_ring, n_ring)], load_sems.at[j])
        for j, (src, at) in enumerate(((q_row, low), (q_mate, 1 - low)))
    ]
    for one in loads:
        one.start()
    greet(around(p) + [("ctx", swap)])
    lanes = Lanes(ss, rs)
    n_chunk = 2 * n_ctx
    ids = (2 * c, n_chunk - 1 - 2 * c)
    k_ref[0], k_ref[1] = k_own[:CHUNK, :], k_far[...]
    v_ref[0], v_ref[1] = v_own[:CHUNK, :], v_far[...]
    dk_acc[...] = jnp.zeros_like(dk_acc)
    dv_acc[...] = jnp.zeros_like(dv_acc)

    def tile(part, group, half, row, key, masked):
        at = half * CHUNK + row
        spot = group * 2 * CHUNK + at
        q = q_ref[group, pl.ds(at, TILE), :]
        do = do_ref[group, pl.ds(at, TILE), :]
        lse = lse_ref[:, pl.ds(spot, TILE)] * LOG2E
        delta = delta_ref[group, :, pl.ds(at, TILE)]
        k = k_ref[part, pl.ds(key, TILE), :]
        v = v_ref[part, pl.ds(key, TILE), :]
        s = contract_last(k, q) * (scale * LOG2E) - lse
        if masked:
            rk = lax.broadcasted_iota(jnp.int32, s.shape, 0)
            cq = lax.broadcasted_iota(jnp.int32, s.shape, 1)
            s = jnp.where(rk <= cq, s, -1e30)
        probs = jnp.exp2(s)
        dp = contract_last(v, do)
        ds = (probs * (dp - delta)).astype(BF)
        dv_acc[part, pl.ds(key, TILE), :] += jnp.dot(
            probs.astype(BF), do, preferred_element_type=F32
        )
        dk_acc[part, pl.ds(key, TILE), :] += jnp.dot(ds, q, preferred_element_type=F32)
        dq_acc[pl.ds(row, TILE), :] += contract_first(ds, k)

    w_rows = dw_ref.shape[1] // 2
    parts = (
        lambda block, h: dq_part.at[block, pl.ds(h * CHUNK, CHUNK)],
        lambda block, h: dw_ref.at[block, pl.ds(h * w_rows, w_rows)],
    )
    slots = (lambda s: dq_buf.at[s], lambda s: dw_buf.at[s])
    n = len(parts)

    def send(k, src, dev):
        for i in range(n):
            lanes.copy(k * n + i, src[i], slots[i](k), "ctx", dev).start()

    def recv(k, dev):
        for i in range(n):
            lanes.copy(k * n + i, slots[i](k), slots[i](k), "ctx", dev).wait_recv()

    def terms(block, h):
        return [parts[i](block, h) for i in range(n)]

    def plain(k, block, h, dev):
        send(k, terms(block, h), dev)

    def summed(k, into, others, block, h, dev):
        for i in range(n):
            add_into(
                slots[i](into), slots[i](into), *[slots[i](o) for o in others], parts[i](block, h)
            )
        send(k, [slots[i](into) for i in range(n)], dev)

    def near_up():
        recv(0, p.down)
        summed(2, 0, (), p.mate_up, 0, p.up)

    def near_down():
        recv(1, p.up)
        summed(5, 1, (), p.mate_down, 1, p.down)

    def over(h):
        recv(2 + h, p.down)
        recv(4 + h, p.up)
        summed(12 + h, 2 + h, (4 + h,), p.mate, h, p.mate)

    def own_up():
        recv(6, p.down)
        summed(8, 6, (), p.up, 0, p.up)

    def own_down():
        recv(7, p.up)
        summed(11, 7, (), p.down, 1, p.down)

    plan = [
        (0, 0, lambda: plain(0, p.mate_far, 0, p.up)),
        (1, 1, lambda: plain(1, p.mate_far, 1, p.down)),
        (3, 3, lambda: plain(3, p.mate_up, 1, p.up)),
        (4, 4, lambda: plain(4, p.mate_down, 0, p.down)),
        (3, 9, near_up),
        (5, 9, near_down),
        (7, 11, lambda: over(0)),
        (8, 12, lambda: over(1)),
        (8, 8, lambda: plain(6, p.far, 0, p.up)),
        (9, 9, lambda: plain(7, p.far, 1, p.down)),
        (11, 11, lambda: plain(9, p.up, 1, p.up)),
        (12, 12, lambda: plain(10, p.down, 0, p.down)),
        (13, 13, own_up),
        (13, 13, own_down),
    ]
    order = [p.mate_far, p.mate_up, p.mate_down, p.mate, p.far, p.up, p.down, p.me]

    def step(t, carry):
        place = t // 2
        half = lax.rem(t, 2)
        group = order[0]
        for j in range(1, len(order)):
            group = jnp.where(place == j, order[j], group)
        chunk = 2 * group + half
        dq_acc[...] = jnp.zeros_like(dq_acc)
        for part in range(2):

            @pl.when(chunk > ids[part])
            def _(part=part):
                for row in range(0, CHUNK, TILE):
                    for key in range(0, CHUNK, TILE):
                        tile(part, group, half, row, key, False)

            @pl.when(chunk == ids[part])
            def _(part=part):
                for row in range(0, CHUNK, TILE):
                    for key in range(0, row + 1, TILE):
                        tile(part, group, half, row, key, key == row)

        dq_part[group, pl.ds(half * CHUNK, CHUNK), :] = (dq_acc[...] * scale).astype(BF)
        for early, late, act in plan:
            pl.when(t == jnp.where(low == 0, early, late))(act)

        return carry

    for one in loads:
        one.wait()
    lax.fori_loop(0, n_chunk, step, 0)

    base = n * AG_LANES
    for j, (acc, factor) in enumerate(((dk_acc, scale), (dv_acc, 1.0))):
        back[j] = (acc[1] * factor).astype(BF)
        lanes.send(base + j, back.at[j], grads_out.at[1 + j, pl.ds(CHUNK, CHUNK)], "ctx", swap)
        grads_out[1 + j, :CHUNK, :] = (acc[0] * factor).astype(BF)
    finals = (
        lambda h: grads_out.at[0, pl.ds(h * CHUNK, CHUNK)],
        lambda h: gw_out.at[pl.ds(h * w_rows, w_rows)],
    )
    for h in range(2):
        recv(8 + h, p.down)
        recv(10 + h, p.up)
        recv(12 + h, p.mate)
        for i in range(n):
            add_into(
                finals[i](h), slots[i](8 + h), slots[i](10 + h), slots[i](12 + h),
                parts[i](p.me, h),
            )
    for k in range(AG_LANES):
        for i in range(n):
            lanes.copy(k * n + i, slots[i](k), slots[i](k), "ctx", p.up).wait_send()
    for j in range(2):
        lanes.recv(base + j, grads_out.at[1 + j, pl.ds(CHUNK, CHUNK)], "ctx", swap)
    lanes.finish()


def attention(keys, k_far, values, v_far, q_row, q_mate, do_all, lse, delta_all, dw_part, scale):
    n_ctx, tok_ctx, head = do_all.shape
    vmem = pl.BlockSpec(memory_space=VM)
    anyw = pl.BlockSpec(memory_space=pl.ANY)
    n_sem = 2 * AG_LANES + 2
    return pl.pallas_call(
        functools.partial(attention_kernel, scale, n_ctx),
        out_shape=(
            jax.ShapeDtypeStruct((3, tok_ctx, head), BF),
            jax.ShapeDtypeStruct(dw_part.shape[1:], BF),
        ),
        in_specs=[vmem] * 4 + [anyw] * 2 + [vmem] * 4,
        out_specs=(vmem,) * 2,
        scratch_shapes=[
            VM(do_all.shape, BF),
            VM((2, CHUNK, head), BF),
            VM((2, CHUNK, head), BF),
            VM(do_all.shape, BF),
            VM((2, CHUNK, head), F32),
            VM((2, CHUNK, head), F32),
            VM((CHUNK, head), F32),
            VM((2, CHUNK, head), BF),
            VM((AG_LANES, CHUNK, head), BF),
            VM((AG_LANES, dw_part.shape[1] // 2, dw_part.shape[2]), BF),
            pltpu.SemaphoreType.DMA((n_sem,)),
            pltpu.SemaphoreType.DMA((n_sem,)),
            pltpu.SemaphoreType.DMA((2,)),
        ],
        compiler_params=pltpu.CompilerParams(
            collective_id=4, has_side_effects=True, vmem_limit_bytes=VLIM
        ),
        cost_estimate=pl.CostEstimate(
            flops=40 * 10**9, bytes_accessed=20 * 10**6, transcendentals=17 * 10**6
        ),
    )(keys, k_far, values, v_far, q_row, q_mate, do_all, lse, delta_all, dw_part)


def body(
    moe_input,
    out_grad,
    w_gate,
    w_up,
    w_down,
    expert_picks,
    gate_probs,
    queries,
    attn_keys,
    values,
    attn_out,
    log_norm,
    w_out,
):
    n_ctx = lax.axis_size("ctx")
    n_exp = lax.axis_size("exp")
    ctx_id = lax.axis_index("ctx")
    exp_id = lax.axis_index("exp")
    tok_dev, feat_width = moe_input.shape
    n_local = w_gate.shape[0]
    group_picks = expert_picks.shape[1] // n_ctx
    tok_ctx, head_dim = queries.shape
    key_scale = head_dim ** (-0.5)
    i32 = jnp.int32

    base_row = (ctx_id * n_exp + exp_id) * tok_dev
    below = jnp.sum((expert_picks < base_row).astype(i32), axis=1, keepdims=True)
    inside = (expert_picks >= base_row) & (expert_picks < base_row + tok_dev)
    spot = jnp.arange(expert_picks.shape[1], dtype=i32)[None, :] - below
    local = expert_picks - base_row
    chosen = jnp.stack(
        [jnp.sum(jnp.where(inside & (spot == s), local + 1, 0), axis=1) - 1 for s in range(MOST)],
        axis=1,
    )
    chosen = chosen.reshape(n_exp, n_local * MOST)
    away = jnp.full_like(chosen, -1)
    columns = jnp.arange(2 * tok_dev, dtype=i32)
    wanted = jnp.stack(
        [chosen, jnp.where(chosen >= 0, chosen + tok_dev, away)], axis=1
    ).reshape(-1)
    pick = (wanted[:, None] == columns[None, :]).astype(BF)

    my_picks = lax.dynamic_slice(
        expert_picks, (exp_id * n_local, ctx_id * group_picks), (n_local, group_picks)
    )
    block_of = my_picks // tok_dev
    src_exp = block_of - ctx_id * n_exp
    slot_rank = jnp.arange(group_picks, dtype=i32)[None, :] - jnp.sum(
        (my_picks[:, None, :] < (block_of * tok_dev)[:, :, None]).astype(i32), axis=2
    )
    dist = lax.rem(exp_id - src_exp + n_exp, n_exp)
    spot_x = dist * 8 + jnp.arange(n_local, dtype=i32)[:, None] * MOST + slot_rank
    spots = jnp.stack([spot_x, spot_x + n_local * MOST]).reshape(-1)
    place = (spots[:, None] == jnp.arange(8 * n_exp, dtype=i32)[None, :]).astype(BF)

    mine, k_far, v_far, q_row = dispatch(
        moe_input, out_grad, pick, place, attn_keys, values, queries
    )
    slots, og_row, w_group, o_group = share(mine, out_grad, w_out, attn_out)
    slots = slots.reshape(2, n_local, n_ctx * group_picks, feat_width)
    slot_rows, slot_grads = slots[0], slots[1]

    gate_rows = lax.dynamic_slice_in_dim(gate_probs, exp_id * n_local, n_local, 0)
    pre_gate = jnp.einsum("kcd,kdf->kcf", slot_rows, w_gate, preferred_element_type=F32)
    pre_up = jnp.einsum("kcd,kdf->kcf", slot_rows, w_up, preferred_element_type=F32)
    gated_act, act_slope = activation(pre_gate)
    hidden_full = gated_act * pre_up
    hidden = hidden_full.astype(BF)
    down_back = jnp.einsum("kcd,kfd->kcf", slot_grads, w_down, preferred_element_type=F32)
    gate_part = jnp.sum(down_back * hidden_full, axis=2).reshape(n_local, n_ctx, 1, group_picks)
    gate_part = jnp.pad(gate_part, ((0, 0), (0, 0), (0, 0), (0, 128 - group_picks)))
    scaled = gate_rows[..., None] * down_back
    d_gate = (scaled * pre_up * act_slope).astype(BF)
    d_up = (scaled * gated_act).astype(BF)
    dx_part = (
        jnp.einsum("kcf,kdf->kcd", d_gate, w_gate, preferred_element_type=F32)
        + jnp.einsum("kcf,kdf->kcd", d_up, w_up, preferred_element_type=F32)
    ).astype(BF)
    dx_all, gate_sum, q_mate, d_base = combine(
        dx_part.reshape(n_local, n_ctx, group_picks, feat_width),
        gate_part,
        queries,
        og_row,
        w_group,
    )
    d_gates = gate_sum[:, 0, :group_picks]
    dx_all = dx_all.reshape(-1, feat_width)

    weighted = (gate_rows[..., None] * slot_grads.astype(F32)).astype(BF)
    dw_down = jnp.einsum("kcf,kcd->kfd", hidden, weighted, preferred_element_type=F32).astype(BF)
    dw_gate = jnp.einsum("kcd,kcf->kdf", slot_rows, d_gate, preferred_element_type=F32).astype(BF)
    dw_up = jnp.einsum("kcd,kcf->kdf", slot_rows, d_up, preferred_element_type=F32).astype(BF)

    group_ids = lax.dynamic_slice_in_dim(
        expert_picks, ctx_id * group_picks, group_picks, 1
    ).reshape(-1) - ctx_id * tok_ctx
    own_hot = (
        (jnp.arange(tok_dev, dtype=i32) + exp_id * tok_dev)[:, None] == group_ids[None, :]
    ).astype(BF)
    d_resid = (
        out_grad.astype(F32) + jnp.dot(own_hot, dx_all, preferred_element_type=F32)
    ).astype(BF)

    do_all, delta_all, dw_part = spread(
        d_base.reshape(tok_ctx, head_dim), w_out, attn_out, group_ids[None, :], dx_all,
        og_row, o_group,
    )
    grads, dw_out = attention(
        attn_keys, k_far, values, v_far, q_row, q_mate, do_all, log_norm, delta_all, dw_part,
        key_scale,
    )
    return (
        d_resid, dw_gate, dw_up, dw_down, d_gates, dw_out, grads[0], grads[1], grads[2],
    )


def solution(mesh):
    return jax.shard_map(
        body,
        mesh=mesh,
        in_specs=(
            P(("ctx", "exp"), None),
            P(("ctx", "exp"), None),
            P("exp", None, "ctx"),
            P("exp", None, "ctx"),
            P("exp", "ctx", None),
            P(),
            P(),
            P("ctx", "exp"),
            P("ctx", "exp"),
            P("ctx", "exp"),
            P("ctx", "exp"),
            P("exp", None),
            P("exp", None),
        ),
        out_specs=(
            P(("ctx", "exp"), None),
            P("exp", None, "ctx"),
            P("exp", None, "ctx"),
            P("exp", "ctx", None),
            P("exp", "ctx"),
            P("exp", "ctx"),
            P("ctx", "exp"),
            P("ctx", "exp"),
            P("ctx", "exp"),
        ),
        check_vma=False,
    )
```

```python
import functools
import math

import jax
import jax.numpy as jnp
from jax import lax
from jax.experimental import pallas as pl
from jax.experimental.pallas import tpu as pltpu
from jax.sharding import PartitionSpec as P

MOST = 2
MESH = pl.DeviceIdType.MESH
LOG2E = 1.4426950408889634
BF = jnp.bfloat16
F32 = jnp.float32
VLIM = 56 * 1024 * 1024
VM = pltpu.VMEM
VMEM_SPEC = pl.BlockSpec(memory_space=pltpu.VMEM)
ANY_SPEC = pl.BlockSpec(memory_space=pl.ANY)


def activation(pre_act):
    sigmoid_val = jax.nn.sigmoid(pre_act)
    return (pre_act * sigmoid_val, sigmoid_val * (1.0 + pre_act * (1.0 - sigmoid_val)))


def contract_first(left, right):
    return lax.dot_general(left, right, (((0,), (0,)), ((), ())), preferred_element_type=F32)


def contract_last(left, right):
    return lax.dot_general(left, right, (((1,), (1,)), ((), ())), preferred_element_type=F32)


class Place:
    def __init__(self, axis):
        self.axis = axis
        me = lax.axis_index(axis)
        if axis == "ctx":
            step, span = 1, 4
        else:
            step, span = 2, 8
        low = lax.rem(me, step)
        pos = lax.rem(me // step, 4)
        row = me // span
        other = 1 - row

        def at(r, p):
            return r * span + lax.rem(p + 4, 4) * step + low

        self.me = me
        self.up, self.down, self.far = at(row, pos + 1), at(row, pos - 1), at(row, pos + 2)
        self.mate = at(other, pos)
        self.mate_up, self.mate_down = at(other, pos + 1), at(other, pos - 1)
        self.mate_far = at(other, pos + 2)
        self.spots = tuple(lax.rem(pos + d, 4) for d in (0, 1, 3, 2))
        self.flip = 1 - 2 * low
        self.twin, self.mate_twin = me + self.flip, self.mate + self.flip


def greet(peers):
    barrier = pltpu.get_barrier_semaphore()
    for axis, dev in peers:
        pl.semaphore_signal(barrier, inc=1, device_id={axis: dev}, device_id_type=MESH)
    pl.semaphore_wait(barrier, len(peers))


class Lanes:
    def __init__(self, send_sems, recv_sems):
        self.send_sems, self.recv_sems, self.sent, self.local = send_sems, recv_sems, [], []

    def copy(self, k, src, dst, axis, dev):
        return pltpu.make_async_remote_copy(
            src_ref=src,
            dst_ref=dst,
            send_sem=self.send_sems.at[k],
            recv_sem=self.recv_sems.at[k],
            device_id={axis: dev},
            device_id_type=MESH,
        )

    def send(self, k, src, dst, axis, dev):
        one = self.copy(k, src, dst, axis, dev)
        one.start()
        self.sent.append(one)

    def recv(self, k, dst, axis, dev):
        self.copy(k, dst, dst, axis, dev).wait_recv()

    def finish(self):
        for one in self.sent:
            one.wait_send()
        for one in self.local:
            one.wait()

    def keep(self, sem, src, dst):
        one = pltpu.make_async_copy(src, dst, sem)
        one.start()
        self.local.append(one)


AG_LANES = 14


def gather_ring(pieces, place, lanes, base, arrived=None, work=(), ready=None, own=None):
    axis = place.axis
    n = len(pieces)
    work = list(work)

    def fill():
        if work:
            work.pop(0)()

    def send(k, block, half, dev):
        for i, piece in enumerate(pieces):
            src = piece(block, half) if own is None or k > 5 else own[i](half)
            lanes.send(base + k * n + i, src, piece(block, half), axis, dev)

    def recv(k, block, half, dev):
        for i, piece in enumerate(pieces):
            lanes.recv(base + k * n + i, piece(block, half), axis, dev)
        if arrived is not None:
            arrived(k, block, half)

    p = place
    if ready is not None:
        ready(0)
    send(0, p.me, 0, p.mate)
    send(2, p.me, 0, p.up)
    send(5, p.me, 0, p.down)
    if ready is not None:
        ready(1)
    send(4, p.me, 1, p.down)
    send(1, p.me, 1, p.mate)
    send(3, p.me, 1, p.up)
    fill()
    recv(2, p.down, 0, p.down)
    send(6, p.down, 0, p.up)
    recv(4, p.up, 1, p.up)
    send(7, p.up, 1, p.down)
    fill()
    recv(0, p.mate, 0, p.mate)
    send(8, p.mate, 0, p.up)
    send(10, p.mate, 0, p.down)
    fill()
    recv(1, p.mate, 1, p.mate)
    send(11, p.mate, 1, p.down)
    send(9, p.mate, 1, p.up)
    fill()
    recv(8, p.mate_down, 0, p.down)
    send(12, p.mate_down, 0, p.up)
    recv(11, p.mate_up, 1, p.up)
    send(13, p.mate_up, 1, p.down)
    while work:
        fill()
    recv(3, p.down, 1, p.down)
    recv(5, p.up, 0, p.up)
    recv(6, p.far, 0, p.down)
    recv(7, p.far, 1, p.up)
    recv(10, p.mate_up, 0, p.up)
    recv(9, p.mate_down, 1, p.down)
    recv(12, p.mate_far, 0, p.down)
    recv(13, p.mate_far, 1, p.up)


RING_LANES = 6


class Ring:
    def __init__(self, piece, place, lanes, base, own=None):
        self.piece, self.place, self.lanes, self.base = piece, place, lanes, base
        self.own = own
        self.pos = place.spots

    def send(self, k, pos, half, dev):
        one = self.piece(pos, half)
        src = one if self.own is None or k > 3 else self.own(half)
        self.lanes.send(self.base + k, src, one, self.place.axis, dev)

    def recv(self, k, pos, half, dev):
        self.lanes.recv(self.base + k, self.piece(pos, half), self.place.axis, dev)

    def begin(self, half):
        me, up, down, far = self.pos
        if half == 0:
            self.send(0, me, 0, self.place.up)
            self.send(2, me, 0, self.place.down)
        else:
            self.send(3, me, 1, self.place.down)
            self.send(1, me, 1, self.place.up)

    def forward(self):
        me, up, down, far = self.pos
        self.recv(0, down, 0, self.place.down)
        self.send(4, down, 0, self.place.up)
        self.recv(3, up, 1, self.place.up)
        self.send(5, up, 1, self.place.down)

    def end(self):
        me, up, down, far = self.pos
        self.recv(1, down, 1, self.place.down)
        self.recv(2, up, 0, self.place.up)
        self.recv(4, far, 0, self.place.down)
        self.recv(5, far, 1, self.place.up)


def add_into(dst, *srcs):
    total = srcs[0][...].astype(F32)
    for src in srcs[1:]:
        total = total + src[...].astype(F32)
    dst[...] = total.astype(dst.dtype)


def scatter_ring(parts, place, lanes, base, bufs, outs, started=None):
    axis = place.axis
    n = len(parts)
    p = place
    groups = (
        (p.mate_far, p.mate_up, p.mate_down, p.mate),
        (p.far, p.up, p.down, p.me),
    )

    def slot(i, s):
        return bufs[i](s)

    def send(k, i, src, s, dev):
        lanes.send(base + k * n + i, src, slot(i, s), axis, dev)

    def recv(k, i, s, dev):
        lanes.recv(base + k * n + i, slot(i, s), axis, dev)

    every = range(n)
    for g, (far, up, down, own) in enumerate(groups):
        for i in every:
            send(6 * g + 0, i, parts[i](far, 0), 6 * g + 0, p.up)
            send(6 * g + 1, i, parts[i](far, 1), 6 * g + 1, p.down)
        for i in every:
            send(6 * g + 3, i, parts[i](up, 1), 6 * g + 3, p.up)
            send(6 * g + 4, i, parts[i](down, 0), 6 * g + 4, p.down)
    if started is not None:
        started()
    for g, (far, up, down, own) in enumerate(groups):
        for i in every:
            recv(6 * g + 0, i, 6 * g + 0, p.down)
            add_into(slot(i, 6 * g + 0), slot(i, 6 * g + 0), parts[i](up, 0))
            send(6 * g + 2, i, slot(i, 6 * g + 0), 6 * g + 2, p.up)
            recv(6 * g + 1, i, 6 * g + 1, p.up)
            add_into(slot(i, 6 * g + 1), slot(i, 6 * g + 1), parts[i](down, 1))
            send(6 * g + 5, i, slot(i, 6 * g + 1), 6 * g + 5, p.down)
    far, up, down, own = groups[0]
    for half in (1, 0):
        for i in every:
            recv(2 + half, i, 2 + half, p.down)
            recv(4 + half, i, 4 + half, p.up)
            add_into(slot(i, 2 + half), slot(i, 2 + half), slot(i, 4 + half), parts[i](own, half))
            send(12 + half, i, slot(i, 2 + half), 12 + half, p.mate)
    for half in (1, 0):
        for i in every:
            recv(8 + half, i, 8 + half, p.down)
            recv(10 + half, i, 10 + half, p.up)
            recv(12 + half, i, 12 + half, p.mate)
            add_into(
                outs[i](half),
                slot(i, 8 + half),
                slot(i, 10 + half),
                slot(i, 12 + half),
                parts[i](p.me, half),
            )


def around(place):
    return [(place.axis, place.up), (place.axis, place.down), (place.axis, place.mate)]


def dispatch_kernel(
    n_ctx, mi_ref, og_ref, pick_ref, place_ref, key_ref, val_ref, q_ref,
    mine_ref, k_out, v_out, q_row, send, got, ss, rs, keep_sem,
):
    me = lax.axis_index("exp")
    ctx = Place("ctx")
    swap = n_ctx - 1 - ctx.me
    n_exp = send.shape[0]
    half = key_ref.shape[0] // 2
    greet(
        [("exp", lax.rem(me + d, n_exp)) for d in range(1, n_exp)]
        + [("ctx", dev) for dev in (ctx.up, ctx.down, swap)]
    )
    lanes = Lanes(ss, rs)
    upper = pl.ds(half, half)
    ring = Ring(
        lambda pos, h: q_row.at[pos, pl.ds(h * half, half)], ctx, lanes, n_exp + 1,
        lambda h: q_ref.at[pl.ds(h * half, half)],
    )
    ring.begin(0)
    ring.begin(1)
    lanes.send(n_exp - 1, key_ref.at[upper], k_out, "ctx", swap)
    lanes.send(n_exp, val_ref.at[upper], v_out, "ctx", swap)
    lanes.keep(keep_sem, q_ref, q_row.at[ctx.spots[0]])
    rows = jnp.dot(pick_ref[:, :128], mi_ref[...], preferred_element_type=F32)
    rows = rows + jnp.dot(pick_ref[:, 128:], og_ref[...], preferred_element_type=F32)
    send[...] = rows.reshape(n_exp, 8, rows.shape[1]).astype(BF)
    for d in range(1, n_exp):
        to = lax.rem(me + d, n_exp)
        lanes.send(d - 1, send.at[to], got.at[d], "exp", to)
    got[0] = send[me]
    ring.forward()
    for d in range(1, n_exp):
        lanes.recv(d - 1, got.at[d], "exp", lax.rem(me + n_exp - d, n_exp))
    flat = got[...].astype(F32).reshape(n_exp * 8, got.shape[2]).astype(BF)
    mine = jnp.dot(place_ref[...], flat, preferred_element_type=F32).astype(BF)
    mine_ref[...] = mine.reshape(2, 2, 16, got.shape[2])
    lanes.recv(n_exp - 1, k_out, "ctx", swap)
    lanes.recv(n_exp, v_out, "ctx", swap)
    ring.end()
    lanes.finish()


def dispatch(moe_input, out_grad, pick, place, keys, values, queries):
    n_exp, n_ctx = lax.axis_size("exp"), lax.axis_size("ctx")
    width = moe_input.shape[1]
    dealt = jax.ShapeDtypeStruct((keys.shape[0] // 2, keys.shape[1]), BF)
    n_sem = n_exp + 1 + RING_LANES
    return pl.pallas_call(
        functools.partial(dispatch_kernel, n_ctx),
        out_shape=(
            jax.ShapeDtypeStruct((2, 2, 16, width), BF),
            dealt,
            dealt,
            jax.ShapeDtypeStruct((4,) + queries.shape, BF),
        ),
        in_specs=[VMEM_SPEC] * 4 + [ANY_SPEC] * 3,
        out_specs=(VMEM_SPEC,) + (ANY_SPEC,) * 3,
        scratch_shapes=[
            VM((n_exp, 8, width), BF),
            VM((n_exp, 8, width), BF),
            pltpu.SemaphoreType.DMA((n_sem,)),
            pltpu.SemaphoreType.DMA((n_sem,)),
            pltpu.SemaphoreType.DMA,
        ],
        compiler_params=pltpu.CompilerParams(
            collective_id=1, has_side_effects=True, vmem_limit_bytes=VLIM
        ),
        cost_estimate=pl.CostEstimate(flops=10**6, bytes_accessed=10**6, transcendentals=0),
    )(moe_input, out_grad, pick, place, keys, values, queries)


def member_of(e):
    return (e // 8) * 2 + lax.rem(e, 2)


def share_kernel(
    mine_ref, og_ref, w_ref, o_ref, out_ref, og_row, w_group, o_group, ss, rs, keep_sems
):
    ctx, exp = Place("ctx"), Place("exp")
    others = (exp.twin, exp.mate, exp.mate_twin)
    greet(around(ctx) + [("exp", d) for d in (exp.up, exp.down) + others])
    lanes = Lanes(ss, rs)
    half_rows = og_ref.shape[0] // 2
    ring = Ring(
        lambda pos, h: og_row.at[pos, pl.ds(h * half_rows, half_rows)], exp, lanes, AG_LANES,
        lambda h: og_ref.at[pl.ds(h * half_rows, half_rows)],
    )
    me = member_of(exp.me)
    base = AG_LANES + RING_LANES

    def more():
        lanes.keep(keep_sems.at[0], mine_ref, out_ref.at[:, :, ctx.me])
        lanes.keep(keep_sems.at[1], og_ref, og_row.at[exp.spots[0]])
        lanes.keep(keep_sems.at[2], w_ref, w_group.at[me])
        own_o = o_ref.at[exp.me // 8, :, lax.rem(exp.me, 2)]
        lanes.keep(keep_sems.at[3], own_o, o_group.at[me])
        ring.begin(0)
        ring.begin(1)
        lanes.send(base, w_ref, w_group.at[me], "exp", exp.mate)
        lanes.send(base + 1, w_ref, w_group.at[me], "exp", exp.twin)
        for j, dev in enumerate(others):
            lanes.send(
                base + 3 + j, o_ref.at[dev // 8, :, lax.rem(dev, 2)], o_group.at[me], "exp", dev
            )

    def pass_on():
        block = w_group.at[member_of(exp.mate)]
        lanes.recv(base, block, "exp", exp.mate)
        lanes.send(base + 2, block, block, "exp", exp.twin)

    nothing = lambda: None
    work = [more, ring.forward, nothing, nothing, pass_on]
    gather_ring(
        [lambda block, half: out_ref.at[half, :, block]], ctx, lanes, 0, work=work,
        own=[lambda half: mine_ref.at[half]],
    )
    ring.end()
    lanes.recv(base + 1, w_group.at[member_of(exp.twin)], "exp", exp.twin)
    lanes.recv(base + 2, w_group.at[member_of(exp.mate_twin)], "exp", exp.twin)
    for j, dev in enumerate(others):
        lanes.recv(base + 3 + j, o_group.at[member_of(dev)], "exp", dev)
    lanes.finish()


def share(mine, out_grad, w_out, attn_out):
    n_ctx = lax.axis_size("ctx")
    rows, head = out_grad.shape[0], attn_out.shape[1]
    n_sem = AG_LANES + RING_LANES + 6
    vmem = pl.BlockSpec(memory_space=VM)
    return pl.pallas_call(
        share_kernel,
        out_shape=(
            jax.ShapeDtypeStruct(mine.shape[:2] + (n_ctx,) + mine.shape[2:], BF),
            jax.ShapeDtypeStruct((4,) + out_grad.shape, BF),
            jax.ShapeDtypeStruct((4,) + w_out.shape, BF),
            jax.ShapeDtypeStruct((4, 4, rows, head), BF),
        ),
        in_specs=[vmem] * 4,
        out_specs=(vmem,) + (ANY_SPEC,) * 3,
        scratch_shapes=[
            pltpu.SemaphoreType.DMA((n_sem,)),
            pltpu.SemaphoreType.DMA((n_sem,)),
            pltpu.SemaphoreType.DMA((4,)),
        ],
        compiler_params=pltpu.CompilerParams(
            collective_id=5, has_side_effects=True, vmem_limit_bytes=VLIM
        ),
        cost_estimate=pl.CostEstimate(flops=10**6, bytes_accessed=10**6, transcendentals=0),
    )(mine, out_grad, w_out, attn_out.reshape(2, 4, 2, rows, head))


def combine_kernel(
    part_ref, gate_ref, q_ref, og_far, w_far, out_ref, gate_out, q_mate, base_out,
    buf, gate_buf, base_send, own_dx, og_row, w_group, ss, rs, keep_sems,
):
    ctx, exp = Place("ctx"), Place("exp")
    twin = exp.twin
    loads = [
        pltpu.make_async_copy(src, dst, keep_sems.at[j])
        for j, (src, dst) in enumerate(((og_far, og_row), (w_far, w_group)))
    ]
    for one in loads:
        one.start()
    greet(around(ctx) + around(exp) + [("exp", twin), ("exp", exp.mate_twin)])
    lanes = Lanes(ss, rs)
    rows = q_ref.shape[0] // 2
    pos = lax.rem(ctx.me, 4)
    q_base = 3 * AG_LANES + 16
    d_base = q_base + 2 + RING_LANES
    others = (exp.twin, exp.mate, exp.mate_twin)

    def q_piece(at, half):
        return q_mate.at[at, pl.ds(half * rows, rows)]

    def q_start():
        for half in range(2):
            src = q_ref.at[pl.ds(half * rows, rows)]
            lanes.send(q_base + half, src, q_piece(pos, half), "ctx", ctx.mate)
        for one in loads:
            one.wait()
        rows_og = og_row[...].reshape(-1, og_row.shape[2])
        y_lo, core = exp.me // 8, lax.rem(exp.me, 2)
        for j, dev in enumerate(others + (exp.me,)):
            value = contract_last(rows_og, w_group[member_of(dev)]).astype(BF)
            value = value.reshape(base_send.shape[1:])
            base_send[j] = value
            to = base_out.at[y_lo, :, core]
            if j < 3:
                lanes.send(d_base + j, base_send.at[j], to, "exp", dev)
            else:
                lanes.keep(keep_sems.at[2], base_send.at[j], to)

    ring = Ring(q_piece, ctx, lanes, q_base + 2)

    def q_ring(half):
        lanes.recv(q_base + half, q_piece(pos, half), "ctx", ctx.mate)
        ring.begin(half)

    scatter_ring(
        [
            lambda block, half: part_ref.at[half, block],
            lambda block, half: gate_ref.at[half, block],
        ],
        ctx,
        lanes,
        0,
        [lambda s: buf.at[s], lambda s: gate_buf.at[s]],
        [lambda half: own_dx.at[half], lambda half: gate_out.at[half]],
        q_start,
    )

    def piece(block, half):
        return out_ref.at[block, half]

    base = 2 * AG_LANES
    over = 3 * AG_LANES
    flip = exp.flip
    for half in range(2):
        lanes.send(over + 14 + half, own_dx.at[half], piece(exp.me, half), "exp", twin)
    lanes.keep(keep_sems.at[3], own_dx, out_ref.at[exp.me])

    def arrived(k, block, half):
        lanes.send(over + k, piece(block, half), piece(block, half), "exp", twin)

    work = [lambda: q_ring(0), lambda: q_ring(1), ring.forward]
    gather_ring([piece], exp, lanes, base, arrived, work, own=[lambda half: own_dx.at[half]])
    ring.end()
    srcs = {
        0: (exp.mate, 0), 1: (exp.mate, 1), 2: (exp.down, 0), 3: (exp.down, 1),
        4: (exp.up, 1), 5: (exp.up, 0), 6: (exp.far, 0), 7: (exp.far, 1),
        8: (exp.mate_down, 0), 9: (exp.mate_down, 1), 10: (exp.mate_up, 0),
        11: (exp.mate_up, 1), 12: (exp.mate_far, 0), 13: (exp.mate_far, 1),
        14: (exp.me, 0), 15: (exp.me, 1),
    }
    for k, (block, half) in srcs.items():
        lanes.recv(over + k, piece(block + flip, half), "exp", twin)
    for j, dev in enumerate(others):
        lanes.recv(d_base + j, base_out.at[dev // 8, :, lax.rem(dev, 2)], "exp", dev)
    lanes.finish()


def combine(part, gate_part, queries, og_row, w_group):
    n_exp = lax.axis_size("exp")
    rows, width = part.shape[2:]
    n_sem = 3 * AG_LANES + 16 + 2 + RING_LANES + 3
    tok, head = og_row.shape[1], queries.shape[1]
    return pl.pallas_call(
        combine_kernel,
        out_shape=(
            jax.ShapeDtypeStruct((n_exp, 2, rows, width), BF),
            jax.ShapeDtypeStruct((2,) + gate_part.shape[2:], F32),
            jax.ShapeDtypeStruct((4,) + queries.shape, BF),
            jax.ShapeDtypeStruct((2, 4, 2, tok, head), BF),
        ),
        in_specs=[VMEM_SPEC] * 2 + [ANY_SPEC] * 3,
        out_specs=(ANY_SPEC, VMEM_SPEC, ANY_SPEC, ANY_SPEC),
        scratch_shapes=[
            VM((14, rows, width), BF),
            VM((14,) + gate_part.shape[2:], F32),
            VM((4, 4, tok, head), BF),
            VM((2, rows, width), BF),
            VM(og_row.shape, BF),
            VM(w_group.shape, BF),
            pltpu.SemaphoreType.DMA((n_sem,)),
            pltpu.SemaphoreType.DMA((n_sem,)),
            pltpu.SemaphoreType.DMA((4,)),
        ],
        compiler_params=pltpu.CompilerParams(
            collective_id=2, has_side_effects=True, vmem_limit_bytes=VLIM
        ),
        cost_estimate=pl.CostEstimate(flops=10**6, bytes_accessed=10**6, transcendentals=0),
    )(part, gate_part, queries, og_row, w_group)


def spread_kernel(
    base_ref, w_ref, o_ref, ids_ref, dx_ref, og_far, o_group,
    do_all, delta_all, dw_ref,
    own_do, own_delta, og_row, dw_acc, dx_out, taken, dw_buf, ss, rs, keep_sems,
):
    ctx, exp = Place("ctx"), Place("exp")
    load = pltpu.make_async_copy(og_far, og_row, keep_sems.at[0])
    load.start()
    greet(around(ctx) + [("exp", exp.twin), ("exp", exp.mate)])
    lanes = Lanes(ss, rs)
    chunk = 256
    rows = base_ref.shape[0] // 2
    n_out, _, part = dw_ref.shape
    taken[...] = jnp.zeros_like(taken)
    dx_out[...] = contract_last(dx_ref[...], w_ref[...]).astype(BF)
    ones = jnp.ones((8, o_ref.shape[1]), BF)

    def project(j, carry):
        here = pl.ds(pl.multiple_of(j * chunk, chunk), chunk)
        o = o_ref[here, :]
        at = lax.broadcasted_iota(jnp.int32, (chunk, ids_ref.shape[1]), 0) + j * chunk
        pick = jnp.where(at == ids_ref[...], 1.0, 0.0).astype(BF)
        value = base_ref[here, :].astype(F32)
        value = value + jnp.dot(pick, dx_out[...], preferred_element_type=F32)
        value = value.astype(BF)
        own_do[here, :] = value
        taken[...] += contract_first(pick, o)
        rest = value.astype(F32) * o.astype(F32)
        total = jnp.zeros((8, chunk), F32)
        for _ in range(3):
            term = rest.astype(BF)
            total = total + contract_last(ones, term)
            rest = rest - term.astype(F32)
        own_delta[:, here] = total[0:1]
        return carry

    def ready(half):
        first = half * (rows // chunk)
        lax.fori_loop(first, first + rows // chunk, project, 0)

    base = 2 * AG_LANES
    n_rows = og_row.shape[0] * og_row.shape[1]

    def term(dev, cols):
        o = o_group[member_of(dev)].reshape(n_rows, o_ref.shape[1])
        return contract_first(o, og_row[:, :, cols].reshape(n_rows, part))

    def fill(slot, dev):
        for b in range(n_out):
            cols = pl.ds(b * part, part)
            dw_buf[slot, :, cols] = term(dev, cols).astype(BF)

    def first():
        lanes.keep(keep_sems.at[1], own_do, do_all.at[ctx.me])
        lanes.keep(keep_sems.at[2], own_delta, delta_all.at[ctx.me])
        load.wait()
        fill(0, exp.mate_twin)
        lanes.send(base, dw_buf.at[0], dw_buf.at[3], "exp", exp.twin)
        fill(1, exp.mate)

    def second():
        lanes.recv(base, dw_buf.at[3], "exp", exp.twin)
        add_into(dw_buf.at[1], dw_buf.at[1], dw_buf.at[3])
        lanes.send(base + 1, dw_buf.at[1], dw_buf.at[4], "exp", exp.mate)

    def third():
        fill(2, exp.twin)
        lanes.send(base + 2, dw_buf.at[2], dw_buf.at[5], "exp", exp.twin)

    def fourth():
        rows_taken = taken[...].astype(BF)
        for b in range(n_out):
            cols = pl.ds(b * part, part)
            dw_acc[:, cols] = term(exp.me, cols) + contract_first(rows_taken, dx_ref[:, cols])

    def close():
        lanes.recv(base + 2, dw_buf.at[5], "exp", exp.twin)
        lanes.recv(base + 1, dw_buf.at[4], "exp", exp.mate)
        for b in range(n_out):
            cols = pl.ds(b * part, part)
            total = dw_acc[:, cols]
            for slot in (4, 5):
                total = total + dw_buf[slot, :, cols].astype(F32)
            dw_ref[b] = total.astype(BF)

    def piece_do(block, half):
        return do_all.at[block, pl.ds(half * rows, rows)]

    def piece_delta(block, half):
        return delta_all.at[block, :, pl.ds(half * rows, rows)]

    gather_ring(
        [piece_do, piece_delta], ctx, lanes, 0,
        work=[first, second, third, fourth], ready=ready,
        own=[
            lambda half: own_do.at[pl.ds(half * rows, rows)],
            lambda half: own_delta.at[:, pl.ds(half * rows, rows)],
        ],
    )
    close()
    lanes.finish()


def spread(d_base, w_out, attn_out, ids, dx_all, og_row, o_group):
    n_ctx = lax.axis_size("ctx")
    n_sem = 2 * AG_LANES + 3
    tokens, head = d_base.shape
    width = w_out.shape[1]
    vmem = pl.BlockSpec(memory_space=VM)
    return pl.pallas_call(
        spread_kernel,
        out_shape=(
            jax.ShapeDtypeStruct((n_ctx, tokens, head), BF),
            jax.ShapeDtypeStruct((n_ctx, 1, tokens), F32),
            jax.ShapeDtypeStruct((n_ctx, head, width // n_ctx), BF),
        ),
        in_specs=[vmem] * 5 + [ANY_SPEC, vmem],
        out_specs=(ANY_SPEC, ANY_SPEC, vmem),
        scratch_shapes=[
            VM((tokens, head), BF),
            VM((1, tokens), F32),
            VM(og_row.shape, BF),
            VM((head, width), F32),
            VM((dx_all.shape[0], head), BF),
            VM((dx_all.shape[0], head), F32),
            VM((6, head, width), BF),
            pltpu.SemaphoreType.DMA((n_sem,)),
            pltpu.SemaphoreType.DMA((n_sem,)),
            pltpu.SemaphoreType.DMA((3,)),
        ],
        compiler_params=pltpu.CompilerParams(
            collective_id=3, has_side_effects=True, vmem_limit_bytes=VLIM
        ),
        cost_estimate=pl.CostEstimate(flops=10**6, bytes_accessed=10**6, transcendentals=0),
    )(d_base, w_out, attn_out, ids, dx_all, og_row, o_group)


CHUNK = 1024
TILE = 512


def attention_kernel(
    scale, n_ctx, k_own, k_far, v_own, v_far, q_row, q_mate, do_far, lse_ref, delta_ref, dw_ref,
    grads_out, gw_out,
    q_ref, do_ref, k_ref, v_ref, hold, dq_part, dk_acc, dv_acc, dq_acc, back, dq_buf, dw_buf, ss, rs, load_sems,
):
    p = Place("ctx")
    c = p.me
    swap = n_ctx - 1 - c
    n_ring = q_row.shape[0]
    low = c // n_ring
    order = [p.mate_far, p.mate_up, p.mate_down, p.mate, p.far, p.up, p.down, p.me]
    for j in (4, 0, 5, 1, 6, 2, 3, 7):
        src = q_row if j > 3 else q_mate
        block = order[j]
        pltpu.make_async_copy(
            src.at[lax.rem(block, n_ring)], q_ref.at[block], load_sems.at[0, j]
        ).start()
        pltpu.make_async_copy(do_far.at[block], do_ref.at[block], load_sems.at[1, j]).start()
    greet(around(p) + [("ctx", swap)])
    lanes = Lanes(ss, rs)
    n_chunk = 2 * n_ctx
    ids = (2 * c, n_chunk - 1 - 2 * c)
    k_ref[0], k_ref[1] = k_own[:CHUNK, :], k_far[...]
    v_ref[0], v_ref[1] = v_own[:CHUNK, :], v_far[...]
    dk_acc[...] = jnp.zeros_like(dk_acc)
    dv_acc[...] = jnp.zeros_like(dv_acc)

    def tile(part, group, half, row, key, masked):
        at = half * CHUNK + row
        spot = group * 2 * CHUNK + at
        q = q_ref[group, pl.ds(at, TILE), :]
        do = do_ref[group, pl.ds(at, TILE), :]
        lse = lse_ref[:, pl.ds(spot, TILE)] * LOG2E
        delta = delta_ref[group, :, pl.ds(at, TILE)]
        k = k_ref[part, pl.ds(key, TILE), :]
        v = v_ref[part, pl.ds(key, TILE), :]
        s = contract_last(k, q) * (scale * LOG2E) - lse
        if masked:
            rk = lax.broadcasted_iota(jnp.int32, s.shape, 0)
            cq = lax.broadcasted_iota(jnp.int32, s.shape, 1)
            s = jnp.where(rk <= cq, s, -1e30)
        probs = jnp.exp2(s)
        dp = contract_last(v, do)
        ds = (probs * (dp - delta)).astype(BF)
        dv_acc[part, pl.ds(key, TILE), :] += jnp.dot(
            probs.astype(BF), do, preferred_element_type=F32
        )
        dk_acc[part, pl.ds(key, TILE), :] += jnp.dot(ds, q, preferred_element_type=F32)
        dq_acc[pl.ds(row, TILE), :] += contract_first(ds, k)

    w_rows = dw_ref.shape[1] // 2
    parts = (
        lambda block, h: dq_part.at[block, pl.ds(h * CHUNK, CHUNK)],
        lambda block, h: dw_ref.at[block, pl.ds(h * w_rows, w_rows)],
    )
    slots = (lambda s: dq_buf.at[s], lambda s: dw_buf.at[s])
    n = len(parts)

    def send(i, k, src, dev):
        lanes.copy(k * n + i, src, slots[i](k), "ctx", dev).start()

    def recv(i, k, dev):
        lanes.copy(k * n + i, slots[i](k), slots[i](k), "ctx", dev).wait_recv()

    def plain(i, k, block, h, dev):
        send(i, k, parts[i](block, h), dev)

    def summed(i, k, into, others, block, h, dev):
        add_into(
            slots[i](into), slots[i](into), *[slots[i](o) for o in others], parts[i](block, h)
        )
        send(i, k, slots[i](into), dev)

    def near_up(i, g, block):
        recv(i, 6 * g, p.down)
        summed(i, 6 * g + 2, 6 * g, (), block, 0, p.up)

    def near_down(i, g, block):
        recv(i, 6 * g + 1, p.up)
        summed(i, 6 * g + 5, 6 * g + 1, (), block, 1, p.down)

    def over(i, h):
        recv(i, 2 + h, p.down)
        recv(i, 4 + h, p.up)
        summed(i, 12 + h, 2 + h, (4 + h,), p.mate, h, p.mate)

    rows = ((p.mate_far, p.mate_up, p.mate_down), (p.far, p.up, p.down))
    base = n * AG_LANES
    last = n_chunk - 1

    def give_back():
        for j, (acc, factor) in enumerate(((dk_acc, scale), (dv_acc, 1.0))):
            back[j] = (acc[1] * factor).astype(BF)
            back_copy(j).start()

    def back_copy(j):
        return lanes.copy(
            base + j, back.at[j], grads_out.at[1 + j, pl.ds(CHUNK, CHUNK)], "ctx", swap
        )

    plan = []
    for g, (far, up, down) in enumerate(rows):
        early = 0 if g == 1 else 2
        late = 2 - early
        plan += [
            (early, late, functools.partial(plain, 0, 6 * g, far, 0, p.up)),
            (early + 1, late + 1, functools.partial(plain, 0, 6 * g + 1, far, 1, p.down)),
            (early + 5, late + 5, functools.partial(plain, 0, 6 * g + 3, up, 1, p.up)),
            (early + 5, late + 5, functools.partial(near_up, 0, g, up)),
            (early + 8, late + 8, functools.partial(plain, 0, 6 * g + 4, down, 0, p.down)),
            (early + 9, late + 9, functools.partial(near_down, 0, g, down)),
            (3, 3, functools.partial(near_up, 1, g, up)),
            (3, 3, functools.partial(near_down, 1, g, down)),
        ]
    plan += [
        (6, 6, functools.partial(over, 1, 0)),
        (6, 6, functools.partial(over, 1, 1)),
        (12, 12, functools.partial(over, 0, 0)),
        (13, 13, functools.partial(over, 0, 1)),
        (last, last, give_back),
    ]
    for g, (far, up, down) in enumerate(rows):
        plain(1, 6 * g, far, 0, p.up)
        plain(1, 6 * g + 1, far, 1, p.down)
        plain(1, 6 * g + 3, up, 1, p.up)
        plain(1, 6 * g + 4, down, 0, p.down)
    first_row = (4, 0, 5, 1, 6, 2, 3, 7, 7)
    other_row = (0, 4, 1, 5, 2, 6, 3, 7, 7)

    def step(t, carry):
        place = t // 2
        half = lax.rem(t, 2)
        spot = jnp.where(low == 0, first_row[0], other_row[0])
        for j in range(1, len(first_row)):
            spot = jnp.where(place == j, jnp.where(low == 0, first_row[j], other_row[j]), spot)
        group = order[0]
        for j in range(1, len(order)):
            group = jnp.where(spot == j, order[j], group)
        chunk = 2 * group + half

        @pl.when((half == 0) & (t < n_chunk))
        def _():
            pltpu.make_async_copy(q_row.at[0], q_ref.at[group], load_sems.at[0, spot]).wait()
            pltpu.make_async_copy(do_far.at[0], do_ref.at[group], load_sems.at[1, spot]).wait()

        @pl.when(t < n_chunk)
        def _():
            dq_acc[...] = jnp.zeros_like(dq_acc)

        @pl.when(t >= n_chunk)
        def _():
            dq_acc[...] = hold[half]

        busy = ((t < n_chunk - 2) | (t >= n_chunk), t < n_chunk)
        for part in range(2):

            @pl.when((chunk > ids[part]) & busy[part])
            def _(part=part):
                for row in range(0, CHUNK, TILE):
                    for key in range(0, CHUNK, TILE):
                        tile(part, group, half, row, key, False)

            @pl.when((chunk == ids[part]) & busy[part])
            def _(part=part):
                for row in range(0, CHUNK, TILE):
                    for key in range(0, row + 1, TILE):
                        tile(part, group, half, row, key, key == row)

        keep = (t >= n_chunk - 2) & (t < n_chunk)

        @pl.when(keep)
        def _():
            hold[half] = dq_acc[...]

        @pl.when(jnp.logical_not(keep))
        def _():
            dq_part[group, pl.ds(half * CHUNK, CHUNK), :] = (dq_acc[...] * scale).astype(BF)

        for early, late, act in plan:
            pl.when(t == jnp.where(low == 0, early, late))(act)

        return carry

    lax.fori_loop(0, n_chunk + 2, step, 0)

    for j, (acc, factor) in enumerate(((dk_acc, scale), (dv_acc, 1.0))):
        grads_out[1 + j, :CHUNK, :] = (acc[0] * factor).astype(BF)
    finals = (
        lambda h: grads_out.at[0, pl.ds(h * CHUNK, CHUNK)],
        lambda h: gw_out.at[pl.ds(h * w_rows, w_rows)],
    )
    for h in range(2):
        for i in range(n):
            recv(i, 8 + h, p.down)
            recv(i, 10 + h, p.up)
            recv(i, 12 + h, p.mate)
            add_into(
                finals[i](h), slots[i](8 + h), slots[i](10 + h), slots[i](12 + h),
                parts[i](p.me, h),
            )
    for k in range(AG_LANES):
        for i in range(n):
            lanes.copy(k * n + i, slots[i](k), slots[i](k), "ctx", p.up).wait_send()
    for j in range(2):
        back_copy(j).wait()


def attention(keys, k_far, values, v_far, q_row, q_mate, do_all, lse, delta_all, dw_part, scale):
    n_ctx, tok_ctx, head = do_all.shape
    vmem = pl.BlockSpec(memory_space=VM)
    anyw = pl.BlockSpec(memory_space=pl.ANY)
    n_sem = 2 * AG_LANES + 2
    return pl.pallas_call(
        functools.partial(attention_kernel, scale, n_ctx),
        out_shape=(
            jax.ShapeDtypeStruct((3, tok_ctx, head), BF),
            jax.ShapeDtypeStruct(dw_part.shape[1:], BF),
        ),
        in_specs=[vmem] * 4 + [anyw] * 3 + [vmem] * 3,
        out_specs=(vmem,) * 2,
        scratch_shapes=[
            VM(do_all.shape, BF),
            VM(do_all.shape, BF),
            VM((2, CHUNK, head), BF),
            VM((2, CHUNK, head), BF),
            VM((2, CHUNK, head), F32),
            VM(do_all.shape, BF),
            VM((2, CHUNK, head), F32),
            VM((2, CHUNK, head), F32),
            VM((CHUNK, head), F32),
            VM((2, CHUNK, head), BF),
            VM((AG_LANES, CHUNK, head), BF),
            VM((AG_LANES, dw_part.shape[1] // 2, dw_part.shape[2]), BF),
            pltpu.SemaphoreType.DMA((n_sem,)),
            pltpu.SemaphoreType.DMA((n_sem,)),
            pltpu.SemaphoreType.DMA((2, 8)),
        ],
        compiler_params=pltpu.CompilerParams(
            collective_id=4, has_side_effects=True, vmem_limit_bytes=VLIM
        ),
        cost_estimate=pl.CostEstimate(
            flops=40 * 10**9, bytes_accessed=20 * 10**6, transcendentals=17 * 10**6
        ),
    )(keys, k_far, values, v_far, q_row, q_mate, do_all, lse, delta_all, dw_part)


def body(
    moe_input,
    out_grad,
    w_gate,
    w_up,
    w_down,
    expert_picks,
    gate_probs,
    queries,
    attn_keys,
    values,
    attn_out,
    log_norm,
    w_out,
):
    n_ctx = lax.axis_size("ctx")
    n_exp = lax.axis_size("exp")
    ctx_id = lax.axis_index("ctx")
    exp_id = lax.axis_index("exp")
    tok_dev, feat_width = moe_input.shape
    n_local = w_gate.shape[0]
    group_picks = expert_picks.shape[1] // n_ctx
    tok_ctx, head_dim = queries.shape
    key_scale = head_dim ** (-0.5)
    i32 = jnp.int32

    base_row = (ctx_id * n_exp + exp_id) * tok_dev
    below = jnp.sum((expert_picks < base_row).astype(i32), axis=1, keepdims=True)
    inside = (expert_picks >= base_row) & (expert_picks < base_row + tok_dev)
    spot = jnp.arange(expert_picks.shape[1], dtype=i32)[None, :] - below
    local = expert_picks - base_row
    chosen = jnp.stack(
        [jnp.sum(jnp.where(inside & (spot == s), local + 1, 0), axis=1) - 1 for s in range(MOST)],
        axis=1,
    )
    chosen = chosen.reshape(n_exp, n_local * MOST)
    away = jnp.full_like(chosen, -1)
    columns = jnp.arange(2 * tok_dev, dtype=i32)
    wanted = jnp.stack(
        [chosen, jnp.where(chosen >= 0, chosen + tok_dev, away)], axis=1
    ).reshape(-1)
    pick = (wanted[:, None] == columns[None, :]).astype(BF)

    my_picks = lax.dynamic_slice(
        expert_picks, (exp_id * n_local, ctx_id * group_picks), (n_local, group_picks)
    )
    block_of = my_picks // tok_dev
    src_exp = block_of - ctx_id * n_exp
    slot_rank = jnp.arange(group_picks, dtype=i32)[None, :] - jnp.sum(
        (my_picks[:, None, :] < (block_of * tok_dev)[:, :, None]).astype(i32), axis=2
    )
    dist = lax.rem(exp_id - src_exp + n_exp, n_exp)
    spot_x = dist * 8 + jnp.arange(n_local, dtype=i32)[:, None] * MOST + slot_rank
    spots = jnp.stack([spot_x, spot_x + n_local * MOST]).reshape(-1)
    place = (spots[:, None] == jnp.arange(8 * n_exp, dtype=i32)[None, :]).astype(BF)

    mine, k_far, v_far, q_row = dispatch(
        moe_input, out_grad, pick, place, attn_keys, values, queries
    )
    slots, og_row, w_group, o_group = share(mine, out_grad, w_out, attn_out)
    slots = slots.reshape(2, n_local, n_ctx * group_picks, feat_width)
    slot_rows, slot_grads = slots[0], slots[1]

    gate_rows = lax.dynamic_slice_in_dim(gate_probs, exp_id * n_local, n_local, 0)
    pre_gate = jnp.einsum("kcd,kdf->kcf", slot_rows, w_gate, preferred_element_type=F32)
    pre_up = jnp.einsum("kcd,kdf->kcf", slot_rows, w_up, preferred_element_type=F32)
    gated_act, act_slope = activation(pre_gate)
    hidden_full = gated_act * pre_up
    hidden = hidden_full.astype(BF)
    down_back = jnp.einsum("kcd,kfd->kcf", slot_grads, w_down, preferred_element_type=F32)
    gate_part = jnp.sum(down_back * hidden_full, axis=2).reshape(n_local, n_ctx, 1, group_picks)
    gate_part = jnp.pad(gate_part, ((0, 0), (0, 0), (0, 0), (0, 128 - group_picks)))
    scaled = gate_rows[..., None] * down_back
    d_gate = (scaled * pre_up * act_slope).astype(BF)
    d_up = (scaled * gated_act).astype(BF)
    dx_part = (
        jnp.einsum("kcf,kdf->kcd", d_gate, w_gate, preferred_element_type=F32)
        + jnp.einsum("kcf,kdf->kcd", d_up, w_up, preferred_element_type=F32)
    ).astype(BF)
    dx_all, gate_sum, q_mate, d_base = combine(
        dx_part.reshape(n_local, n_ctx, group_picks, feat_width),
        gate_part,
        queries,
        og_row,
        w_group,
    )
    d_gates = gate_sum[:, 0, :group_picks]
    dx_all = dx_all.reshape(-1, feat_width)

    weighted = (gate_rows[..., None] * slot_grads.astype(F32)).astype(BF)
    dw_down = jnp.einsum("kcf,kcd->kfd", hidden, weighted, preferred_element_type=F32).astype(BF)
    dw_gate = jnp.einsum("kcd,kcf->kdf", slot_rows, d_gate, preferred_element_type=F32).astype(BF)
    dw_up = jnp.einsum("kcd,kcf->kdf", slot_rows, d_up, preferred_element_type=F32).astype(BF)

    group_ids = lax.dynamic_slice_in_dim(
        expert_picks, ctx_id * group_picks, group_picks, 1
    ).reshape(-1) - ctx_id * tok_ctx
    own_hot = (
        (jnp.arange(tok_dev, dtype=i32) + exp_id * tok_dev)[:, None] == group_ids[None, :]
    ).astype(BF)
    d_resid = (
        out_grad.astype(F32) + jnp.dot(own_hot, dx_all, preferred_element_type=F32)
    ).astype(BF)

    do_all, delta_all, dw_part = spread(
        d_base.reshape(tok_ctx, head_dim), w_out, attn_out, group_ids[None, :], dx_all,
        og_row, o_group,
    )
    grads, dw_out = attention(
        attn_keys, k_far, values, v_far, q_row, q_mate, do_all, log_norm, delta_all, dw_part,
        key_scale,
    )
    return (
        d_resid, dw_gate, dw_up, dw_down, d_gates, dw_out, grads[0], grads[1], grads[2],
    )


def solution(mesh):
    return jax.shard_map(
        body,
        mesh=mesh,
        in_specs=(
            P(("ctx", "exp"), None),
            P(("ctx", "exp"), None),
            P("exp", None, "ctx"),
            P("exp", None, "ctx"),
            P("exp", "ctx", None),
            P(),
            P(),
            P("ctx", "exp"),
            P("ctx", "exp"),
            P("ctx", "exp"),
            P("ctx", "exp"),
            P("exp", None),
            P("exp", None),
        ),
        out_specs=(
            P(("ctx", "exp"), None),
            P("exp", None, "ctx"),
            P("exp", None, "ctx"),
            P("exp", "ctx", None),
            P("exp", "ctx"),
            P("exp", "ctx"),
            P("ctx", "exp"),
            P("ctx", "exp"),
            P("ctx", "exp"),
        ),
        check_vma=False,
    )
```

```python
import functools
import math

import jax
import jax.numpy as jnp
from jax import lax
from jax.experimental import pallas as pl
from jax.experimental.pallas import tpu as pltpu
from jax.sharding import PartitionSpec as P

MOST = 2
MESH = pl.DeviceIdType.MESH
LOG2E = 1.4426950408889634
BF = jnp.bfloat16
F32 = jnp.float32
VLIM = 56 * 1024 * 1024
VM = pltpu.VMEM
VMEM_SPEC = pl.BlockSpec(memory_space=pltpu.VMEM)
ANY_SPEC = pl.BlockSpec(memory_space=pl.ANY)


def activation(pre_act):
    sigmoid_val = jax.nn.sigmoid(pre_act)
    return (pre_act * sigmoid_val, sigmoid_val * (1.0 + pre_act * (1.0 - sigmoid_val)))


def contract_first(left, right):
    return lax.dot_general(left, right, (((0,), (0,)), ((), ())), preferred_element_type=F32)


def contract_last(left, right):
    return lax.dot_general(left, right, (((1,), (1,)), ((), ())), preferred_element_type=F32)


class Place:
    def __init__(self, axis):
        self.axis = axis
        me = lax.axis_index(axis)
        if axis == "ctx":
            step, span = 1, 4
        else:
            step, span = 2, 8
        low = lax.rem(me, step)
        pos = lax.rem(me // step, 4)
        row = me // span
        other = 1 - row

        def at(r, p):
            return r * span + lax.rem(p + 4, 4) * step + low

        self.me = me
        self.up, self.down, self.far = at(row, pos + 1), at(row, pos - 1), at(row, pos + 2)
        self.mate = at(other, pos)
        self.mate_up, self.mate_down = at(other, pos + 1), at(other, pos - 1)
        self.mate_far = at(other, pos + 2)
        self.spots = tuple(lax.rem(pos + d, 4) for d in (0, 1, 3, 2))
        self.flip = 1 - 2 * low
        self.twin, self.mate_twin = me + self.flip, self.mate + self.flip


def greet(peers):
    barrier = pltpu.get_barrier_semaphore()
    for axis, dev in peers:
        pl.semaphore_signal(barrier, inc=1, device_id={axis: dev}, device_id_type=MESH)
    pl.semaphore_wait(barrier, len(peers))


class Lanes:
    def __init__(self, send_sems, recv_sems):
        self.send_sems, self.recv_sems, self.sent, self.local = send_sems, recv_sems, [], []

    def copy(self, k, src, dst, axis, dev):
        return pltpu.make_async_remote_copy(
            src_ref=src,
            dst_ref=dst,
            send_sem=self.send_sems.at[k],
            recv_sem=self.recv_sems.at[k],
            device_id={axis: dev},
            device_id_type=MESH,
        )

    def send(self, k, src, dst, axis, dev):
        one = self.copy(k, src, dst, axis, dev)
        one.start()
        self.sent.append(one)

    def recv(self, k, dst, axis, dev):
        self.copy(k, dst, dst, axis, dev).wait_recv()

    def finish(self):
        for one in self.sent:
            one.wait_send()
        for one in self.local:
            one.wait()

    def keep(self, sem, src, dst):
        one = pltpu.make_async_copy(src, dst, sem)
        one.start()
        self.local.append(one)


AG_LANES = 14


def gather_ring(pieces, place, lanes, base, arrived=None, work=(), ready=None, own=None):
    axis = place.axis
    n = len(pieces)
    work = list(work)

    def fill():
        if work:
            work.pop(0)()

    def send(k, block, half, dev):
        for i, piece in enumerate(pieces):
            src = piece(block, half) if own is None or k > 5 else own[i](half)
            lanes.send(base + k * n + i, src, piece(block, half), axis, dev)

    def recv(k, block, half, dev):
        for i, piece in enumerate(pieces):
            lanes.recv(base + k * n + i, piece(block, half), axis, dev)
        if arrived is not None:
            arrived(k, block, half)

    p = place
    if ready is not None:
        ready(0)
    send(0, p.me, 0, p.mate)
    send(2, p.me, 0, p.up)
    send(5, p.me, 0, p.down)
    if ready is not None:
        ready(1)
    send(4, p.me, 1, p.down)
    send(1, p.me, 1, p.mate)
    send(3, p.me, 1, p.up)
    fill()
    recv(2, p.down, 0, p.down)
    send(6, p.down, 0, p.up)
    recv(4, p.up, 1, p.up)
    send(7, p.up, 1, p.down)
    fill()
    recv(0, p.mate, 0, p.mate)
    send(8, p.mate, 0, p.up)
    send(10, p.mate, 0, p.down)
    fill()
    recv(1, p.mate, 1, p.mate)
    send(11, p.mate, 1, p.down)
    send(9, p.mate, 1, p.up)
    fill()
    recv(8, p.mate_down, 0, p.down)
    send(12, p.mate_down, 0, p.up)
    recv(11, p.mate_up, 1, p.up)
    send(13, p.mate_up, 1, p.down)
    while work:
        fill()
    recv(3, p.down, 1, p.down)
    recv(5, p.up, 0, p.up)
    recv(6, p.far, 0, p.down)
    recv(7, p.far, 1, p.up)
    recv(10, p.mate_up, 0, p.up)
    recv(9, p.mate_down, 1, p.down)
    recv(12, p.mate_far, 0, p.down)
    recv(13, p.mate_far, 1, p.up)


RING_LANES = 6


class Ring:
    def __init__(self, piece, place, lanes, base, own=None):
        self.piece, self.place, self.lanes, self.base = piece, place, lanes, base
        self.own = own
        self.pos = place.spots

    def send(self, k, pos, half, dev):
        one = self.piece(pos, half)
        src = one if self.own is None or k > 3 else self.own(half)
        self.lanes.send(self.base + k, src, one, self.place.axis, dev)

    def recv(self, k, pos, half, dev):
        self.lanes.recv(self.base + k, self.piece(pos, half), self.place.axis, dev)

    def begin(self, half):
        me, up, down, far = self.pos
        if half == 0:
            self.send(0, me, 0, self.place.up)
            self.send(2, me, 0, self.place.down)
        else:
            self.send(3, me, 1, self.place.down)
            self.send(1, me, 1, self.place.up)

    def forward(self):
        me, up, down, far = self.pos
        self.recv(0, down, 0, self.place.down)
        self.send(4, down, 0, self.place.up)
        self.recv(3, up, 1, self.place.up)
        self.send(5, up, 1, self.place.down)

    def end(self):
        me, up, down, far = self.pos
        self.recv(1, down, 1, self.place.down)
        self.recv(2, up, 0, self.place.up)
        self.recv(4, far, 0, self.place.down)
        self.recv(5, far, 1, self.place.up)


def add_into(dst, *srcs):
    total = srcs[0][...].astype(F32)
    for src in srcs[1:]:
        total = total + src[...].astype(F32)
    dst[...] = total.astype(dst.dtype)


def scatter_ring(parts, place, lanes, base, bufs, outs, started=None):
    axis = place.axis
    n = len(parts)
    p = place
    groups = (
        (p.mate_far, p.mate_up, p.mate_down, p.mate),
        (p.far, p.up, p.down, p.me),
    )

    def slot(i, s):
        return bufs[i](s)

    def send(k, i, src, s, dev):
        lanes.send(base + k * n + i, src, slot(i, s), axis, dev)

    def recv(k, i, s, dev):
        lanes.recv(base + k * n + i, slot(i, s), axis, dev)

    every = range(n)
    for g, (far, up, down, own) in enumerate(groups):
        for i in every:
            send(6 * g + 0, i, parts[i](far, 0), 6 * g + 0, p.up)
            send(6 * g + 1, i, parts[i](far, 1), 6 * g + 1, p.down)
        for i in every:
            send(6 * g + 3, i, parts[i](up, 1), 6 * g + 3, p.up)
            send(6 * g + 4, i, parts[i](down, 0), 6 * g + 4, p.down)
    if started is not None:
        started()
    for g, (far, up, down, own) in enumerate(groups):
        for i in every:
            recv(6 * g + 0, i, 6 * g + 0, p.down)
            add_into(slot(i, 6 * g + 0), slot(i, 6 * g + 0), parts[i](up, 0))
            send(6 * g + 2, i, slot(i, 6 * g + 0), 6 * g + 2, p.up)
            recv(6 * g + 1, i, 6 * g + 1, p.up)
            add_into(slot(i, 6 * g + 1), slot(i, 6 * g + 1), parts[i](down, 1))
            send(6 * g + 5, i, slot(i, 6 * g + 1), 6 * g + 5, p.down)
    far, up, down, own = groups[0]
    for half in (1, 0):
        for i in every:
            recv(2 + half, i, 2 + half, p.down)
            recv(4 + half, i, 4 + half, p.up)
            add_into(slot(i, 2 + half), slot(i, 2 + half), slot(i, 4 + half), parts[i](own, half))
            send(12 + half, i, slot(i, 2 + half), 12 + half, p.mate)
    for half in (1, 0):
        for i in every:
            recv(8 + half, i, 8 + half, p.down)
            recv(10 + half, i, 10 + half, p.up)
            recv(12 + half, i, 12 + half, p.mate)
            add_into(
                outs[i](half),
                slot(i, 8 + half),
                slot(i, 10 + half),
                slot(i, 12 + half),
                parts[i](p.me, half),
            )


def around(place):
    return [(place.axis, place.up), (place.axis, place.down), (place.axis, place.mate)]


def dispatch_kernel(
    n_ctx, mi_ref, og_ref, pick_ref, place_ref, key_ref, val_ref, q_ref,
    mine_ref, k_out, v_out, q_row, send, got, ss, rs, keep_sem,
):
    me = lax.axis_index("exp")
    ctx = Place("ctx")
    swap = n_ctx - 1 - ctx.me
    n_exp = send.shape[0]
    half = key_ref.shape[0] // 2
    greet(
        [("exp", lax.rem(me + d, n_exp)) for d in range(1, n_exp)]
        + [("ctx", dev) for dev in (ctx.up, ctx.down, swap)]
    )
    lanes = Lanes(ss, rs)
    upper = pl.ds(half, half)
    ring = Ring(
        lambda pos, h: q_row.at[pos, pl.ds(h * half, half)], ctx, lanes, n_exp + 1,
        lambda h: q_ref.at[pl.ds(h * half, half)],
    )
    ring.begin(0)
    ring.begin(1)
    lanes.send(n_exp - 1, key_ref.at[upper], k_out, "ctx", swap)
    lanes.send(n_exp, val_ref.at[upper], v_out, "ctx", swap)
    lanes.keep(keep_sem, q_ref, q_row.at[ctx.spots[0]])
    rows = jnp.dot(pick_ref[:, :128], mi_ref[...], preferred_element_type=F32)
    rows = rows + jnp.dot(pick_ref[:, 128:], og_ref[...], preferred_element_type=F32)
    send[...] = rows.reshape(n_exp, 8, rows.shape[1]).astype(BF)
    for d in range(1, n_exp):
        to = lax.rem(me + d, n_exp)
        lanes.send(d - 1, send.at[to], got.at[d], "exp", to)
    got[0] = send[me]
    ring.forward()
    for d in range(1, n_exp):
        lanes.recv(d - 1, got.at[d], "exp", lax.rem(me + n_exp - d, n_exp))
    flat = got[...].astype(F32).reshape(n_exp * 8, got.shape[2]).astype(BF)
    mine = jnp.dot(place_ref[...], flat, preferred_element_type=F32).astype(BF)
    mine_ref[...] = mine.reshape(2, 2, 16, got.shape[2])
    lanes.recv(n_exp - 1, k_out, "ctx", swap)
    lanes.recv(n_exp, v_out, "ctx", swap)
    ring.end()
    lanes.finish()


def dispatch(moe_input, out_grad, pick, place, keys, values, queries):
    n_exp, n_ctx = lax.axis_size("exp"), lax.axis_size("ctx")
    width = moe_input.shape[1]
    dealt = jax.ShapeDtypeStruct((keys.shape[0] // 2, keys.shape[1]), BF)
    n_sem = n_exp + 1 + RING_LANES
    return pl.pallas_call(
        functools.partial(dispatch_kernel, n_ctx),
        out_shape=(
            jax.ShapeDtypeStruct((2, 2, 16, width), BF),
            dealt,
            dealt,
            jax.ShapeDtypeStruct((4,) + queries.shape, BF),
        ),
        in_specs=[VMEM_SPEC] * 4 + [ANY_SPEC] * 3,
        out_specs=(VMEM_SPEC,) + (ANY_SPEC,) * 3,
        scratch_shapes=[
            VM((n_exp, 8, width), BF),
            VM((n_exp, 8, width), BF),
            pltpu.SemaphoreType.DMA((n_sem,)),
            pltpu.SemaphoreType.DMA((n_sem,)),
            pltpu.SemaphoreType.DMA,
        ],
        compiler_params=pltpu.CompilerParams(
            collective_id=1, has_side_effects=True, vmem_limit_bytes=VLIM
        ),
        cost_estimate=pl.CostEstimate(flops=10**6, bytes_accessed=10**6, transcendentals=0),
    )(moe_input, out_grad, pick, place, keys, values, queries)


def member_of(e):
    return (e // 8) * 2 + lax.rem(e, 2)


def share_kernel(
    mine_ref, og_ref, w_ref, o_ref, x_all, y_all, og_row, w_group, o_group, ss, rs, keep_sems
):
    ctx, exp = Place("ctx"), Place("exp")
    others = (exp.twin, exp.mate, exp.mate_twin)
    greet(around(ctx) + [("exp", d) for d in (exp.up, exp.down) + others])
    lanes = Lanes(ss, rs)
    half_rows = og_ref.shape[0] // 2
    ring = Ring(
        lambda pos, h: og_row.at[pos, pl.ds(h * half_rows, half_rows)], exp, lanes, AG_LANES,
        lambda h: og_ref.at[pl.ds(h * half_rows, half_rows)],
    )
    me = member_of(exp.me)
    base = AG_LANES + RING_LANES

    def more():
        lanes.keep(keep_sems.at[0], mine_ref.at[0], x_all.at[:, ctx.me])
        lanes.keep(keep_sems.at[4], mine_ref.at[1], y_all.at[:, ctx.me])
        lanes.keep(keep_sems.at[1], og_ref, og_row.at[exp.spots[0]])
        lanes.keep(keep_sems.at[2], w_ref, w_group.at[me])
        own_o = o_ref.at[exp.me // 8, :, lax.rem(exp.me, 2)]
        lanes.keep(keep_sems.at[3], own_o, o_group.at[me])
        ring.begin(0)
        ring.begin(1)
        lanes.send(base, w_ref, w_group.at[me], "exp", exp.mate)
        lanes.send(base + 1, w_ref, w_group.at[me], "exp", exp.twin)
        for j, dev in enumerate(others):
            lanes.send(
                base + 3 + j, o_ref.at[dev // 8, :, lax.rem(dev, 2)], o_group.at[me], "exp", dev
            )

    def pass_on():
        block = w_group.at[member_of(exp.mate)]
        lanes.recv(base, block, "exp", exp.mate)
        lanes.send(base + 2, block, block, "exp", exp.twin)

    nothing = lambda: None
    work = [more, ring.forward, nothing, nothing, pass_on]
    gather_ring(
        [lambda block, half: (x_all, y_all)[half].at[:, block]], ctx, lanes, 0, work=work,
        own=[lambda half: mine_ref.at[half]],
    )
    ring.end()
    lanes.recv(base + 1, w_group.at[member_of(exp.twin)], "exp", exp.twin)
    lanes.recv(base + 2, w_group.at[member_of(exp.mate_twin)], "exp", exp.twin)
    for j, dev in enumerate(others):
        lanes.recv(base + 3 + j, o_group.at[member_of(dev)], "exp", dev)
    lanes.finish()


def share(mine, out_grad, w_out, attn_out):
    n_ctx = lax.axis_size("ctx")
    rows, head = out_grad.shape[0], attn_out.shape[1]
    n_sem = AG_LANES + RING_LANES + 6
    slots = jax.ShapeDtypeStruct((mine.shape[1], n_ctx) + mine.shape[2:], BF)
    vmem = pl.BlockSpec(memory_space=VM)
    return pl.pallas_call(
        share_kernel,
        out_shape=(
            slots,
            slots,
            jax.ShapeDtypeStruct((4,) + out_grad.shape, BF),
            jax.ShapeDtypeStruct((4,) + w_out.shape, BF),
            jax.ShapeDtypeStruct((4, 4, rows, head), BF),
        ),
        in_specs=[vmem] * 4,
        out_specs=(vmem,) * 2 + (ANY_SPEC,) * 3,
        scratch_shapes=[
            pltpu.SemaphoreType.DMA((n_sem,)),
            pltpu.SemaphoreType.DMA((n_sem,)),
            pltpu.SemaphoreType.DMA((5,)),
        ],
        compiler_params=pltpu.CompilerParams(
            collective_id=5, has_side_effects=True, vmem_limit_bytes=VLIM
        ),
        cost_estimate=pl.CostEstimate(flops=10**6, bytes_accessed=10**6, transcendentals=0),
    )(mine, out_grad, w_out, attn_out.reshape(2, 4, 2, rows, head))


def combine_kernel(
    part_ref, gate_ref, q_ref, og_far, w_far, out_ref, gate_out, q_mate, base_out,
    buf, gate_buf, base_send, own_dx, og_row, w_group, ss, rs, keep_sems,
):
    ctx, exp = Place("ctx"), Place("exp")
    twin = exp.twin
    loads = [
        pltpu.make_async_copy(src, dst, keep_sems.at[j])
        for j, (src, dst) in enumerate(((og_far, og_row), (w_far, w_group)))
    ]
    for one in loads:
        one.start()
    greet(around(ctx) + around(exp) + [("exp", twin), ("exp", exp.mate_twin)])
    lanes = Lanes(ss, rs)
    rows = q_ref.shape[0] // 2
    pos = lax.rem(ctx.me, 4)
    q_base = 3 * AG_LANES + 16
    d_base = q_base + 2 + RING_LANES
    others = (exp.twin, exp.mate, exp.mate_twin)

    def q_piece(at, half):
        return q_mate.at[at, pl.ds(half * rows, rows)]

    def q_start():
        for half in range(2):
            src = q_ref.at[pl.ds(half * rows, rows)]
            lanes.send(q_base + half, src, q_piece(pos, half), "ctx", ctx.mate)
        for one in loads:
            one.wait()
        rows_og = og_row[...].reshape(-1, og_row.shape[2])
        y_lo, core = exp.me // 8, lax.rem(exp.me, 2)
        for j, dev in enumerate(others + (exp.me,)):
            value = contract_last(rows_og, w_group[member_of(dev)]).astype(BF)
            value = value.reshape(base_send.shape[1:])
            base_send[j] = value
            to = base_out.at[y_lo, :, core]
            if j < 3:
                lanes.send(d_base + j, base_send.at[j], to, "exp", dev)
            else:
                lanes.keep(keep_sems.at[2], base_send.at[j], to)

    ring = Ring(q_piece, ctx, lanes, q_base + 2)

    def q_ring(half):
        lanes.recv(q_base + half, q_piece(pos, half), "ctx", ctx.mate)
        ring.begin(half)

    scatter_ring(
        [
            lambda block, half: part_ref.at[half, block],
            lambda block, half: gate_ref.at[half, block],
        ],
        ctx,
        lanes,
        0,
        [lambda s: buf.at[s], lambda s: gate_buf.at[s]],
        [lambda half: own_dx.at[half], lambda half: gate_out.at[half]],
        q_start,
    )

    def piece(block, half):
        return out_ref.at[block, half]

    base = 2 * AG_LANES
    over = 3 * AG_LANES
    flip = exp.flip
    for half in range(2):
        lanes.send(over + 14 + half, own_dx.at[half], piece(exp.me, half), "exp", twin)
    lanes.keep(keep_sems.at[3], own_dx, out_ref.at[exp.me])

    def arrived(k, block, half):
        lanes.send(over + k, piece(block, half), piece(block, half), "exp", twin)

    work = [lambda: q_ring(0), lambda: q_ring(1), ring.forward]
    gather_ring([piece], exp, lanes, base, arrived, work, own=[lambda half: own_dx.at[half]])
    ring.end()
    srcs = {
        0: (exp.mate, 0), 1: (exp.mate, 1), 2: (exp.down, 0), 3: (exp.down, 1),
        4: (exp.up, 1), 5: (exp.up, 0), 6: (exp.far, 0), 7: (exp.far, 1),
        8: (exp.mate_down, 0), 9: (exp.mate_down, 1), 10: (exp.mate_up, 0),
        11: (exp.mate_up, 1), 12: (exp.mate_far, 0), 13: (exp.mate_far, 1),
        14: (exp.me, 0), 15: (exp.me, 1),
    }
    for k, (block, half) in srcs.items():
        lanes.recv(over + k, piece(block + flip, half), "exp", twin)
    for j, dev in enumerate(others):
        lanes.recv(d_base + j, base_out.at[dev // 8, :, lax.rem(dev, 2)], "exp", dev)
    lanes.finish()


def combine(part, gate_part, queries, og_row, w_group):
    n_exp = lax.axis_size("exp")
    rows, width = part.shape[2:]
    n_sem = 3 * AG_LANES + 16 + 2 + RING_LANES + 3
    tok, head = og_row.shape[1], queries.shape[1]
    return pl.pallas_call(
        combine_kernel,
        out_shape=(
            jax.ShapeDtypeStruct((n_exp, 2, rows, width), BF),
            jax.ShapeDtypeStruct((2,) + gate_part.shape[2:], F32),
            jax.ShapeDtypeStruct((4,) + queries.shape, BF),
            jax.ShapeDtypeStruct((2, 4, 2, tok, head), BF),
        ),
        in_specs=[VMEM_SPEC] * 2 + [ANY_SPEC] * 3,
        out_specs=(ANY_SPEC, VMEM_SPEC, ANY_SPEC, ANY_SPEC),
        scratch_shapes=[
            VM((14, rows, width), BF),
            VM((14,) + gate_part.shape[2:], F32),
            VM((4, 4, tok, head), BF),
            VM((2, rows, width), BF),
            VM(og_row.shape, BF),
            VM(w_group.shape, BF),
            pltpu.SemaphoreType.DMA((n_sem,)),
            pltpu.SemaphoreType.DMA((n_sem,)),
            pltpu.SemaphoreType.DMA((4,)),
        ],
        compiler_params=pltpu.CompilerParams(
            collective_id=2, has_side_effects=True, vmem_limit_bytes=VLIM
        ),
        cost_estimate=pl.CostEstimate(flops=10**6, bytes_accessed=10**6, transcendentals=0),
    )(part, gate_part, queries, og_row, w_group)


def spread_kernel(
    base_ref, w_ref, o_ref, ids_ref, dx_ref, og_far, o_group,
    do_all, delta_all, dw_ref,
    own_do, own_delta, og_row, dw_acc, dx_out, taken, dw_buf, ss, rs, keep_sems,
):
    ctx, exp = Place("ctx"), Place("exp")
    load = pltpu.make_async_copy(og_far, og_row, keep_sems.at[0])
    load.start()
    greet(around(ctx) + [("exp", exp.twin), ("exp", exp.mate)])
    lanes = Lanes(ss, rs)
    chunk = 256
    rows = base_ref.shape[0] // 2
    n_out, _, part = dw_ref.shape
    taken[...] = jnp.zeros_like(taken)
    dx_out[...] = contract_last(dx_ref[...], w_ref[...]).astype(BF)
    ones = jnp.ones((8, o_ref.shape[1]), BF)

    def project(j, carry):
        here = pl.ds(pl.multiple_of(j * chunk, chunk), chunk)
        o = o_ref[here, :]
        at = lax.broadcasted_iota(jnp.int32, (chunk, ids_ref.shape[1]), 0) + j * chunk
        pick = jnp.where(at == ids_ref[...], 1.0, 0.0).astype(BF)
        value = base_ref[here, :].astype(F32)
        value = value + jnp.dot(pick, dx_out[...], preferred_element_type=F32)
        value = value.astype(BF)
        own_do[here, :] = value
        taken[...] += contract_first(pick, o)
        rest = value.astype(F32) * o.astype(F32)
        total = jnp.zeros((8, chunk), F32)
        for _ in range(3):
            term = rest.astype(BF)
            total = total + contract_last(ones, term)
            rest = rest - term.astype(F32)
        own_delta[:, here] = total[0:1]
        return carry

    def ready(half):
        first = half * (rows // chunk)
        lax.fori_loop(first, first + rows // chunk, project, 0)

    base = 2 * AG_LANES
    n_rows = og_row.shape[0] * og_row.shape[1]

    def term(dev, cols):
        o = o_group[member_of(dev)].reshape(n_rows, o_ref.shape[1])
        return contract_first(o, og_row[:, :, cols].reshape(n_rows, part))

    def fill(slot, dev):
        for b in range(n_out):
            cols = pl.ds(b * part, part)
            dw_buf[slot, :, cols] = term(dev, cols).astype(BF)

    def first():
        lanes.keep(keep_sems.at[1], own_do, do_all.at[ctx.me])
        lanes.keep(keep_sems.at[2], own_delta, delta_all.at[ctx.me])
        load.wait()
        fill(0, exp.mate_twin)
        lanes.send(base, dw_buf.at[0], dw_buf.at[3], "exp", exp.twin)
        fill(1, exp.mate)

    def second():
        lanes.recv(base, dw_buf.at[3], "exp", exp.twin)
        add_into(dw_buf.at[1], dw_buf.at[1], dw_buf.at[3])
        lanes.send(base + 1, dw_buf.at[1], dw_buf.at[4], "exp", exp.mate)

    def third():
        fill(2, exp.twin)
        lanes.send(base + 2, dw_buf.at[2], dw_buf.at[5], "exp", exp.twin)

    def fourth():
        rows_taken = taken[...].astype(BF)
        for b in range(n_out):
            cols = pl.ds(b * part, part)
            dw_acc[:, cols] = term(exp.me, cols) + contract_first(rows_taken, dx_ref[:, cols])

    def close():
        lanes.recv(base + 2, dw_buf.at[5], "exp", exp.twin)
        lanes.recv(base + 1, dw_buf.at[4], "exp", exp.mate)
        for b in range(n_out):
            cols = pl.ds(b * part, part)
            total = dw_acc[:, cols]
            for slot in (4, 5):
                total = total + dw_buf[slot, :, cols].astype(F32)
            dw_ref[b] = total.astype(BF)

    def piece_do(block, half):
        return do_all.at[block, pl.ds(half * rows, rows)]

    def piece_delta(block, half):
        return delta_all.at[block, :, pl.ds(half * rows, rows)]

    gather_ring(
        [piece_do, piece_delta], ctx, lanes, 0,
        work=[first, second, third, fourth], ready=ready,
        own=[
            lambda half: own_do.at[pl.ds(half * rows, rows)],
            lambda half: own_delta.at[:, pl.ds(half * rows, rows)],
        ],
    )
    close()
    lanes.finish()


def spread(d_base, w_out, attn_out, ids, dx_all, og_row, o_group):
    n_ctx = lax.axis_size("ctx")
    n_sem = 2 * AG_LANES + 3
    tokens, head = d_base.shape
    width = w_out.shape[1]
    vmem = pl.BlockSpec(memory_space=VM)
    return pl.pallas_call(
        spread_kernel,
        out_shape=(
            jax.ShapeDtypeStruct((n_ctx, tokens, head), BF),
            jax.ShapeDtypeStruct((n_ctx, 1, tokens), F32),
            jax.ShapeDtypeStruct((n_ctx, head, width // n_ctx), BF),
        ),
        in_specs=[vmem] * 5 + [ANY_SPEC, vmem],
        out_specs=(ANY_SPEC, ANY_SPEC, vmem),
        scratch_shapes=[
            VM((tokens, head), BF),
            VM((1, tokens), F32),
            VM(og_row.shape, BF),
            VM((head, width), F32),
            VM((dx_all.shape[0], head), BF),
            VM((dx_all.shape[0], head), F32),
            VM((6, head, width), BF),
            pltpu.SemaphoreType.DMA((n_sem,)),
            pltpu.SemaphoreType.DMA((n_sem,)),
            pltpu.SemaphoreType.DMA((3,)),
        ],
        compiler_params=pltpu.CompilerParams(
            collective_id=3, has_side_effects=True, vmem_limit_bytes=VLIM
        ),
        cost_estimate=pl.CostEstimate(flops=10**6, bytes_accessed=10**6, transcendentals=0),
    )(d_base, w_out, attn_out, ids, dx_all, og_row, o_group)


CHUNK = 1024
TILE = 512


def attention_kernel(
    scale, n_ctx, k_own, k_far, v_own, v_far, q_row, q_mate, do_far, lse_ref, delta_ref, dw_ref,
    grads_out, gw_out,
    q_ref, do_ref, k_ref, v_ref, hold, dq_part, dk_acc, dv_acc, dq_acc, back, dq_buf, dw_buf, ss, rs, load_sems,
):
    p = Place("ctx")
    c = p.me
    swap = n_ctx - 1 - c
    n_ring = q_row.shape[0]
    low = c // n_ring
    order = [p.mate_far, p.mate_up, p.mate_down, p.mate, p.far, p.up, p.down, p.me]
    for j in (4, 0, 5, 1, 6, 2, 3, 7):
        src = q_row if j > 3 else q_mate
        block = order[j]
        pltpu.make_async_copy(
            src.at[lax.rem(block, n_ring)], q_ref.at[block], load_sems.at[0, j]
        ).start()
        pltpu.make_async_copy(do_far.at[block], do_ref.at[block], load_sems.at[1, j]).start()
    greet(around(p) + [("ctx", swap)])
    lanes = Lanes(ss, rs)
    n_chunk = 2 * n_ctx
    ids = (2 * c, n_chunk - 1 - 2 * c)
    k_ref[0], k_ref[1] = k_own[:CHUNK, :], k_far[...]
    v_ref[0], v_ref[1] = v_own[:CHUNK, :], v_far[...]
    dk_acc[...] = jnp.zeros_like(dk_acc)
    dv_acc[...] = jnp.zeros_like(dv_acc)

    def tile(part, group, half, row, key, masked):
        at = half * CHUNK + row
        spot = group * 2 * CHUNK + at
        q = q_ref[group, pl.ds(at, TILE), :]
        do = do_ref[group, pl.ds(at, TILE), :]
        lse = lse_ref[:, pl.ds(spot, TILE)] * LOG2E
        delta = delta_ref[group, :, pl.ds(at, TILE)]
        k = k_ref[part, pl.ds(key, TILE), :]
        v = v_ref[part, pl.ds(key, TILE), :]
        s = contract_last(k, q) * (scale * LOG2E) - lse
        if masked:
            rk = lax.broadcasted_iota(jnp.int32, s.shape, 0)
            cq = lax.broadcasted_iota(jnp.int32, s.shape, 1)
            s = jnp.where(rk <= cq, s, -1e30)
        probs = jnp.exp2(s)
        dp = contract_last(v, do)
        ds = (probs * (dp - delta)).astype(BF)
        dv_acc[part, pl.ds(key, TILE), :] += jnp.dot(
            probs.astype(BF), do, preferred_element_type=F32
        )
        dk_acc[part, pl.ds(key, TILE), :] += jnp.dot(ds, q, preferred_element_type=F32)
        dq_acc[pl.ds(row, TILE), :] += contract_first(ds, k)

    w_rows = dw_ref.shape[1] // 2
    parts = (
        lambda block, h: dq_part.at[block, pl.ds(h * CHUNK, CHUNK)],
        lambda block, h: dw_ref.at[block, pl.ds(h * w_rows, w_rows)],
    )
    slots = (lambda s: dq_buf.at[s], lambda s: dw_buf.at[s])
    n = len(parts)

    def send(i, k, src, dev):
        lanes.copy(k * n + i, src, slots[i](k), "ctx", dev).start()

    def recv(i, k, dev):
        lanes.copy(k * n + i, slots[i](k), slots[i](k), "ctx", dev).wait_recv()

    def plain(i, k, block, h, dev):
        send(i, k, parts[i](block, h), dev)

    def summed(i, k, into, others, block, h, dev):
        add_into(
            slots[i](into), slots[i](into), *[slots[i](o) for o in others], parts[i](block, h)
        )
        send(i, k, slots[i](into), dev)

    def near_up(i, g, block):
        recv(i, 6 * g, p.down)
        summed(i, 6 * g + 2, 6 * g, (), block, 0, p.up)

    def near_down(i, g, block):
        recv(i, 6 * g + 1, p.up)
        summed(i, 6 * g + 5, 6 * g + 1, (), block, 1, p.down)

    def over(i, h):
        recv(i, 2 + h, p.down)
        recv(i, 4 + h, p.up)
        summed(i, 12 + h, 2 + h, (4 + h,), p.mate, h, p.mate)

    rows = ((p.mate_far, p.mate_up, p.mate_down), (p.far, p.up, p.down))
    base = n * AG_LANES
    last = n_chunk - 1

    def give_back():
        for j, (acc, factor) in enumerate(((dk_acc, scale), (dv_acc, 1.0))):
            back[j] = (acc[1] * factor).astype(BF)
            back_copy(j).start()

    def back_copy(j):
        return lanes.copy(
            base + j, back.at[j], grads_out.at[1 + j, pl.ds(CHUNK, CHUNK)], "ctx", swap
        )

    plan = []
    for g, (far, up, down) in enumerate(rows):
        early = 0 if g == 1 else 2
        late = 2 - early
        plan += [
            (early, late, functools.partial(plain, 0, 6 * g, far, 0, p.up)),
            (early + 1, late + 1, functools.partial(plain, 0, 6 * g + 1, far, 1, p.down)),
            (early + 5, late + 5, functools.partial(plain, 0, 6 * g + 3, up, 1, p.up)),
            (early + 5, late + 5, functools.partial(near_up, 0, g, up)),
            (early + 8, late + 8, functools.partial(plain, 0, 6 * g + 4, down, 0, p.down)),
            (early + 9, late + 9, functools.partial(near_down, 0, g, down)),
            (3, 3, functools.partial(near_up, 1, g, up)),
            (3, 3, functools.partial(near_down, 1, g, down)),
        ]
    plan += [
        (6, 6, functools.partial(over, 1, 0)),
        (6, 6, functools.partial(over, 1, 1)),
        (12, 12, functools.partial(over, 0, 0)),
        (13, 13, functools.partial(over, 0, 1)),
        (last, last, give_back),
    ]
    for g, (far, up, down) in enumerate(rows):
        plain(1, 6 * g, far, 0, p.up)
        plain(1, 6 * g + 1, far, 1, p.down)
        plain(1, 6 * g + 3, up, 1, p.up)
        plain(1, 6 * g + 4, down, 0, p.down)
    first_row = (4, 0, 5, 1, 6, 2, 3, 7, 7)
    other_row = (0, 4, 1, 5, 2, 6, 3, 7, 7)

    def step(t, carry):
        place = t // 2
        half = lax.rem(t, 2)
        spot = jnp.where(low == 0, first_row[0], other_row[0])
        for j in range(1, len(first_row)):
            spot = jnp.where(place == j, jnp.where(low == 0, first_row[j], other_row[j]), spot)
        group = order[0]
        for j in range(1, len(order)):
            group = jnp.where(spot == j, order[j], group)
        chunk = 2 * group + half

        @pl.when((half == 0) & (t < n_chunk))
        def _():
            pltpu.make_async_copy(q_row.at[0], q_ref.at[group], load_sems.at[0, spot]).wait()
            pltpu.make_async_copy(do_far.at[0], do_ref.at[group], load_sems.at[1, spot]).wait()

        @pl.when(t < n_chunk)
        def _():
            dq_acc[...] = jnp.zeros_like(dq_acc)

        @pl.when(t >= n_chunk)
        def _():
            dq_acc[...] = hold[half]

        busy = ((t < n_chunk - 2) | (t >= n_chunk), t < n_chunk)
        for part in range(2):

            @pl.when((chunk > ids[part]) & busy[part])
            def _(part=part):
                for row in range(0, CHUNK, TILE):
                    for key in range(0, CHUNK, TILE):
                        tile(part, group, half, row, key, False)

            @pl.when((chunk == ids[part]) & busy[part])
            def _(part=part):
                for row in range(0, CHUNK, TILE):
                    for key in range(0, row + 1, TILE):
                        tile(part, group, half, row, key, key == row)

        keep = (t >= n_chunk - 2) & (t < n_chunk)

        @pl.when(keep)
        def _():
            hold[half] = dq_acc[...]

        @pl.when(jnp.logical_not(keep))
        def _():
            dq_part[group, pl.ds(half * CHUNK, CHUNK), :] = (dq_acc[...] * scale).astype(BF)

        for early, late, act in plan:
            pl.when(t == jnp.where(low == 0, early, late))(act)

        return carry

    lax.fori_loop(0, n_chunk + 2, step, 0)

    for j, (acc, factor) in enumerate(((dk_acc, scale), (dv_acc, 1.0))):
        grads_out[1 + j, :CHUNK, :] = (acc[0] * factor).astype(BF)
    finals = (
        lambda h: grads_out.at[0, pl.ds(h * CHUNK, CHUNK)],
        lambda h: gw_out.at[pl.ds(h * w_rows, w_rows)],
    )
    for h in range(2):
        for i in range(n):
            recv(i, 8 + h, p.down)
            recv(i, 10 + h, p.up)
            recv(i, 12 + h, p.mate)
            add_into(
                finals[i](h), slots[i](8 + h), slots[i](10 + h), slots[i](12 + h),
                parts[i](p.me, h),
            )
    for k in range(AG_LANES):
        for i in range(n):
            lanes.copy(k * n + i, slots[i](k), slots[i](k), "ctx", p.up).wait_send()
    for j in range(2):
        back_copy(j).wait()


def attention(keys, k_far, values, v_far, q_row, q_mate, do_all, lse, delta_all, dw_part, scale):
    n_ctx, tok_ctx, head = do_all.shape
    vmem = pl.BlockSpec(memory_space=VM)
    anyw = pl.BlockSpec(memory_space=pl.ANY)
    n_sem = 2 * AG_LANES + 2
    return pl.pallas_call(
        functools.partial(attention_kernel, scale, n_ctx),
        out_shape=(
            jax.ShapeDtypeStruct((3, tok_ctx, head), BF),
            jax.ShapeDtypeStruct(dw_part.shape[1:], BF),
        ),
        in_specs=[vmem] * 4 + [anyw] * 3 + [vmem] * 3,
        out_specs=(vmem,) * 2,
        scratch_shapes=[
            VM(do_all.shape, BF),
            VM(do_all.shape, BF),
            VM((2, CHUNK, head), BF),
            VM((2, CHUNK, head), BF),
            VM((2, CHUNK, head), F32),
            VM(do_all.shape, BF),
            VM((2, CHUNK, head), F32),
            VM((2, CHUNK, head), F32),
            VM((CHUNK, head), F32),
            VM((2, CHUNK, head), BF),
            VM((AG_LANES, CHUNK, head), BF),
            VM((AG_LANES, dw_part.shape[1] // 2, dw_part.shape[2]), BF),
            pltpu.SemaphoreType.DMA((n_sem,)),
            pltpu.SemaphoreType.DMA((n_sem,)),
            pltpu.SemaphoreType.DMA((2, 8)),
        ],
        compiler_params=pltpu.CompilerParams(
            collective_id=4, has_side_effects=True, vmem_limit_bytes=VLIM
        ),
        cost_estimate=pl.CostEstimate(
            flops=40 * 10**9, bytes_accessed=20 * 10**6, transcendentals=17 * 10**6
        ),
    )(keys, k_far, values, v_far, q_row, q_mate, do_all, lse, delta_all, dw_part)


def body(
    moe_input,
    out_grad,
    w_gate,
    w_up,
    w_down,
    expert_picks,
    gate_probs,
    queries,
    attn_keys,
    values,
    attn_out,
    log_norm,
    w_out,
):
    n_ctx = lax.axis_size("ctx")
    n_exp = lax.axis_size("exp")
    ctx_id = lax.axis_index("ctx")
    exp_id = lax.axis_index("exp")
    tok_dev, feat_width = moe_input.shape
    n_local = w_gate.shape[0]
    group_picks = expert_picks.shape[1] // n_ctx
    tok_ctx, head_dim = queries.shape
    key_scale = head_dim ** (-0.5)
    i32 = jnp.int32

    base_row = (ctx_id * n_exp + exp_id) * tok_dev
    below = jnp.sum((expert_picks < base_row).astype(i32), axis=1, keepdims=True)
    inside = (expert_picks >= base_row) & (expert_picks < base_row + tok_dev)
    spot = jnp.arange(expert_picks.shape[1], dtype=i32)[None, :] - below
    local = expert_picks - base_row
    chosen = jnp.stack(
        [jnp.sum(jnp.where(inside & (spot == s), local + 1, 0), axis=1) - 1 for s in range(MOST)],
        axis=1,
    )
    chosen = chosen.reshape(n_exp, n_local * MOST)
    away = jnp.full_like(chosen, -1)
    columns = jnp.arange(2 * tok_dev, dtype=i32)
    wanted = jnp.stack(
        [chosen, jnp.where(chosen >= 0, chosen + tok_dev, away)], axis=1
    ).reshape(-1)
    pick = (wanted[:, None] == columns[None, :]).astype(BF)

    my_picks = lax.dynamic_slice(
        expert_picks, (exp_id * n_local, ctx_id * group_picks), (n_local, group_picks)
    )
    block_of = my_picks // tok_dev
    src_exp = block_of - ctx_id * n_exp
    slot_rank = jnp.arange(group_picks, dtype=i32)[None, :] - jnp.sum(
        (my_picks[:, None, :] < (block_of * tok_dev)[:, :, None]).astype(i32), axis=2
    )
    dist = lax.rem(exp_id - src_exp + n_exp, n_exp)
    spot_x = dist * 8 + jnp.arange(n_local, dtype=i32)[:, None] * MOST + slot_rank
    spots = jnp.stack([spot_x, spot_x + n_local * MOST]).reshape(-1)
    place = (spots[:, None] == jnp.arange(8 * n_exp, dtype=i32)[None, :]).astype(BF)

    mine, k_far, v_far, q_row = dispatch(
        moe_input, out_grad, pick, place, attn_keys, values, queries
    )
    slot_rows, slot_grads, og_row, w_group, o_group = share(mine, out_grad, w_out, attn_out)
    slot_rows = slot_rows.reshape(n_local, n_ctx * group_picks, feat_width)
    slot_grads = slot_grads.reshape(n_local, n_ctx * group_picks, feat_width)

    gate_rows = lax.dynamic_slice_in_dim(gate_probs, exp_id * n_local, n_local, 0)
    pre_gate = jnp.einsum("kcd,kdf->kcf", slot_rows, w_gate, preferred_element_type=F32)
    pre_up = jnp.einsum("kcd,kdf->kcf", slot_rows, w_up, preferred_element_type=F32)
    gated_act, act_slope = activation(pre_gate)
    hidden_full = gated_act * pre_up
    hidden = hidden_full.astype(BF)
    down_back = jnp.einsum("kcd,kfd->kcf", slot_grads, w_down, preferred_element_type=F32)
    gate_part = jnp.sum(down_back * hidden_full, axis=2).reshape(n_local, n_ctx, 1, group_picks)
    gate_part = jnp.pad(gate_part, ((0, 0), (0, 0), (0, 0), (0, 128 - group_picks)))
    scaled = gate_rows[..., None] * down_back
    d_gate = (scaled * pre_up * act_slope).astype(BF)
    d_up = (scaled * gated_act).astype(BF)
    dx_part = (
        jnp.einsum("kcf,kdf->kcd", d_gate, w_gate, preferred_element_type=F32)
        + jnp.einsum("kcf,kdf->kcd", d_up, w_up, preferred_element_type=F32)
    ).astype(BF)
    dx_all, gate_sum, q_mate, d_base = combine(
        dx_part.reshape(n_local, n_ctx, group_picks, feat_width),
        gate_part,
        queries,
        og_row,
        w_group,
    )
    d_gates = gate_sum[:, 0, :group_picks]
    dx_all = dx_all.reshape(-1, feat_width)

    weighted = (gate_rows[..., None] * slot_grads.astype(F32)).astype(BF)
    dw_down = jnp.einsum("kcf,kcd->kfd", hidden, weighted, preferred_element_type=F32).astype(BF)
    dw_gate = jnp.einsum("kcd,kcf->kdf", slot_rows, d_gate, preferred_element_type=F32).astype(BF)
    dw_up = jnp.einsum("kcd,kcf->kdf", slot_rows, d_up, preferred_element_type=F32).astype(BF)

    group_ids = lax.dynamic_slice_in_dim(
        expert_picks, ctx_id * group_picks, group_picks, 1
    ).reshape(-1) - ctx_id * tok_ctx
    own_hot = (
        (jnp.arange(tok_dev, dtype=i32) + exp_id * tok_dev)[:, None] == group_ids[None, :]
    ).astype(BF)
    d_resid = (
        out_grad.astype(F32) + jnp.dot(own_hot, dx_all, preferred_element_type=F32)
    ).astype(BF)

    do_all, delta_all, dw_part = spread(
        d_base.reshape(tok_ctx, head_dim), w_out, attn_out, group_ids[None, :], dx_all,
        og_row, o_group,
    )
    grads, dw_out = attention(
        attn_keys, k_far, values, v_far, q_row, q_mate, do_all, log_norm, delta_all, dw_part,
        key_scale,
    )
    return (
        d_resid, dw_gate, dw_up, dw_down, d_gates, dw_out, grads[0], grads[1], grads[2],
    )


def solution(mesh):
    return jax.shard_map(
        body,
        mesh=mesh,
        in_specs=(
            P(("ctx", "exp"), None),
            P(("ctx", "exp"), None),
            P("exp", None, "ctx"),
            P("exp", None, "ctx"),
            P("exp", "ctx", None),
            P(),
            P(),
            P("ctx", "exp"),
            P("ctx", "exp"),
            P("ctx", "exp"),
            P("ctx", "exp"),
            P("exp", None),
            P("exp", None),
        ),
        out_specs=(
            P(("ctx", "exp"), None),
            P("exp", None, "ctx"),
            P("exp", None, "ctx"),
            P("exp", "ctx", None),
            P("exp", "ctx"),
            P("exp", "ctx"),
            P("ctx", "exp"),
            P("ctx", "exp"),
            P("ctx", "exp"),
        ),
        check_vma=False,
    )
```
